32 devices in a mesh: groups: 2 (over x), pages: 16 (over z, y, core).
Axes of the slice: x: 2, y: 2, z: 4, core: 2. Of those that a mesh axis runs over, the one named last changes fastest.
Arguments:
- queries: bfloat16 [2, 512, 8192], P(None, 'groups'), parts along dimension 1, may hold values from -14 to 14
- kv_cache: bfloat16 [256, 128, 2, 1024], P(('groups', 'pages')), parts along dimension 0, may hold values from -14 to 14
- w_out: bfloat16 [8192, 8192], P('pages'), may hold values from -0.0625 to 0.0625
- slot_page_before: int32 [256], P(('groups', 'pages')), parts along dimension 0, may hold values from -1 to 127, as said below
- slot_page_after: int32 [256], P(('groups', 'pages')), parts along dimension 0, may hold values from -1 to 127, as said below
- move_out: int32 [32, 4], P(('groups', 'pages')), parts along dimension 0, may hold values from -1 to 7, as said below
- move_in: int32 [32, 4], P(('groups', 'pages')), parts along dimension 0, may hold values from -1 to 7, as said below
- positions: int32 [2, 512], P(None, 'groups'), parts along dimension 1, may hold values from 0 to 16383, as said below
Outputs:
- attn_output: bfloat16 [2, 512, 8192], P(None, ('groups', 'pages')), parts along dimension 1
- cache_after: bfloat16 [256, 128, 2, 1024], P(('groups', 'pages')), parts along dimension 0
The draws below stay inside these ranges and needn't reach their ends.
There are 2 independent parts, one for each index of `groups`. The reference program is written for one: setup_inputs(seed, part) draws one part's arguments, and reference() takes and returns one part's arrays. A program takes and returns all parts, laid end to end along the dimension named above; an argument that names none is the same for every part. Nothing has to cross between parts.
Inputs may be any that keep to these rules, and one draw needn't show every extreme that they name: `slot_page_before`: the logical page held by each slot; -1 marks a free slot; the live pages are the last ones of the sequence, numbered consecutively up to 127, each in exactly one slot; an owner's free slots are its last ones. `slot_page_after`: pages that are not sent keep their slot, each sent page sits in the slot that move_in names at its new owner, and a slot that sent its page is free. `move_out`: entry [j, o - 1] is a slot of owner j holding a live page, sent to owner (j + o) mod 16, or -1; the slots of one row differ; an owner sends at most one page to each of its next 4 owners. `move_in`: entry [j, o - 1] is a slot of owner j that is free before the moves, or -1, which it is exactly where move_out[(j - o) mod 16, o - 1] is -1; the slots of one row differ. Each row holds 256 consecutive positions; row 1 ends at the last position of the last live page; at most 256 positions lie between the end of row 0 and the start of row 1; all lie within the live pages.
All inputs are finite; a program needn't handle non-finite values.
Results may differ from the reference program's by a relative error of at most 0.0055.
Values may be sent and summed in bfloat16 or wider, within the bound.
No kernel may reach another device: no remote copies, remote signals or barrier semaphores. Data moves between devices by JAX's collectives and lax.ppermute only.
A program may use at most 192 MiB of HBM per device.

```python
import jax
import jax.numpy as jnp
from jax import lax

HEADS = 64
KV_HEADS = 8
HEAD_DIM = 128
D = 8192
PAGE_TOK = 128
BLOCK = 256
PAGES_DEV = 8
MOVE_WIN = 4
OWNERS = 16
SLOTS = 128


def layout_plan(seed_key):
    base_key = jax.random.fold_in(seed_key, 7001)
    subkeys = jax.random.split(base_key, 6)
    levels = jax.random.randint(subkeys[0], (OWNERS,), 0, 4)
    percent = jnp.array([10, 40, 70, 100], jnp.int32)[levels]
    rolled = jax.random.randint(subkeys[1], (OWNERS, MOVE_WIN), 0, 100)
    send_flags = (rolled < percent[:, None]).astype(jnp.int32)
    picked = jax.random.randint(subkeys[2], (2,), 0, OWNERS)
    owner_ids = jnp.arange(OWNERS, dtype=jnp.int32)[:, None]
    offset = jnp.arange(1, MOVE_WIN + 1, dtype=jnp.int32)[None, :]
    quiet_owner = (picked[0] + OWNERS // 2) % OWNERS
    send_flags = jnp.where(owner_ids == quiet_owner, 0, send_flags)
    send_flags = jnp.where(owner_ids == picked[0], 1, send_flags)
    send_flags = jnp.where(owner_ids == (picked[1] - offset) % OWNERS, 1, send_flags)
    source = ((owner_ids - offset) % OWNERS).astype(jnp.int32)
    incoming = jnp.take_along_axis(send_flags, source, axis=0)
    received = jnp.sum(incoming, axis=1).astype(jnp.int32)
    slot_ids = jnp.arange(PAGES_DEV, dtype=jnp.int32)[None, :]
    occupied = slot_ids < (PAGES_DEV - received)[:, None]
    noise_ints = jax.random.randint(subkeys[3], (OWNERS, PAGES_DEV), 0, 1 << 20)
    ranked = jnp.where(occupied, noise_ints * PAGES_DEV + slot_ids, (1 << 20) * PAGES_DEV + slot_ids)
    order_rows = jnp.argsort(ranked, axis=1).astype(jnp.int32)
    out_rank = jnp.maximum(jnp.cumsum(send_flags, axis=1) - 1, 0).astype(jnp.int32)
    move_out = jnp.where(send_flags == 1, jnp.take_along_axis(order_rows, out_rank, axis=1), -1).astype(jnp.int32)
    in_rank = (jnp.cumsum(incoming, axis=1) - 1).astype(jnp.int32)
    move_in = jnp.where(incoming == 1, (PAGES_DEV - received)[:, None] + in_rank, -1).astype(jnp.int32)
    shuffled = jax.random.permutation(subkeys[4], SLOTS).astype(jnp.int32)
    flat_occupied = occupied.reshape(SLOTS)
    order_all = jnp.argsort(jnp.where(flat_occupied, shuffled, SLOTS + shuffled))
    rank_all = jnp.argsort(order_all).astype(jnp.int32)
    live_pages = (SLOTS - jnp.sum(received)).astype(jnp.int32)
    first_page = (SLOTS - live_pages).astype(jnp.int32)
    before = jnp.where(flat_occupied, rank_all + first_page, -1).astype(jnp.int32)
    before_grid = before.reshape(OWNERS, PAGES_DEV)
    sent_slots = jnp.any(move_out[:, :, None] == slot_ids[:, None, :], axis=1)
    after_ids = jnp.where(occupied & jnp.logical_not(sent_slots), before_grid, -1)
    sender_slot = jnp.take_along_axis(move_out, source, axis=0)
    arriving = jnp.where(incoming == 1, before[source * PAGES_DEV + jnp.maximum(sender_slot, 0)], -1)
    for column in range(MOVE_WIN):
        after_ids = jnp.where(slot_ids == move_in[:, column:column + 1], arriving[:, column:column + 1], after_ids)
    last_end = SLOTS * PAGE_TOK
    gap = jax.random.randint(subkeys[5], (), 0, 2 * PAGE_TOK + 1)
    steps_in = jnp.arange(BLOCK, dtype=jnp.int32)
    row_one = last_end - BLOCK + steps_in
    row_zero = last_end - 2 * BLOCK - gap + steps_in
    positions = jnp.stack([row_zero, row_one]).astype(jnp.int32)
    return (before, after_ids.reshape(SLOTS).astype(jnp.int32), move_out, move_in, positions)


def draw_slot_page_before(key, part):
    return layout_plan(key)[0]


def draw_slot_page_after(key, part):
    return layout_plan(key)[1]


def draw_move_out(key, part):
    return layout_plan(key)[2]


def draw_move_in(key, part):
    return layout_plan(key)[3]


def draw_positions(key, part):
    return layout_plan(key)[4]


def draw_kv_cache(key, part):
    shape_all = (SLOTS, PAGE_TOK, 2, KV_HEADS * HEAD_DIM)
    sample = jax.random.normal(jax.random.fold_in(key, 7003), shape_all, jnp.float32)
    key_rows = jnp.clip(sample[:, :, 0] * 2.0, -14.0, 14.0)
    value_rows = jnp.clip(sample[:, :, 1], -6.0, 6.0)
    return jnp.stack([key_rows, value_rows], axis=2).astype(jnp.bfloat16)


def draw_queries(key, part):
    shape_all = (2, BLOCK, D)
    sample = jnp.clip(jax.random.normal(jax.random.fold_in(key, 7004), shape_all, jnp.float32), -6.0, 6.0)
    return sample.astype(jnp.bfloat16)


def level_of(key, extent, cuts, smallest, top_value):
    level, own = 1.0, jax.random.fold_in(key, 6)
    for dim, shards_of in cuts:
        draws = jnp.exp(jax.random.uniform(jax.random.fold_in(own, dim), (shards_of,), jnp.float32, smallest / len(cuts), top_value / len(cuts)))
        level = level * jnp.repeat(draws, extent[dim] // shards_of).reshape([-1 if axis == dim else 1 for axis in range(len(extent))])
    return level


def normal_values(key, dims, scale, bound, shards=(), kind=jnp.bfloat16):
    level = level_of(key, dims, shards, -0.22, 0.18) if shards else 1.0
    drawn = jax.random.normal(key, dims, jnp.float32) * scale * level
    return jnp.minimum(jnp.maximum(drawn, -bound), bound).astype(kind)


def setup_inputs(seed: int = 0, part: int = 0) -> dict:
    splits = jax.random.split(jax.random.key(seed), 9)
    part_keys = jax.random.split(jax.random.fold_in(splits[8], part), 9)
    queries = draw_queries(jax.random.fold_in(jax.random.fold_in(splits[8], part), 71), part)
    kv_cache = draw_kv_cache(jax.random.fold_in(jax.random.fold_in(splits[8], part), 71), part)
    w_out = normal_values(splits[2], (D, D), D ** -0.5, 0.0625, ((0, 16),))
    slot_page_before = draw_slot_page_before(jax.random.fold_in(jax.random.fold_in(splits[8], part), 71), part)
    slot_page_after = draw_slot_page_after(jax.random.fold_in(jax.random.fold_in(splits[8], part), 71), part)
    move_out = draw_move_out(jax.random.fold_in(jax.random.fold_in(splits[8], part), 71), part)
    move_in = draw_move_in(jax.random.fold_in(jax.random.fold_in(splits[8], part), 71), part)
    positions = draw_positions(jax.random.fold_in(jax.random.fold_in(splits[8], part), 71), part)
    return dict(queries=queries, kv_cache=kv_cache, w_out=w_out, slot_page_before=slot_page_before, slot_page_after=slot_page_after, move_out=move_out, move_in=move_in, positions=positions)


floor_score = -1e30


def group_partials(query_rows, cache_rows, slot_table, positions_row):
    key_count = PAGES_DEV * PAGE_TOK
    head_group = HEADS // KV_HEADS
    key_rows = cache_rows[:, :, 0, :].reshape(key_count, KV_HEADS, HEAD_DIM).astype(jnp.float32)
    value_rows = cache_rows[:, :, 1, :].reshape(key_count, KV_HEADS, HEAD_DIM).astype(jnp.float32)
    key_pos = (slot_table[:, None] * PAGE_TOK + jnp.arange(PAGE_TOK, dtype=jnp.int32)[None, :]).reshape(key_count)
    live_keys = jnp.repeat(slot_table >= 0, PAGE_TOK)
    query_all = query_rows.reshape(BLOCK, KV_HEADS, head_group, HEAD_DIM).astype(jnp.float32)
    scores = jnp.einsum("qhgd,khd->qhgk", query_all, key_rows) * (HEAD_DIM ** -0.5)
    visible = (live_keys[None, :] & (key_pos[None, :] <= positions_row[:, None]))[:, None, None, :]
    scores = jnp.where(visible, scores, floor_score)
    row_max = jnp.max(scores, axis=-1)
    weights = jnp.where(visible, jnp.exp(scores - row_max[..., None]), 0.0).astype(jnp.bfloat16)
    row_sum = jnp.sum(weights.astype(jnp.float32), axis=-1)
    mixed_rows = jnp.einsum("qhgk,khd->qhgd", weights.astype(jnp.float32), value_rows)
    return mixed_rows.reshape(BLOCK, HEADS, HEAD_DIM), row_max.reshape(BLOCK, HEADS), row_sum.reshape(BLOCK, HEADS)


def attend(query_rows, cache_all, slot_table, positions_row, w_out):
    grouped = cache_all.reshape(OWNERS, PAGES_DEV, PAGE_TOK, 2, KV_HEADS * HEAD_DIM)
    tables = slot_table.reshape(OWNERS, PAGES_DEV)
    part_out, part_max, part_sum = lax.map(
        lambda inputs: group_partials(query_rows, inputs[0], inputs[1], positions_row), (grouped, tables))
    overall = jnp.max(part_max, axis=0)
    factor = jnp.exp(part_max - overall[None])
    weighted = jnp.sum(factor[..., None] * part_out, axis=0)
    normalizer = jnp.sum(factor * part_sum, axis=0)
    attended = (weighted / normalizer[..., None]).reshape(BLOCK, D).astype(jnp.bfloat16)
    return jnp.dot(attended, w_out, preferred_element_type=jnp.float32).astype(jnp.bfloat16)


def migrate(kv_cache, slot_page_after, move_out, move_in):
    grouped = kv_cache.reshape(OWNERS, PAGES_DEV, PAGE_TOK, 2, KV_HEADS * HEAD_DIM)
    after_ids = slot_page_after.reshape(OWNERS, PAGES_DEV)
    arranged = jnp.where((after_ids >= 0)[:, :, None, None, None], grouped, jnp.zeros((), grouped.dtype))
    slot_ids = jnp.arange(PAGES_DEV, dtype=jnp.int32)
    for offset in range(1, MOVE_WIN + 1):
        sender = jnp.roll(grouped, offset, axis=0)
        sender_slot = jnp.maximum(jnp.roll(move_out[:, offset - 1], offset), 0).astype(jnp.int32)
        arrived = jnp.take_along_axis(sender, sender_slot[:, None, None, None, None], axis=1)
        landing = (slot_ids[None, :] == move_in[:, offset - 1][:, None])[:, :, None, None, None]
        arranged = jnp.where(landing, arrived, arranged)
    return arranged.reshape(SLOTS, PAGE_TOK, 2, KV_HEADS * HEAD_DIM)


def reference(queries, kv_cache, w_out, slot_page_before, slot_page_after, move_out, move_in, positions):
    cache_after = migrate(kv_cache, slot_page_after, move_out, move_in)
    first_out = attend(queries[0], kv_cache, slot_page_before, positions[0], w_out)
    second = attend(queries[1], cache_after, slot_page_after, positions[1], w_out)
    return jnp.stack([first_out, second]), cache_after
```

```python
import functools

import jax
import jax.numpy as jnp
from jax import lax
from jax.experimental import pallas as pl
from jax.experimental.pallas import tpu as pltpu
from jax.sharding import PartitionSpec as P

HEADS = 64
KV_HEADS = 8
HEAD_DIM = 128
D = 8192
PAGE_TOK = 128
BLOCK = 256
MOVE_WIN = 4
GROUP = HEADS // KV_HEADS

LOG2E = 1.4426950408889634
FLOOR = -1e30
FAR = 1 << 30


def bits_of(n):
    return n.bit_length() - 1


def permute_to(x, n, target):
    return lax.ppermute(x, "pages", [(i, target(i)) for i in range(n)])


def head_of(j):
    half = KV_HEADS // 2
    return (j % 2) * half + j // 2


def attend_kernel(
    order, counts, x_ref, q_ref, qpos_ref, kpos_ref, *refs, first, last, tile, rows, tok
):
    n_in = 0 if first else 2
    carried = refs[:n_in]
    outs = refs[n_in : n_in + 2]
    k_s, v_s, acc_s, m_s = refs[n_in + 2 :]
    step = pl.program_id(0)
    per_tile = tile // PAGE_TOK
    n_full = counts[0]
    n_tiles = counts[1]
    src_slots = x_ref.shape[1]

    @pl.when(step == 0)
    def _():
        row = lax.broadcasted_iota(jnp.int32, (2 * PAGE_TOK, 2 * PAGE_TOK), 0)
        col = lax.broadcasted_iota(jnp.int32, (2 * PAGE_TOK, 2 * PAGE_TOK), 1)
        want = jnp.where(row < PAGE_TOK, 2 * row, 2 * (row - PAGE_TOK) + 1)
        pick = jnp.where(col == want, 1.0, 0.0).astype(jnp.bfloat16)
        ones = jnp.ones((PAGE_TOK, HEAD_DIM), jnp.bfloat16)

        def split_tile(i, carry):
            for s in range(per_tile):
                slot = order[i * per_tile + s]
                both = jnp.dot(
                    pick,
                    x_ref[slot // src_slots, slot % src_slots],
                    preferred_element_type=jnp.float32,
                ).astype(jnp.bfloat16)
                at = pl.multiple_of(i * tile + s * PAGE_TOK, PAGE_TOK)
                k_s[pl.ds(at, PAGE_TOK), :] = both[:PAGE_TOK]
                v_s[pl.ds(at, PAGE_TOK), :HEAD_DIM] = both[PAGE_TOK:]
                v_s[pl.ds(at, PAGE_TOK), HEAD_DIM:] = ones
            return carry

        lax.fori_loop(0, n_tiles, split_tile, 0)

    total = GROUP * tok
    if first:
        m_s[...] = jnp.full(m_s.shape, FLOOR, jnp.float32)
        acc_s[...] = jnp.zeros(acc_s.shape, jnp.float32)
    else:
        acc_s[...] = carried[0][0]
        m_s[...] = carried[1][0]

    scale = HEAD_DIM**-0.5 * LOG2E

    def tile_step(i, carry, masked):
        at = pl.multiple_of(i * tile, tile)
        keys = k_s[pl.ds(at, tile), :]
        values = v_s[pl.ds(at, tile), :]
        if masked:
            visible = kpos_ref[pl.ds(i, 1), :] <= qpos_ref[0]
            visible = jnp.concatenate([visible] * (rows // tok), axis=0)
        for part in range(total // rows):
            span = slice(part * rows, (part + 1) * rows)
            scores = lax.dot_general(
                q_ref[0, span, :],
                keys,
                (((1,), (1,)), ((), ())),
                preferred_element_type=jnp.float32,
            )
            if masked:
                scores = jnp.where(visible, scores, FLOOR)
            m_old = m_s[span, :]
            m_new = jnp.maximum(m_old, jnp.max(scores, axis=1, keepdims=True) * scale)
            shift = jnp.maximum(m_new, 0.5 * FLOOR * scale)[:, :1]
            weights = jnp.exp2(scores * scale - shift).astype(jnp.bfloat16)
            alpha = jnp.exp2(m_old - m_new)
            mixed = jnp.dot(weights, values, preferred_element_type=jnp.float32)
            acc_s[span, :HEAD_DIM] = acc_s[span, :HEAD_DIM] * alpha + mixed[:, :HEAD_DIM]
            acc_s[span, HEAD_DIM:] = acc_s[span, HEAD_DIM:] * alpha + mixed[:, HEAD_DIM:]
            m_s[span, :] = m_new
        return carry

    lax.fori_loop(0, n_full, functools.partial(tile_step, masked=False), 0)
    lax.fori_loop(n_full, n_tiles, functools.partial(tile_step, masked=True), 0)

    if not last:
        outs[0][0] = acc_s[...]
        outs[1][0] = m_s[...]
    else:
        out_ref, ml_ref = outs
        out_ref[0] = acc_s[:, :HEAD_DIM].astype(jnp.bfloat16)
        row = lax.broadcasted_iota(jnp.int32, (tok, HEAD_DIM), 0)
        col = lax.broadcasted_iota(jnp.int32, (tok, HEAD_DIM), 1)
        eye = row == col
        for g in range(GROUP):
            span = slice(g * tok, (g + 1) * tok)
            ml_ref[0, 0, g : g + 1, :] = jnp.sum(
                jnp.where(eye, m_s[span, :], 0.0), axis=0, keepdims=True
            )
            ml_ref[0, 1, g : g + 1, :] = jnp.sum(
                jnp.where(eye, acc_s[span, HEAD_DIM:], 0.0), axis=0, keepdims=True
            )


def attend(x, q, qpos, kpos, order, counts, carried, last, tile, rows):
    sources, src_slots = x.shape[:2]
    steps, total, _ = q.shape
    tok = total // GROUP
    first = carried is None
    n_slots = sources * src_slots
    spec3 = lambda i, *_: (i, 0, 0)
    spec4 = lambda i, *_: (i, 0, 0, 0)
    fixed2 = lambda i, *_: (0, 0)
    in_specs = [
        pl.BlockSpec(x.shape, lambda i, *_: (0, 0, 0, 0)),
        pl.BlockSpec((1, total, HEAD_DIM), spec3),
        pl.BlockSpec((1, tok, 1), spec3),
        pl.BlockSpec(kpos.shape, fixed2),
    ]
    if last:
        out_shape = (
            jax.ShapeDtypeStruct((steps, total, HEAD_DIM), jnp.bfloat16),
            jax.ShapeDtypeStruct((steps, 2, GROUP, HEAD_DIM), jnp.float32),
        )
        out_specs = (
            pl.BlockSpec((1, total, HEAD_DIM), spec3),
            pl.BlockSpec((1, 2, GROUP, HEAD_DIM), spec4),
        )
    else:
        out_shape = (
            jax.ShapeDtypeStruct((steps, total, 2 * HEAD_DIM), jnp.float32),
            jax.ShapeDtypeStruct((steps, total, HEAD_DIM), jnp.float32),
        )
        out_specs = (
            pl.BlockSpec((1, total, 2 * HEAD_DIM), spec3),
            pl.BlockSpec((1, total, HEAD_DIM), spec3),
        )
    extra = ()
    if not first:
        extra = tuple(carried)
        in_specs += [
            pl.BlockSpec((1, total, 2 * HEAD_DIM), spec3),
            pl.BlockSpec((1, total, HEAD_DIM), spec3),
        ]
    flops = 4 * steps * total * n_slots * PAGE_TOK * HEAD_DIM
    return pl.pallas_call(
        functools.partial(
            attend_kernel, first=first, last=last, tile=tile, rows=rows, tok=tok
        ),
        out_shape=out_shape,
        grid_spec=pltpu.PrefetchScalarGridSpec(
            num_scalar_prefetch=2,
            grid=(steps,),
            in_specs=in_specs,
            out_specs=out_specs,
            scratch_shapes=[
                pltpu.VMEM((n_slots * PAGE_TOK, HEAD_DIM), jnp.bfloat16),
                pltpu.VMEM((n_slots * PAGE_TOK, 2 * HEAD_DIM), jnp.bfloat16),
                pltpu.VMEM((total, 2 * HEAD_DIM), jnp.float32),
                pltpu.VMEM((total, HEAD_DIM), jnp.float32),
            ],
        ),
        cost_estimate=pl.CostEstimate(
            flops=flops,
            transcendentals=flops // (4 * HEAD_DIM),
            bytes_accessed=x.size * 2 + q.size * 2,
        ),
        name="attend_last" if last else "attend_first",
    )(order, counts, x, q, qpos, kpos, *extra)


def project_kernel(*refs, parts, tok):
    outs = refs[:parts]
    mls = refs[parts : 2 * parts]
    ws = refs[2 * parts : 3 * parts]
    keep_ref, send_ref, a_s = refs[3 * parts :]

    @pl.when(pl.program_id(0) == 0)
    def _():
        row = lax.broadcasted_iota(jnp.int32, (tok, HEAD_DIM), 0)
        col = lax.broadcasted_iota(jnp.int32, (tok, HEAD_DIM), 1)
        eye = row == col
        for g in range(GROUP):
            ms = [ml[0, g : g + 1, :] for ml in mls]
            top = functools.reduce(jnp.maximum, ms)
            factors = [jnp.exp2(m - top) for m in ms]
            total = sum(f * ml[1, g : g + 1, :] for f, ml in zip(factors, mls))
            span = slice(g * tok, (g + 1) * tok)
            mixed = 0.0
            for f, out in zip(factors, outs):
                ratio = jnp.where(eye, f / total, 0.0)
                mixed += jnp.sum(ratio, axis=1, keepdims=True) * out[span, :].astype(
                    jnp.float32
                )
            a_s[:, g * HEAD_DIM : (g + 1) * HEAD_DIM] = mixed.astype(jnp.bfloat16)

    depth = a_s.shape[1] // parts
    total = 0.0
    for s in range(parts):
        total += jnp.dot(
            a_s[:, s * depth : (s + 1) * depth], ws[s][...], preferred_element_type=jnp.float32
        )
    half = tok // 2
    keep_ref[...] = total[:half]
    send_ref[...] = total[half:].astype(jnp.bfloat16)


def project(outs, mls, ws, tok, width):
    parts = len(outs)
    columns = ws[0].shape[1]
    fixed2 = lambda i: (0, 0)
    fixed3 = lambda i: (0, 0, 0)
    half = tok // 2
    depth = sum(w.shape[0] for w in ws)
    return pl.pallas_call(
        functools.partial(project_kernel, parts=parts, tok=tok),
        out_shape=(
            jax.ShapeDtypeStruct((half, columns), jnp.float32),
            jax.ShapeDtypeStruct((half, columns), jnp.bfloat16),
        ),
        grid=(columns // width,),
        in_specs=[pl.BlockSpec(o.shape, fixed2) for o in outs]
        + [pl.BlockSpec(m.shape, fixed3) for m in mls]
        + [pl.BlockSpec((w.shape[0], width), lambda i: (0, i)) for w in ws],
        out_specs=(
            pl.BlockSpec((half, width), lambda i: (0, i)),
            pl.BlockSpec((half, width), lambda i: (0, i)),
        ),
        scratch_shapes=[pltpu.VMEM((tok, depth), jnp.bfloat16)],
        cost_estimate=pl.CostEstimate(
            flops=2 * tok * depth * columns, transcendentals=0, bytes_accessed=2 * depth * columns
        ),
        name="project",
    )(*outs, *mls, *ws)


def migrate_pages(kv_cache, outgoing, slot_page_after, move_in, n):
    slot_ids = jnp.arange(kv_cache.shape[0], dtype=jnp.int32)
    arranged = jnp.where(
        (slot_page_after >= 0)[:, None, None, None], kv_cache, jnp.zeros((), kv_cache.dtype)
    )
    for offset in range(1, MOVE_WIN + 1):
        arrived = permute_to(outgoing[offset - 1], n, lambda i: (i + offset) % n)
        landing = (slot_ids == move_in[0, offset - 1])[:, None, None, None]
        arranged = jnp.where(landing, arrived[None], arranged)
    return arranged


def local(
    queries, kv_cache, w_out, slot_page_before, slot_page_after, move_out, move_in, positions
):
    n = lax.axis_size("pages")
    slots = kv_cache.shape[0]
    ways = n // KV_HEADS
    tok_rows = BLOCK // n
    tok = BLOCK // ways
    gp = GROUP // ways
    me = lax.axis_index("pages")
    u = me // KV_HEADS
    j = me % KV_HEADS
    head = head_of(j)
    groups = [[a * KV_HEADS + b for b in range(KV_HEADS)] for a in range(ways)]
    dest_head = [head_of(b) for b in range(KV_HEADS)]

    chunks = 2
    per = slots // chunks
    by_head = kv_cache.reshape(slots, PAGE_TOK, 2, KV_HEADS, HEAD_DIM)
    by_head = jnp.transpose(by_head, (3, 0, 1, 2, 4))
    by_dest = jnp.concatenate([by_head[h : h + 1] for h in dest_head], axis=0)
    arrived = []
    for c in range(chunks):
        piece = by_dest[:, c * per : (c + 1) * per]
        got = lax.all_to_all(
            piece, "pages", 0, 0, axis_index_groups=groups, tiled=True
        )
        arrived.append(got.reshape(KV_HEADS, per, 2 * PAGE_TOK, HEAD_DIM))
    table = lax.all_to_all(
        jnp.broadcast_to(slot_page_before[None, None], (KV_HEADS, 1, slots)),
        "pages",
        0,
        0,
        axis_index_groups=groups,
        tiled=True,
    ).reshape(KV_HEADS, slots)

    xs = lambda m: jnp.arange(m, dtype=jnp.int32)
    t_of = u ^ xs(ways)
    kx = (xs(KV_HEADS) % (KV_HEADS // 2)) * 2 + xs(KV_HEADS) // (KV_HEADS // 2)
    owner = (kx[None, :] ^ head) * ways + t_of[:, None]
    g_of = ((xs(GROUP) // gp)[None, :] ^ t_of[:, None]) * gp + (xs(GROUP) % gp)[None, :]
    mine = lax.dynamic_slice_in_dim(queries, head * GROUP * HEAD_DIM, GROUP * HEAD_DIM, axis=2)
    mine = mine.reshape(2, n, tok_rows, GROUP, HEAD_DIM)
    pos = positions.reshape(2, n, tok_rows)
    q_rows = []
    q_pos = []
    for tx in range(ways):
        taken = jnp.take(jnp.take(mine, owner[tx], axis=1), g_of[tx], axis=3)
        q_rows.append(jnp.transpose(taken, (0, 3, 1, 2, 4)).reshape(2, GROUP * tok, HEAD_DIM))
        q_pos.append(jnp.take(pos, owner[tx], axis=1).reshape(2, tok, 1))
    q = jnp.concatenate(q_rows, axis=0)
    qpos = jnp.concatenate(q_pos, axis=0)

    tile = 1024
    rows = 2 * tok
    lowest = jnp.min(positions)
    carried = None
    for c in range(chunks):
        pages = table[:, c * per : (c + 1) * per].reshape(-1)
        live = pages >= 0
        full = live & (pages * PAGE_TOK + (PAGE_TOK - 1) <= lowest)
        rank = jnp.where(full, 0, jnp.where(live, 1, 2))
        order = jnp.argsort(rank, stable=True).astype(jnp.int32)
        n_live = jnp.sum(live.astype(jnp.int32)) * PAGE_TOK
        n_full = jnp.sum(full.astype(jnp.int32)) * PAGE_TOK
        counts = jnp.stack([n_full // tile, (n_live + tile - 1) // tile]).astype(jnp.int32)
        start = jnp.where(live, pages * PAGE_TOK, FAR)[order]
        kpos = (start[:, None] + xs(PAGE_TOK)[None, :]).reshape(-1, tile)
        carried = attend(
            arrived[c], q, qpos, kpos, order, counts, carried, c == chunks - 1, tile, rows
        )
    out, ml = carried
    out = out.reshape(ways, 2, GROUP * tok, HEAD_DIM)
    ml = ml.reshape(ways, 2, 2, GROUP, HEAD_DIM)

    ws = [w_out] + [permute_to(w_out, n, lambda i: i ^ s) for s in range(1, ways)]

    def merger(i, s):
        return head_of(i % KV_HEADS) * ways + ((i // KV_HEADS) ^ s)

    results = []
    for b in range(2):
        got_out = [permute_to(out[s, b], n, lambda i: merger(i, s)) for s in range(ways)]
        got_ml = [permute_to(ml[s, b], n, lambda i: merger(i, s)) for s in range(ways)]
        keep, send = project(got_out, got_ml, ws, tok, 1024)
        got = permute_to(send, n, lambda i: i ^ ways)
        total = (keep + got.astype(jnp.float32)).reshape(KV_HEADS // 2, tok_rows, D)
        mine_rows = total[0]
        for zx in range(1, KV_HEADS // 2):
            got = permute_to(
                total[zx].astype(jnp.bfloat16), n, lambda i: i ^ (zx * 2 * ways)
            )
            mine_rows = mine_rows + got.astype(jnp.float32)
        results.append(mine_rows.astype(jnp.bfloat16))

    outgoing = kv_cache[jnp.maximum(move_out[0], 0)]
    cache_after = migrate_pages(kv_cache, outgoing, slot_page_after, move_in, n)
    return (jnp.stack(results), cache_after)


def solution(mesh):
    in_specs = (
        P(None, "groups", None),
        P(("groups", "pages"), None, None, None),
        P("pages", None),
        P(("groups", "pages")),
        P(("groups", "pages")),
        P(("groups", "pages"), None),
        P(("groups", "pages"), None),
        P(None, "groups"),
    )
    out_specs = (P(None, ("groups", "pages"), None), P(("groups", "pages"), None, None, None))
    return jax.shard_map(local, mesh=mesh, in_specs=in_specs, out_specs=out_specs, check_vma=False)
```

```python
import functools

import jax
import jax.numpy as jnp
from jax import lax
from jax.experimental import pallas as pl
from jax.experimental.pallas import tpu as pltpu
from jax.sharding import PartitionSpec as P

HEADS = 64
KV_HEADS = 8
HEAD_DIM = 128
D = 8192
PAGE_TOK = 128
BLOCK = 256
MOVE_WIN = 4
GROUP = HEADS // KV_HEADS

FLOOR = -1e30
FAR = 1 << 30
SCALE = HEAD_DIM**-0.5 * 1.4426950408889634

WIDE = 16
NARROW = 8
FIRST_SLOTS = 5
COLUMN_PARTS = 2

ANY = pl.BlockSpec(memory_space=pl.ANY)


def permute_to(x, n, target):
    return lax.ppermute(x, "pages", [(i, target(i)) for i in range(n)])


def head_of(j):
    half = KV_HEADS // 2
    return (j % 2) * half + j // 2


def split_heads_kernel(kv_ref, out_ref, sems, *, first):
    copies = []
    for d in range(KV_HEADS):
        copies.append(
            pltpu.make_async_copy(
                kv_ref.at[
                    pl.ds(first, out_ref.shape[1]),
                    :,
                    :,
                    pl.ds(head_of(d) * HEAD_DIM, HEAD_DIM),
                ],
                out_ref.at[d],
                sems.at[d],
            )
        )
    for copy in copies:
        copy.start()
    for copy in copies:
        copy.wait()


def split_heads(kv_cache, first, count):
    return pl.pallas_call(
        functools.partial(split_heads_kernel, first=first),
        out_shape=jax.ShapeDtypeStruct(
            (KV_HEADS, count, PAGE_TOK, 2, HEAD_DIM), kv_cache.dtype
        ),
        in_specs=[ANY],
        out_specs=ANY,
        scratch_shapes=[pltpu.SemaphoreType.DMA((KV_HEADS,))],
        name="split_heads",
    )(kv_cache)


def outgoing_kernel(move_out, kv_ref, after_ref, *refs):
    outs, sems = refs[:MOVE_WIN], refs[MOVE_WIN]
    copies = [
        pltpu.make_async_copy(
            kv_ref.at[jnp.maximum(move_out[o], 0)], outs[o], sems.at[o]
        )
        for o in range(MOVE_WIN)
    ]
    for copy in copies:
        copy.start()
    for copy in copies:
        copy.wait()


def outgoing_pages(kv_cache, move_out, after):
    page = jax.ShapeDtypeStruct(kv_cache.shape[1:], kv_cache.dtype)
    return pl.pallas_call(
        outgoing_kernel,
        out_shape=(page,) * MOVE_WIN,
        grid_spec=pltpu.PrefetchScalarGridSpec(
            num_scalar_prefetch=1,
            grid=(),
            in_specs=[ANY, ANY],
            out_specs=(ANY,) * MOVE_WIN,
            scratch_shapes=[pltpu.SemaphoreType.DMA((MOVE_WIN,))],
        ),
        name="outgoing_pages",
    )(move_out, kv_cache, after)


def arrange_kernel(page_after, move_in, kv_ref, *refs):
    arrived = refs[:MOVE_WIN]
    _, out_ref, zero_ref, sems = refs[MOVE_WIN:]
    zero_ref[...] = jnp.zeros(zero_ref.shape, zero_ref.dtype)
    slots = out_ref.shape[0]
    for s in range(slots):
        taken = jnp.zeros((), jnp.bool_)
        for o in reversed(range(MOVE_WIN)):
            lands = move_in[o] == s

            @pl.when(lands & jnp.logical_not(taken))
            def _():
                pltpu.make_async_copy(arrived[o], out_ref.at[s], sems.at[s]).start()

            taken = taken | lands
        kept = page_after[s] >= 0

        @pl.when(kept & jnp.logical_not(taken))
        def _():
            pltpu.make_async_copy(kv_ref.at[s], out_ref.at[s], sems.at[s]).start()

        @pl.when(jnp.logical_not(kept | taken))
        def _():
            pltpu.make_async_copy(zero_ref, out_ref.at[s], sems.at[s]).start()

    for s in range(slots):
        pltpu.make_async_copy(kv_ref.at[s], out_ref.at[s], sems.at[s]).wait()


def arrange_pages(kv_cache, arrived, page_after, move_in, after):
    return pl.pallas_call(
        arrange_kernel,
        out_shape=jax.ShapeDtypeStruct(kv_cache.shape, kv_cache.dtype),
        grid_spec=pltpu.PrefetchScalarGridSpec(
            num_scalar_prefetch=2,
            grid=(),
            in_specs=[ANY] * (2 + MOVE_WIN),
            out_specs=ANY,
            scratch_shapes=[
                pltpu.VMEM(kv_cache.shape[1:], kv_cache.dtype),
                pltpu.SemaphoreType.DMA((kv_cache.shape[0],)),
            ],
        ),
        name="arrange_pages",
    )(page_after, move_in, kv_cache, *arrived, after)


def three_parts(x):
    high = x.astype(jnp.bfloat16)
    rest = x - high.astype(jnp.float32)
    mid = rest.astype(jnp.bfloat16)
    low = (rest - mid.astype(jnp.float32)).astype(jnp.bfloat16)
    return high, mid, low


def attend_kernel(
    pages, place, x_ref, q_ref, *refs, first, last, rows, tok, ways, tok_rows, block
):
    n_in = 0 if first else 2
    carried = refs[:n_in]
    outs = refs[n_in : n_in + (1 if last else 2)]
    k_s, v_s, acc_s, m_s, order, counts = refs[n_in + len(outs) :]
    step = pl.program_id(0)
    src_slots = x_ref.shape[1]
    n_slots = x_ref.shape[0] * src_slots
    head, way = place[0], place[1]

    @pl.when(step == 0)
    def _():
        lowest = jnp.minimum(place[2], place[3])

        def fully(page):
            return (page >= 0) & (page * PAGE_TOK + (PAGE_TOK - 1) <= lowest)

        def put_full(i, count):
            yes = fully(pages[i])

            @pl.when(yes)
            def _():
                order[count] = i

            return count + yes.astype(jnp.int32)

        def put_rest(i, count):
            yes = (pages[i] >= 0) & jnp.logical_not(fully(pages[i]))

            @pl.when(yes)
            def _():
                order[count] = i

            return count + yes.astype(jnp.int32)

        n_full = lax.fori_loop(0, n_slots, put_full, 0)
        n_live = lax.fori_loop(0, n_slots, put_rest, n_full)
        counts[0] = n_full
        counts[1] = n_live

        row = lax.broadcasted_iota(jnp.int32, (2 * PAGE_TOK, 2 * PAGE_TOK), 0)
        col = lax.broadcasted_iota(jnp.int32, (2 * PAGE_TOK, 2 * PAGE_TOK), 1)
        want = jnp.where(row < PAGE_TOK, 2 * row, 2 * (row - PAGE_TOK) + 1)
        pick = jnp.where(col == want, 1.0, 0.0).astype(jnp.bfloat16)
        ones = jnp.ones((PAGE_TOK, HEAD_DIM), jnp.bfloat16)

        def split_step(i, carry):
            for s in range(NARROW):
                at = i * NARROW + s
                slot = order[jnp.minimum(at, n_live - 1)]
                both = jnp.dot(
                    pick,
                    x_ref[slot // src_slots, slot % src_slots],
                    preferred_element_type=jnp.float32,
                ).astype(jnp.bfloat16)
                to = pl.ds(pl.multiple_of(at * PAGE_TOK, PAGE_TOK), PAGE_TOK)
                k_s[to, :] = both[:PAGE_TOK]
                v_s[to, :HEAD_DIM] = both[PAGE_TOK:]
                v_s[to, HEAD_DIM:] = ones
            return carry

        lax.fori_loop(0, (n_live + NARROW - 1) // NARROW, split_step, 0)

    n_full, n_live = counts[0], counts[1]
    total = GROUP * tok
    if first:
        m_s[...] = jnp.full(m_s.shape, FLOOR, jnp.float32)
        acc_s[...] = jnp.zeros(acc_s.shape, jnp.float32)
    else:
        acc_s[...] = carried[0][0]
        m_s[...] = carried[1][0]

    if block is None:
        t_rel, b = step // 2, step % 2
    else:
        t_rel, b = step, block
    line = lax.broadcasted_iota(jnp.int32, (tok, PAGE_TOK), 0)
    p = line // tok_rows
    kx = (p % (KV_HEADS // 2)) * 2 + p // (KV_HEADS // 2)
    token = ((kx ^ head) * ways + (t_rel ^ way)) * tok_rows + line % tok_rows
    q_at = token + jnp.where(b == 0, place[2], place[3])

    def tile_step(at, size, masked):
        span_k = pl.ds(pl.multiple_of(at * PAGE_TOK, PAGE_TOK), size * PAGE_TOK)
        keys = k_s[span_k, :]
        values = v_s[span_k, :]
        if masked:
            lane = lax.broadcasted_iota(jnp.int32, (tok, PAGE_TOK), 1)
            visible = []
            for s in range(size):
                slot = order[jnp.minimum(at + s, n_live - 1)]
                start = jnp.where(at + s < n_live, pages[slot] * PAGE_TOK, FAR)
                seen = lane + start <= q_at
                visible.append(jnp.concatenate([seen] * (rows // tok), axis=0))

        def score(part):
            return lax.dot_general(
                q_ref[0, part * rows : (part + 1) * rows, :],
                keys,
                (((1,), (1,)), ((), ())),
                preferred_element_type=jnp.float32,
            )

        def soften(part, scores):
            span = slice(part * rows, (part + 1) * rows)
            pieces = [scores[:, s * PAGE_TOK : (s + 1) * PAGE_TOK] for s in range(size)]
            if masked:
                pieces = [jnp.where(v, x, FLOOR) for v, x in zip(visible, pieces)]
            peak = functools.reduce(jnp.maximum, pieces)
            m_old = m_s[span, :]
            m_new = jnp.maximum(m_old, jnp.max(peak, axis=1, keepdims=True) * SCALE)
            shift = jnp.maximum(m_new, 0.5 * FLOOR * SCALE) if masked else m_new
            weights = jnp.concatenate(
                [jnp.exp2(x * SCALE - shift).astype(jnp.bfloat16) for x in pieces], axis=1
            )
            m_s[span, :] = m_new
            return weights, jnp.exp2(m_old - m_new)

        def gather(part, weights, alpha):
            span = slice(part * rows, (part + 1) * rows)
            mixed = jnp.dot(weights, values, preferred_element_type=jnp.float32)
            acc_s[span, :HEAD_DIM] = acc_s[span, :HEAD_DIM] * alpha + mixed[:, :HEAD_DIM]
            acc_s[span, HEAD_DIM:] = acc_s[span, HEAD_DIM:] * alpha + mixed[:, HEAD_DIM:]

        parts = total // rows
        scores = score(0)
        waiting = None
        for part in range(parts):
            following = score(part + 1) if part + 1 < parts else None
            weights, alpha = soften(part, scores)
            if waiting is not None:
                gather(*waiting)
            waiting = (part, weights, alpha)
            scores = following
        gather(*waiting)

    n_wide = n_full // WIDE
    n_open = (n_full - n_wide * WIDE) // NARROW
    base = n_wide * WIDE
    done = base + n_open * NARROW
    n_masked = (n_live - done + NARROW - 1) // NARROW

    def wide(i, carry):
        tile_step(i * WIDE, WIDE, False)
        return carry

    def narrow(i, carry):
        tile_step(base + i * NARROW, NARROW, False)
        return carry

    def masked(i, carry):
        tile_step(done + i * NARROW, NARROW, True)
        return carry

    lax.fori_loop(0, n_wide, wide, 0)
    lax.fori_loop(0, n_open, narrow, 0)
    lax.fori_loop(0, n_masked, masked, 0)

    if not last:
        outs[0][0] = acc_s[...]
        outs[1][0] = m_s[...]
    else:
        out_ref = outs[0]
        out_ref[0, :total, :] = acc_s[:, :HEAD_DIM].astype(jnp.bfloat16)
        row = lax.broadcasted_iota(jnp.int32, (tok, HEAD_DIM), 0)
        col = lax.broadcasted_iota(jnp.int32, (tok, HEAD_DIM), 1)
        eye = row == col
        lines = []
        for ref, lanes in ((m_s, slice(0, HEAD_DIM)), (acc_s, slice(HEAD_DIM, 2 * HEAD_DIM))):
            for g in range(GROUP):
                span = slice(g * tok, (g + 1) * tok)
                lines.append(
                    jnp.sum(jnp.where(eye, ref[span, lanes], 0.0), axis=0, keepdims=True)
                )
        stats = jnp.concatenate(lines, axis=0)
        for i, piece in enumerate(three_parts(stats)):
            at = total + i * 2 * GROUP
            out_ref[0, at : at + 2 * GROUP, :] = piece


def attend(pages, place, x, q, carried, block, tok_rows, rows):
    sources, src_slots = x.shape[:2]
    steps, total, _ = q.shape
    tok = total // GROUP
    first = carried is None
    last = block is not None
    ways = steps // 2
    pad = WIDE - 1
    n_slots = -(-sources * src_slots // WIDE) * WIDE
    if last:
        grid = ways
        at = lambda i, *_: (2 * i + block, 0, 0)
    else:
        grid = steps
        at = lambda i, *_: (i, 0, 0)
    straight = lambda i, *_: (i, 0, 0)
    in_specs = [
        pl.BlockSpec(x.shape, lambda i, *_: (0, 0, 0, 0)),
        pl.BlockSpec((1, total, HEAD_DIM), at),
    ]
    sent = total + 3 * 2 * GROUP
    if last:
        out_shape = (jax.ShapeDtypeStruct((ways, sent, HEAD_DIM), jnp.bfloat16),)
        out_specs = (pl.BlockSpec((1, sent, HEAD_DIM), straight),)
    else:
        out_shape = (
            jax.ShapeDtypeStruct((steps, total, 2 * HEAD_DIM), jnp.float32),
            jax.ShapeDtypeStruct((steps, total, HEAD_DIM), jnp.float32),
        )
        out_specs = (
            pl.BlockSpec((1, total, 2 * HEAD_DIM), at),
            pl.BlockSpec((1, total, HEAD_DIM), at),
        )
    extra = ()
    if not first:
        extra = tuple(carried)
        in_specs += [
            pl.BlockSpec((1, total, 2 * HEAD_DIM), at),
            pl.BlockSpec((1, total, HEAD_DIM), at),
        ]
    flops = 8 * grid * total * sources * src_slots * PAGE_TOK * HEAD_DIM
    return pl.pallas_call(
        functools.partial(
            attend_kernel,
            first=first,
            last=last,
            rows=rows,
            tok=tok,
            ways=ways,
            tok_rows=tok_rows,
            block=block,
        ),
        out_shape=out_shape,
        grid_spec=pltpu.PrefetchScalarGridSpec(
            num_scalar_prefetch=2,
            grid=(grid,),
            in_specs=in_specs,
            out_specs=out_specs,
            scratch_shapes=[
                pltpu.VMEM((n_slots * PAGE_TOK, HEAD_DIM), jnp.bfloat16),
                pltpu.VMEM((n_slots * PAGE_TOK, 2 * HEAD_DIM), jnp.bfloat16),
                pltpu.VMEM((total, 2 * HEAD_DIM), jnp.float32),
                pltpu.VMEM((total, HEAD_DIM), jnp.float32),
                pltpu.SMEM((n_slots,), jnp.int32),
                pltpu.SMEM((2,), jnp.int32),
            ],
        ),
        cost_estimate=pl.CostEstimate(
            flops=flops, transcendentals=flops // (8 * HEAD_DIM), bytes_accessed=x.size * 2
        ),
        name="attend_last" if last else "attend_first",
    )(pages, place, x, q, *extra)


def merge(parts, a_ref, tok):
    total = GROUP * tok
    row = lax.broadcasted_iota(jnp.int32, (tok, HEAD_DIM), 0)
    col = lax.broadcasted_iota(jnp.int32, (tok, HEAD_DIM), 1)
    eye = row == col
    stats = []
    for part in parts:
        pieces = [
            part[total + i * 2 * GROUP : total + (i + 1) * 2 * GROUP, :].astype(jnp.float32)
            for i in range(3)
        ]
        stats.append((pieces[0] + pieces[1]) + pieces[2])
    tops = functools.reduce(jnp.maximum, [s[:GROUP] for s in stats])
    factors = [jnp.exp2(s[:GROUP] - tops) for s in stats]
    totals = sum(f * s[GROUP:] for f, s in zip(factors, stats))
    for g in range(GROUP):
        span = slice(g * tok, (g + 1) * tok)
        mixed = 0.0
        for f, part in zip(factors, parts):
            ratio = jnp.where(eye, f[g : g + 1] / totals[g : g + 1], 0.0)
            mixed += jnp.sum(ratio, axis=1, keepdims=True) * part[span, :].astype(jnp.float32)
        a_ref[:, g * HEAD_DIM : (g + 1) * HEAD_DIM] = mixed.astype(jnp.bfloat16)


def project_kernel(*refs, n_parts, n_ws, tok):
    parts = refs[:n_parts]
    ws = refs[n_parts : n_parts + n_ws]
    outs = refs[n_parts + n_ws :]
    keep_ref, send_ref = outs[:2]
    if n_parts == n_ws:
        a_ref = outs[2]

        @pl.when(pl.program_id(0) == 0)
        def _():
            merge(parts, a_ref, tok)

    else:
        a_ref = parts[0]
    depth = a_ref.shape[1] // n_ws
    total = 0.0
    for s in range(n_ws):
        total += jnp.dot(
            a_ref[:, s * depth : (s + 1) * depth], ws[s][...], preferred_element_type=jnp.float32
        )
    half = tok // 2
    keep_ref[...] = total[:half]
    send_ref[...] = total[half:].astype(jnp.bfloat16)


def project(parts, ws, tok, column_part, width=1024):
    columns = ws[0].shape[1] // COLUMN_PARTS
    steps = columns // width
    fixed = lambda i: (0, 0)
    half = tok // 2
    depth = sum(w.shape[0] for w in ws)
    merging = len(parts) == len(ws)
    out_shape = [
        jax.ShapeDtypeStruct((half, columns), jnp.float32),
        jax.ShapeDtypeStruct((half, columns), jnp.bfloat16),
    ]
    out_specs = [
        pl.BlockSpec((half, width), lambda i: (0, i)),
        pl.BlockSpec((half, width), lambda i: (0, i)),
    ]
    if merging:
        out_shape.append(jax.ShapeDtypeStruct((tok, depth), jnp.bfloat16))
        out_specs.append(pl.BlockSpec((tok, depth), fixed))
    return pl.pallas_call(
        functools.partial(project_kernel, n_parts=len(parts), n_ws=len(ws), tok=tok),
        out_shape=out_shape,
        grid=(steps,),
        in_specs=[pl.BlockSpec(o.shape, fixed) for o in parts]
        + [
            pl.BlockSpec((w.shape[0], width), lambda i: (0, column_part * steps + i)) for w in ws
        ],
        out_specs=out_specs,
        cost_estimate=pl.CostEstimate(
            flops=2 * tok * depth * columns, transcendentals=0, bytes_accessed=2 * depth * columns
        ),
        name="project",
    )(*parts, *ws)


def local(
    queries, kv_cache, w_out, slot_page_before, slot_page_after, move_out, move_in, positions
):
    n = lax.axis_size("pages")
    slots = kv_cache.shape[0]
    ways = n // KV_HEADS
    tok_rows = BLOCK // n
    tok = BLOCK // ways
    gp = GROUP // ways
    me = lax.axis_index("pages")
    way = me // KV_HEADS
    head = head_of(me % KV_HEADS)
    groups = [[a * KV_HEADS + b for b in range(KV_HEADS)] for a in range(ways)]

    def exchange(x):
        return lax.all_to_all(x, "pages", 0, 0, axis_index_groups=groups, tiled=True)

    cuts = [(0, FIRST_SLOTS), (FIRST_SLOTS, slots - FIRST_SLOTS)]
    pieces = [split_heads(kv_cache, at, count) for at, count in cuts]
    arrived = [
        exchange(piece).reshape(KV_HEADS, count, 2 * PAGE_TOK, HEAD_DIM)
        for piece, (_, count) in zip(pieces, cuts)
    ]
    table_in, _ = lax.optimization_barrier((slot_page_before, pieces[0]))
    table = exchange(jnp.broadcast_to(table_in[None, None], (KV_HEADS, 1, slots)))
    table = table.reshape(KV_HEADS, slots)
    place = jnp.stack([head, way, positions[0, 0], positions[1, 0]]).astype(jnp.int32)

    xs = lambda m: jnp.arange(m, dtype=jnp.int32)
    t_of = way ^ xs(ways)
    kx = (xs(KV_HEADS) % (KV_HEADS // 2)) * 2 + xs(KV_HEADS) // (KV_HEADS // 2)
    owner = (kx[None, :] ^ head) * ways + t_of[:, None]
    g_of = ((xs(GROUP) // gp)[None, :] ^ t_of[:, None]) * gp + (xs(GROUP) % gp)[None, :]
    mine = lax.dynamic_slice_in_dim(queries, head * GROUP * HEAD_DIM, GROUP * HEAD_DIM, axis=2)
    mine = mine.reshape(2, n, tok_rows, GROUP, HEAD_DIM)
    q_rows = []
    for tx in range(ways):
        taken = jnp.take(jnp.take(mine, owner[tx], axis=1), g_of[tx], axis=3)
        q_rows.append(jnp.transpose(taken, (0, 3, 1, 2, 4)).reshape(2, GROUP * tok, HEAD_DIM))
    q = jnp.concatenate(q_rows, axis=0)

    rows = 2 * tok
    pages = [table[:, at : at + count].reshape(-1) for at, count in cuts]
    carried = attend(pages[0], place, arrived[0], q, None, None, tok_rows, rows)

    leaving = outgoing_pages(kv_cache, move_out[0], arrived[0])
    landed = [
        permute_to(leaving[o - 1], n, lambda i: (i + o) % n) for o in range(1, MOVE_WIN + 1)
    ]

    ws = [w_out] + [permute_to(w_out, n, lambda i: i ^ s) for s in range(1, ways)]

    def merger(i, s):
        return head_of(i % KV_HEADS) * ways + ((i // KV_HEADS) ^ s)

    partial = []
    for b in range(2):
        (out,) = attend(pages[1], place, arrived[1], q, carried, b, tok_rows, rows)
        partial.append([permute_to(out[s], n, lambda i: merger(i, s)) for s in range(ways)])

    results = []
    for b in range(2):
        merged = partial[b]
        columns = []
        for c in range(COLUMN_PARTS):
            keep, send, *a = project(merged, ws, tok, c)
            if a:
                merged = a
            got = permute_to(send, n, lambda i: i ^ ways)
            total = (keep + got.astype(jnp.float32)).reshape(KV_HEADS // 2, tok_rows, -1)
            mine_rows = total[0]
            for zx in range(1, KV_HEADS // 2):
                got = permute_to(
                    total[zx].astype(jnp.bfloat16), n, lambda i: i ^ (zx * 2 * ways)
                )
                mine_rows = mine_rows + got.astype(jnp.float32)
            columns.append(mine_rows.astype(jnp.bfloat16))
        results.append(jnp.concatenate(columns, axis=1))

    cache_after = arrange_pages(kv_cache, landed, slot_page_after, move_in[0], send)
    return (jnp.stack(results), cache_after)


def solution(mesh):
    in_specs = (
        P(None, "groups", None),
        P(("groups", "pages"), None, None, None),
        P("pages", None),
        P(("groups", "pages")),
        P(("groups", "pages")),
        P(("groups", "pages"), None),
        P(("groups", "pages"), None),
        P(None, "groups"),
    )
    out_specs = (P(None, ("groups", "pages"), None), P(("groups", "pages"), None, None, None))
    return jax.shard_map(local, mesh=mesh, in_specs=in_specs, out_specs=out_specs, check_vma=False)
```

```python
import functools

import jax
import jax.numpy as jnp
from jax import lax
from jax.experimental import pallas as pl
from jax.experimental.pallas import tpu as pltpu
from jax.sharding import PartitionSpec as P

HEADS = 64
KV_HEADS = 8
HEAD_DIM = 128
PAGE_TOK = 128
BLOCK = 256
MOVE_WIN = 4
GROUP = HEADS // KV_HEADS

FLOOR = -1e30
FAR = 1 << 30
SCALE = HEAD_DIM**-0.5 * 1.4426950408889634

WIDE = 16
NARROW = 8
FIRST_SLOTS = 5
COLUMN_PARTS = 2

ANY = pl.BlockSpec(memory_space=pl.ANY)


def permute_to(x, n, target):
    return lax.ppermute(x, "pages", [(i, target(i)) for i in range(n)])


def head_of(j):
    half = KV_HEADS // 2
    return (j % 2) * half + j // 2


def split_heads_kernel(kv_ref, out_ref, buf, in_sems, out_sems, *, first):
    count = out_ref.shape[1]
    loads = [
        pltpu.make_async_copy(
            kv_ref.at[pl.ds(first, count), :, :, pl.ds(head_of(d) * HEAD_DIM, HEAD_DIM)],
            buf.at[d],
            in_sems.at[d],
        )
        for d in range(KV_HEADS)
    ]
    stores = [
        pltpu.make_async_copy(buf.at[d], out_ref.at[d], out_sems.at[d])
        for d in range(KV_HEADS)
    ]
    for load in loads:
        load.start()
    for load, store in zip(loads, stores):
        load.wait()
        store.start()
    for store in stores:
        store.wait()


def split_heads(kv_cache, first, count):
    shape = (KV_HEADS, count, PAGE_TOK, 2, HEAD_DIM)
    return pl.pallas_call(
        functools.partial(split_heads_kernel, first=first),
        out_shape=jax.ShapeDtypeStruct(shape, kv_cache.dtype),
        in_specs=[ANY],
        out_specs=ANY,
        scratch_shapes=[
            pltpu.VMEM(shape, kv_cache.dtype),
            pltpu.SemaphoreType.DMA((KV_HEADS,)),
            pltpu.SemaphoreType.DMA((KV_HEADS,)),
        ],
        name="split_heads",
    )(kv_cache)


def outgoing_kernel(move_out, kv_ref, after_ref, *refs):
    outs = refs[:MOVE_WIN]
    buf, in_sems, out_sems = refs[MOVE_WIN:]
    loads = [
        pltpu.make_async_copy(
            kv_ref.at[jnp.maximum(move_out[o], 0)], buf.at[o], in_sems.at[o]
        )
        for o in range(MOVE_WIN)
    ]
    stores = [
        pltpu.make_async_copy(buf.at[o], outs[o], out_sems.at[o]) for o in range(MOVE_WIN)
    ]
    for load in loads:
        load.start()
    for load, store in zip(loads, stores):
        load.wait()
        store.start()
    for store in stores:
        store.wait()


def outgoing_pages(kv_cache, move_out, after):
    page = jax.ShapeDtypeStruct(kv_cache.shape[1:], kv_cache.dtype)
    return pl.pallas_call(
        outgoing_kernel,
        out_shape=(page,) * MOVE_WIN,
        grid_spec=pltpu.PrefetchScalarGridSpec(
            num_scalar_prefetch=1,
            grid=(),
            in_specs=[ANY, ANY],
            out_specs=(ANY,) * MOVE_WIN,
            scratch_shapes=[
                pltpu.VMEM((MOVE_WIN,) + kv_cache.shape[1:], kv_cache.dtype),
                pltpu.SemaphoreType.DMA((MOVE_WIN,)),
                pltpu.SemaphoreType.DMA((MOVE_WIN,)),
            ],
        ),
        name="outgoing_pages",
    )(move_out, kv_cache, after)


def arrange_kernel(page_after, move_in, kv_ref, *refs):
    arrived = refs[:MOVE_WIN]
    _, out_ref, buf, zero_ref, in_sems, out_sems = refs[MOVE_WIN:]
    slots = out_ref.shape[0]
    filled = []
    for s in range(slots):
        taken = jnp.zeros((), jnp.bool_)
        for o in reversed(range(MOVE_WIN)):
            lands = move_in[o] == s

            @pl.when(lands & jnp.logical_not(taken))
            def _():
                pltpu.make_async_copy(arrived[o], buf.at[s], in_sems.at[s]).start()

            taken = taken | lands
        kept = page_after[s] >= 0

        @pl.when(kept & jnp.logical_not(taken))
        def _():
            pltpu.make_async_copy(kv_ref.at[s], buf.at[s], in_sems.at[s]).start()

        filled.append(kept | taken)
    zero_ref[...] = jnp.zeros(zero_ref.shape, zero_ref.dtype)
    for s in range(slots):

        @pl.when(filled[s])
        def _():
            pltpu.make_async_copy(kv_ref.at[s], buf.at[s], in_sems.at[s]).wait()
            pltpu.make_async_copy(buf.at[s], out_ref.at[s], out_sems.at[s]).start()

        @pl.when(jnp.logical_not(filled[s]))
        def _():
            pltpu.make_async_copy(zero_ref, out_ref.at[s], out_sems.at[s]).start()

    for s in range(slots):
        pltpu.make_async_copy(zero_ref, out_ref.at[s], out_sems.at[s]).wait()


def arrange_pages(kv_cache, arrived, page_after, move_in, after):
    slots = kv_cache.shape[0]
    return pl.pallas_call(
        arrange_kernel,
        out_shape=jax.ShapeDtypeStruct(kv_cache.shape, kv_cache.dtype),
        grid_spec=pltpu.PrefetchScalarGridSpec(
            num_scalar_prefetch=2,
            grid=(),
            in_specs=[ANY] * (2 + MOVE_WIN),
            out_specs=ANY,
            scratch_shapes=[
                pltpu.VMEM(kv_cache.shape, kv_cache.dtype),
                pltpu.VMEM(kv_cache.shape[1:], kv_cache.dtype),
                pltpu.SemaphoreType.DMA((slots,)),
                pltpu.SemaphoreType.DMA((slots,)),
            ],
        ),
        name="arrange_pages",
    )(page_after, move_in, kv_cache, *arrived, after)


def rows_kernel(place, q_ref, out_ref, *, ways, tok_rows):
    tok = out_ref.shape[1] // GROUP
    gp = GROUP // ways
    head = place[0]
    t_rel = pl.program_id(0) // 2
    t = place[1] ^ t_rel
    for p in range(KV_HEADS):
        kx = (p % (KV_HEADS // 2)) * 2 + p // (KV_HEADS // 2)
        at = pl.multiple_of(((kx ^ head) * ways + t) * tok_rows, tok_rows)
        for gx in range(GROUP):
            g = ((gx // gp) ^ t) * gp + gx % gp
            lanes = pl.ds(pl.multiple_of(g * HEAD_DIM, HEAD_DIM), HEAD_DIM)
            to = gx * tok + p * tok_rows
            out_ref[0, to : to + tok_rows, :] = q_ref[0, pl.ds(at, tok_rows), lanes]


def query_rows(queries, place, ways, tok_rows):
    width = GROUP * HEAD_DIM
    tok = KV_HEADS * tok_rows
    dtype = queries.dtype
    if tok_rows % 16:
        queries = lax.dynamic_slice_in_dim(queries, place[0] * width, width, axis=2)
        queries = queries.astype(jnp.float32)
        column = lambda i, place: (i % 2, 0, 0)
    else:
        column = lambda i, place: (i % 2, 0, place[0])
    return pl.pallas_call(
        functools.partial(rows_kernel, ways=ways, tok_rows=tok_rows),
        out_shape=jax.ShapeDtypeStruct((2 * ways, GROUP * tok, HEAD_DIM), queries.dtype),
        grid_spec=pltpu.PrefetchScalarGridSpec(
            num_scalar_prefetch=1,
            grid=(2 * ways,),
            in_specs=[pl.BlockSpec((1, queries.shape[1], width), column)],
            out_specs=pl.BlockSpec((1, GROUP * tok, HEAD_DIM), lambda i, place: (i, 0, 0)),
        ),
        name="query_rows",
    )(place, queries).astype(dtype)


def three_parts(x):
    high = x.astype(jnp.bfloat16)
    rest = x - high.astype(jnp.float32)
    mid = rest.astype(jnp.bfloat16)
    low = (rest - mid.astype(jnp.float32)).astype(jnp.bfloat16)
    return high, mid, low


def attend_kernel(
    pages, place, x_ref, q_ref, after_ref, *refs, first, last, rows, tok, ways, tok_rows, block
):
    n_in = 0 if first else 2
    carried = refs[:n_in]
    outs = refs[n_in : n_in + (1 if last else 2)]
    k_s, v_s, acc_s, m_s, order, counts = refs[n_in + len(outs) :]
    step = pl.program_id(0)
    src_slots = x_ref.shape[1]
    n_slots = x_ref.shape[0] * src_slots
    head, way = place[0], place[1]

    @pl.when(step == 0)
    def _():
        lowest = jnp.minimum(place[2], place[3])

        def fully(page):
            return (page >= 0) & (page * PAGE_TOK + (PAGE_TOK - 1) <= lowest)

        def put_full(i, count):
            yes = fully(pages[i])

            @pl.when(yes)
            def _():
                order[count] = i

            return count + yes.astype(jnp.int32)

        def put_rest(i, count):
            yes = (pages[i] >= 0) & jnp.logical_not(fully(pages[i]))

            @pl.when(yes)
            def _():
                order[count] = i

            return count + yes.astype(jnp.int32)

        n_full = lax.fori_loop(0, n_slots, put_full, 0)
        n_live = lax.fori_loop(0, n_slots, put_rest, n_full)
        counts[0] = n_full
        counts[1] = n_live

        row = lax.broadcasted_iota(jnp.int32, (2 * PAGE_TOK, 2 * PAGE_TOK), 0)
        col = lax.broadcasted_iota(jnp.int32, (2 * PAGE_TOK, 2 * PAGE_TOK), 1)
        want = jnp.where(row < PAGE_TOK, 2 * row, 2 * (row - PAGE_TOK) + 1)
        pick = jnp.where(col == want, 1.0, 0.0).astype(jnp.bfloat16)
        ones = jnp.ones((PAGE_TOK, HEAD_DIM), jnp.bfloat16)

        def split_step(i, carry):
            for s in range(NARROW):
                at = i * NARROW + s
                slot = order[jnp.minimum(at, n_live - 1)]
                both = jnp.dot(
                    pick,
                    x_ref[slot // src_slots, slot % src_slots],
                    preferred_element_type=jnp.float32,
                ).astype(jnp.bfloat16)
                to = pl.ds(pl.multiple_of(at * PAGE_TOK, PAGE_TOK), PAGE_TOK)
                k_s[to, :] = both[:PAGE_TOK]
                v_s[to, :HEAD_DIM] = both[PAGE_TOK:]
                v_s[to, HEAD_DIM:] = ones
            return carry

        lax.fori_loop(0, (n_live + NARROW - 1) // NARROW, split_step, 0)

    n_full, n_live = counts[0], counts[1]
    total = GROUP * tok
    if first:
        m_s[...] = jnp.full(m_s.shape, FLOOR, jnp.float32)
        acc_s[...] = jnp.zeros(acc_s.shape, jnp.float32)
    else:
        acc_s[...] = carried[0][0]
        m_s[...] = carried[1][0]

    if block is None:
        t_rel, b = step // 2, step % 2
    else:
        t_rel, b = step, block
    line = lax.broadcasted_iota(jnp.int32, (tok, PAGE_TOK), 0)
    p = line // tok_rows
    kx = (p % (KV_HEADS // 2)) * 2 + p // (KV_HEADS // 2)
    token = ((kx ^ head) * ways + (t_rel ^ way)) * tok_rows + line % tok_rows
    q_at = token + jnp.where(b == 0, place[2], place[3])

    def tile_step(at, size, masked):
        span_k = pl.ds(pl.multiple_of(at * PAGE_TOK, PAGE_TOK), size * PAGE_TOK)
        keys = k_s[span_k, :]
        values = v_s[span_k, :]
        if masked:
            lane = lax.broadcasted_iota(jnp.int32, (tok, PAGE_TOK), 1)
            visible = []
            for s in range(size):
                slot = order[jnp.minimum(at + s, n_live - 1)]
                start = jnp.where(at + s < n_live, pages[slot] * PAGE_TOK, FAR)
                seen = lane + start <= q_at
                visible.append(jnp.concatenate([seen] * (rows // tok), axis=0))

        def score(part):
            return lax.dot_general(
                q_ref[0, part * rows : (part + 1) * rows, :],
                keys,
                (((1,), (1,)), ((), ())),
                preferred_element_type=jnp.float32,
            )

        def soften(part, scores):
            span = slice(part * rows, (part + 1) * rows)
            pieces = [scores[:, s * PAGE_TOK : (s + 1) * PAGE_TOK] for s in range(size)]
            if masked:
                pieces = [jnp.where(v, x, FLOOR) for v, x in zip(visible, pieces)]
            peak = functools.reduce(jnp.maximum, pieces)
            m_old = m_s[span, :]
            m_new = jnp.maximum(m_old, jnp.max(peak, axis=1, keepdims=True) * SCALE)
            shift = jnp.maximum(m_new, 0.5 * FLOOR * SCALE) if masked else m_new
            weights = jnp.concatenate(
                [jnp.exp2(x * SCALE - shift).astype(jnp.bfloat16) for x in pieces], axis=1
            )
            m_s[span, :] = m_new
            return weights, jnp.exp2(m_old - m_new)

        def gather(part, weights, alpha):
            span = slice(part * rows, (part + 1) * rows)
            mixed = jnp.dot(weights, values, preferred_element_type=jnp.float32)
            acc_s[span, :HEAD_DIM] = acc_s[span, :HEAD_DIM] * alpha + mixed[:, :HEAD_DIM]
            acc_s[span, HEAD_DIM:] = acc_s[span, HEAD_DIM:] * alpha + mixed[:, HEAD_DIM:]

        parts = total // rows
        scores = score(0)
        waiting = None
        for part in range(parts):
            following = score(part + 1) if part + 1 < parts else None
            weights, alpha = soften(part, scores)
            if waiting is not None:
                gather(*waiting)
            waiting = (part, weights, alpha)
            scores = following
        gather(*waiting)

    n_wide = n_full // WIDE
    n_open = (n_full - n_wide * WIDE) // NARROW
    base = n_wide * WIDE
    done = base + n_open * NARROW
    n_masked = (n_live - done + NARROW - 1) // NARROW

    def wide(i, carry):
        tile_step(i * WIDE, WIDE, False)
        return carry

    def narrow(i, carry):
        tile_step(base + i * NARROW, NARROW, False)
        return carry

    def masked(i, carry):
        tile_step(done + i * NARROW, NARROW, True)
        return carry

    lax.fori_loop(0, n_wide, wide, 0)
    lax.fori_loop(0, n_open, narrow, 0)
    lax.fori_loop(0, n_masked, masked, 0)

    if not last:
        outs[0][0] = acc_s[...]
        outs[1][0] = m_s[...]
    else:
        out_ref = outs[0]
        out_ref[0, :total, :] = acc_s[:, :HEAD_DIM].astype(jnp.bfloat16)
        row = lax.broadcasted_iota(jnp.int32, (tok, HEAD_DIM), 0)
        col = lax.broadcasted_iota(jnp.int32, (tok, HEAD_DIM), 1)
        eye = row == col
        lines = []
        for ref, lanes in ((m_s, slice(0, HEAD_DIM)), (acc_s, slice(HEAD_DIM, 2 * HEAD_DIM))):
            for g in range(GROUP):
                span = slice(g * tok, (g + 1) * tok)
                lines.append(
                    jnp.sum(jnp.where(eye, ref[span, lanes], 0.0), axis=0, keepdims=True)
                )
        stats = jnp.concatenate(lines, axis=0)
        for i, piece in enumerate(three_parts(stats)):
            at = total + i * 2 * GROUP
            out_ref[0, at : at + 2 * GROUP, :] = piece


def attend(pages, place, x, q, after, carried, block, tok_rows, rows):
    sources, src_slots = x.shape[:2]
    steps, total, _ = q.shape
    tok = total // GROUP
    first = carried is None
    last = block is not None
    ways = steps // 2
    n_slots = -(-sources * src_slots // WIDE) * WIDE
    if last:
        grid = ways
        at = lambda i, *_: (2 * i + block, 0, 0)
    else:
        grid = steps
        at = lambda i, *_: (i, 0, 0)
    straight = lambda i, *_: (i, 0, 0)
    in_specs = [
        pl.BlockSpec(x.shape, lambda i, *_: (0, 0, 0, 0)),
        pl.BlockSpec((1, total, HEAD_DIM), at),
        ANY,
    ]
    sent = total + 3 * 2 * GROUP
    if last:
        out_shape = (jax.ShapeDtypeStruct((ways, sent, HEAD_DIM), jnp.bfloat16),)
        out_specs = (pl.BlockSpec((1, sent, HEAD_DIM), straight),)
    else:
        out_shape = (
            jax.ShapeDtypeStruct((steps, total, 2 * HEAD_DIM), jnp.float32),
            jax.ShapeDtypeStruct((steps, total, HEAD_DIM), jnp.float32),
        )
        out_specs = (
            pl.BlockSpec((1, total, 2 * HEAD_DIM), at),
            pl.BlockSpec((1, total, HEAD_DIM), at),
        )
    extra = ()
    if not first:
        extra = tuple(carried)
        in_specs += [
            pl.BlockSpec((1, total, 2 * HEAD_DIM), at),
            pl.BlockSpec((1, total, HEAD_DIM), at),
        ]
    flops = 8 * grid * total * sources * src_slots * PAGE_TOK * HEAD_DIM
    return pl.pallas_call(
        functools.partial(
            attend_kernel,
            first=first,
            last=last,
            rows=rows,
            tok=tok,
            ways=ways,
            tok_rows=tok_rows,
            block=block,
        ),
        out_shape=out_shape,
        grid_spec=pltpu.PrefetchScalarGridSpec(
            num_scalar_prefetch=2,
            grid=(grid,),
            in_specs=in_specs,
            out_specs=out_specs,
            scratch_shapes=[
                pltpu.VMEM((n_slots * PAGE_TOK, HEAD_DIM), jnp.bfloat16),
                pltpu.VMEM((n_slots * PAGE_TOK, 2 * HEAD_DIM), jnp.bfloat16),
                pltpu.VMEM((total, 2 * HEAD_DIM), jnp.float32),
                pltpu.VMEM((total, HEAD_DIM), jnp.float32),
                pltpu.SMEM((n_slots,), jnp.int32),
                pltpu.SMEM((2,), jnp.int32),
            ],
        ),
        cost_estimate=pl.CostEstimate(
            flops=flops, transcendentals=flops // (8 * HEAD_DIM), bytes_accessed=x.size * 2
        ),
        name="attend_last" if last else "attend_first",
    )(pages, place, x, q, after, *extra)


def merge(parts, a_ref, tok):
    total = GROUP * tok
    row = lax.broadcasted_iota(jnp.int32, (tok, HEAD_DIM), 0)
    col = lax.broadcasted_iota(jnp.int32, (tok, HEAD_DIM), 1)
    eye = row == col
    stats = []
    for part in parts:
        pieces = [
            part[total + i * 2 * GROUP : total + (i + 1) * 2 * GROUP, :].astype(jnp.float32)
            for i in range(3)
        ]
        stats.append((pieces[0] + pieces[1]) + pieces[2])
    tops = functools.reduce(jnp.maximum, [s[:GROUP] for s in stats])
    factors = [jnp.exp2(s[:GROUP] - tops) for s in stats]
    totals = sum(f * s[GROUP:] for f, s in zip(factors, stats))
    for g in range(GROUP):
        span = slice(g * tok, (g + 1) * tok)
        mixed = 0.0
        for f, part in zip(factors, parts):
            ratio = jnp.where(eye, f[g : g + 1] / totals[g : g + 1], 0.0)
            mixed += jnp.sum(ratio, axis=1, keepdims=True) * part[span, :].astype(jnp.float32)
        a_ref[:, g * HEAD_DIM : (g + 1) * HEAD_DIM] = mixed.astype(jnp.bfloat16)


def project_kernel(*refs, n_parts, n_ws, tok):
    parts = refs[:n_parts]
    ws = refs[n_parts : n_parts + n_ws]
    outs = refs[n_parts + n_ws :]
    keep_ref, send_ref = outs[:2]
    if n_parts == n_ws:
        a_ref = outs[2]

        @pl.when(pl.program_id(0) == 0)
        def _():
            merge(parts, a_ref, tok)

    else:
        a_ref = parts[0]
    depth = a_ref.shape[1] // n_ws
    total = 0.0
    for s in range(n_ws):
        total += jnp.dot(
            a_ref[:, s * depth : (s + 1) * depth], ws[s][...], preferred_element_type=jnp.float32
        )
    half = tok // 2
    keep_ref[...] = total[:half]
    send_ref[...] = total[half:].astype(jnp.bfloat16)


def project(parts, ws, tok, column_part, width=1024):
    columns = ws[0].shape[1] // COLUMN_PARTS
    steps = columns // width
    fixed = lambda i: (0, 0)
    half = tok // 2
    depth = sum(w.shape[0] for w in ws)
    merging = len(parts) == len(ws)
    out_shape = [
        jax.ShapeDtypeStruct((half, columns), jnp.float32),
        jax.ShapeDtypeStruct((half, columns), jnp.bfloat16),
    ]
    out_specs = [
        pl.BlockSpec((half, width), lambda i: (0, i)),
        pl.BlockSpec((half, width), lambda i: (0, i)),
    ]
    if merging:
        out_shape.append(jax.ShapeDtypeStruct((tok, depth), jnp.bfloat16))
        out_specs.append(pl.BlockSpec((tok, depth), fixed))
    return pl.pallas_call(
        functools.partial(project_kernel, n_parts=len(parts), n_ws=len(ws), tok=tok),
        out_shape=out_shape,
        grid=(steps,),
        in_specs=[pl.BlockSpec(o.shape, fixed) for o in parts]
        + [
            pl.BlockSpec((w.shape[0], width), lambda i: (0, column_part * steps + i)) for w in ws
        ],
        out_specs=out_specs,
        cost_estimate=pl.CostEstimate(
            flops=2 * tok * depth * columns, transcendentals=0, bytes_accessed=2 * depth * columns
        ),
        name="project",
    )(*parts, *ws)


def local(
    queries, kv_cache, w_out, slot_page_before, slot_page_after, move_out, move_in, positions
):
    n = lax.axis_size("pages")
    slots = kv_cache.shape[0]
    ways = n // KV_HEADS
    tok_rows = BLOCK // n
    tok = BLOCK // ways
    me = lax.axis_index("pages")
    way = me // KV_HEADS
    head = head_of(me % KV_HEADS)
    groups = [[a * KV_HEADS + b for b in range(KV_HEADS)] for a in range(ways)]

    def exchange(x):
        return lax.all_to_all(x, "pages", 0, 0, axis_index_groups=groups, tiled=True)

    cuts = [(0, FIRST_SLOTS), (FIRST_SLOTS, slots - FIRST_SLOTS)]
    arrived = []
    for at, count in cuts:
        piece = split_heads(kv_cache, at, count)
        got = exchange(piece)
        arrived.append(got.reshape(KV_HEADS, count, 2 * PAGE_TOK, HEAD_DIM))
    table = exchange(jnp.broadcast_to(slot_page_before[None, None], (KV_HEADS, 1, slots)))
    table = table.reshape(KV_HEADS, slots)
    pages = [table[:, at : at + count].reshape(-1) for at, count in cuts]
    place = jnp.stack([head, way, positions[0, 0], positions[1, 0]]).astype(jnp.int32)
    q = query_rows(queries, place, ways, tok_rows)

    leaving = outgoing_pages(kv_cache, move_out[0], arrived[0])
    landed = []
    for o in range(1, MOVE_WIN + 1):
        landed.append(permute_to(leaving[o - 1], n, lambda i: (i + o) % n))

    ws = [w_out]
    for s in range(1, ways):
        ws.append(permute_to(w_out, n, lambda i: i ^ s))

    rows = 2 * tok
    carried = attend(pages[0], place, arrived[0], q, leaving[0], None, None, tok_rows, rows)

    def merger(i, s):
        return head_of(i % KV_HEADS) * ways + ((i // KV_HEADS) ^ s)

    partial = []
    for b in range(2):
        (out,) = attend(
            pages[1], place, arrived[1], q, leaving[0], carried, b, tok_rows, rows
        )
        parts = []
        for s in range(ways):
            parts.append(permute_to(out[s], n, lambda i: merger(i, s)))
        partial.append(parts)

    sums = []
    for b in range(2):
        merged = partial[b]
        for c in range(COLUMN_PARTS):
            keep, send, *a = project(merged, ws, tok, c)
            if a:
                merged = a
            got = permute_to(send, n, lambda i: i ^ ways)
            sums.append((keep, got))
    cache_after = arrange_pages(kv_cache, landed, slot_page_after, move_in[0], send)

    results = []
    for keep, got in sums:
        total = (keep + got.astype(jnp.float32)).reshape(KV_HEADS // 2, tok_rows, -1)
        mine_rows = total[0]
        for zx in range(1, KV_HEADS // 2):
            got = permute_to(
                total[zx].astype(jnp.bfloat16), n, lambda i: i ^ (zx * 2 * ways)
            )
            mine_rows = mine_rows + got.astype(jnp.float32)
        results.append(mine_rows.astype(jnp.bfloat16))
    out = jnp.stack(
        [
            jnp.concatenate(results[b * COLUMN_PARTS : (b + 1) * COLUMN_PARTS], axis=1)
            for b in range(2)
        ]
    )
    return (out, cache_after)


def solution(mesh):
    in_specs = (
        P(None, "groups", None),
        P(("groups", "pages"), None, None, None),
        P("pages", None),
        P(("groups", "pages")),
        P(("groups", "pages")),
        P(("groups", "pages"), None),
        P(("groups", "pages"), None),
        P(None, "groups"),
    )
    out_specs = (P(None, ("groups", "pages"), None), P(("groups", "pages"), None, None, None))
    return jax.shard_map(local, mesh=mesh, in_specs=in_specs, out_specs=out_specs, check_vma=False)
```

```python
import functools

import jax
import jax.numpy as jnp
from jax import lax
from jax.experimental import pallas as pl
from jax.experimental.pallas import tpu as pltpu
from jax.sharding import PartitionSpec as P

HEADS = 64
KV_HEADS = 8
HEAD_DIM = 128
PAGE_TOK = 128
BLOCK = 256
MOVE_WIN = 4
GROUP = HEADS // KV_HEADS

FLOOR = -1e30
FAR = 1 << 30
SCALE = HEAD_DIM**-0.5 * 1.4426950408889634

WIDE = 16
NARROW = 8
FIRST_SLOTS = 5
COLUMN_PARTS = 2

ANY = pl.BlockSpec(memory_space=pl.ANY)


def permute_to(x, n, target):
    return lax.ppermute(x, "pages", [(i, target(i)) for i in range(n)])


def head_of(j):
    half = KV_HEADS // 2
    return (j % 2) * half + j // 2


def place_of(p):
    return (p % 2) * 4 + (p // 2 % 2) * 2 + p // 4


def split_heads_kernel(kv_ref, ids_ref, out_ref, buf, in_sems, out_sems, *, first, count):
    extra = ids_ref.shape[0]
    loads = []
    for d in range(KV_HEADS):
        lanes = pl.ds(head_of(d) * HEAD_DIM, HEAD_DIM)
        row = [
            pltpu.make_async_copy(
                kv_ref.at[first + i, :, :, lanes],
                buf.at[d, pl.ds(i * PAGE_TOK, PAGE_TOK)],
                in_sems.at[d, i],
            )
            for i in range(count)
        ]
        row.append(
            pltpu.make_async_copy(
                ids_ref, buf.at[d, pl.ds(count * PAGE_TOK, extra)], in_sems.at[d, count]
            )
        )
        loads.append(row)
    stores = [
        pltpu.make_async_copy(buf.at[d], out_ref.at[d], out_sems.at[d])
        for d in range(KV_HEADS)
    ]
    for row in loads:
        for load in row:
            load.start()
    for row, store in zip(loads, stores):
        for load in row:
            load.wait()
        store.start()
    for store in stores:
        store.wait()


def split_heads(kv_cache, ids, first, count):
    shape = (KV_HEADS, count * PAGE_TOK + ids.shape[0], 2, HEAD_DIM)
    return pl.pallas_call(
        functools.partial(split_heads_kernel, first=first, count=count),
        out_shape=jax.ShapeDtypeStruct(shape, kv_cache.dtype),
        in_specs=[ANY, ANY],
        out_specs=ANY,
        scratch_shapes=[
            pltpu.VMEM(shape, kv_cache.dtype),
            pltpu.SemaphoreType.DMA((KV_HEADS, count + 1)),
            pltpu.SemaphoreType.DMA((KV_HEADS,)),
        ],
        name="split_heads",
    )(kv_cache, ids)


def outgoing_kernel(move_out, kv_ref, *refs):
    outs = refs[:MOVE_WIN]
    buf, in_sems, out_sems = refs[MOVE_WIN:]
    loads = [
        pltpu.make_async_copy(
            kv_ref.at[jnp.maximum(move_out[o], 0)], buf.at[o], in_sems.at[o]
        )
        for o in range(MOVE_WIN)
    ]
    stores = [
        pltpu.make_async_copy(buf.at[o], outs[o], out_sems.at[o]) for o in range(MOVE_WIN)
    ]
    for load in loads:
        load.start()
    for load, store in zip(loads, stores):
        load.wait()
        store.start()
    for store in stores:
        store.wait()


def outgoing_pages(kv_cache, move_out):
    page = jax.ShapeDtypeStruct(kv_cache.shape[1:], kv_cache.dtype)
    return pl.pallas_call(
        outgoing_kernel,
        out_shape=(page,) * MOVE_WIN,
        grid_spec=pltpu.PrefetchScalarGridSpec(
            num_scalar_prefetch=1,
            grid=(),
            in_specs=[ANY],
            out_specs=(ANY,) * MOVE_WIN,
            scratch_shapes=[
                pltpu.VMEM((MOVE_WIN,) + kv_cache.shape[1:], kv_cache.dtype),
                pltpu.SemaphoreType.DMA((MOVE_WIN,)),
                pltpu.SemaphoreType.DMA((MOVE_WIN,)),
            ],
        ),
        name="outgoing_pages",
    )(move_out, kv_cache)


def arrange_kernel(page_after, move_in, kv_ref, *refs):
    arrived = refs[:MOVE_WIN]
    _, out_ref, buf, zero_ref, in_sems, out_sems = refs[MOVE_WIN:]
    slots = out_ref.shape[0]
    filled = []
    for s in range(slots):
        taken = jnp.zeros((), jnp.bool_)
        for o in reversed(range(MOVE_WIN)):
            lands = move_in[o] == s

            @pl.when(lands & jnp.logical_not(taken))
            def _():
                pltpu.make_async_copy(arrived[o], buf.at[s], in_sems.at[s]).start()

            taken = taken | lands
        kept = page_after[s] >= 0

        @pl.when(kept & jnp.logical_not(taken))
        def _():
            pltpu.make_async_copy(kv_ref.at[s], buf.at[s], in_sems.at[s]).start()

        filled.append(kept | taken)
    zero_ref[...] = jnp.zeros(zero_ref.shape, zero_ref.dtype)
    for s in range(slots):

        @pl.when(filled[s])
        def _():
            pltpu.make_async_copy(kv_ref.at[s], buf.at[s], in_sems.at[s]).wait()
            pltpu.make_async_copy(buf.at[s], out_ref.at[s], out_sems.at[s]).start()

        @pl.when(jnp.logical_not(filled[s]))
        def _():
            pltpu.make_async_copy(zero_ref, out_ref.at[s], out_sems.at[s]).start()

    for s in range(slots):
        pltpu.make_async_copy(zero_ref, out_ref.at[s], out_sems.at[s]).wait()


def arrange_pages(kv_cache, arrived, page_after, move_in, after):
    slots = kv_cache.shape[0]
    return pl.pallas_call(
        arrange_kernel,
        out_shape=jax.ShapeDtypeStruct(kv_cache.shape, kv_cache.dtype),
        grid_spec=pltpu.PrefetchScalarGridSpec(
            num_scalar_prefetch=2,
            grid=(),
            in_specs=[ANY] * (2 + MOVE_WIN),
            out_specs=ANY,
            scratch_shapes=[
                pltpu.VMEM(kv_cache.shape, kv_cache.dtype),
                pltpu.VMEM(kv_cache.shape[1:], kv_cache.dtype),
                pltpu.SemaphoreType.DMA((slots,)),
                pltpu.SemaphoreType.DMA((slots,)),
            ],
        ),
        name="arrange_pages",
    )(page_after, move_in, kv_cache, *arrived, after)


def rows_kernel(place, q_ref, out_ref, *, ways, tok_rows):
    tok = out_ref.shape[1] // GROUP
    gp = GROUP // ways
    head = place[0]
    t_rel = pl.program_id(0) // 2
    t = place[1] ^ t_rel
    for p in range(KV_HEADS):
        kx = place_of(p)
        at = pl.multiple_of(((kx ^ head) * ways + t) * tok_rows, tok_rows)
        for gx in range(GROUP):
            g = ((gx // gp) ^ t) * gp + gx % gp
            lanes = pl.ds(pl.multiple_of(g * HEAD_DIM, HEAD_DIM), HEAD_DIM)
            to = gx * tok + p * tok_rows
            out_ref[0, to : to + tok_rows, :] = q_ref[0, pl.ds(at, tok_rows), lanes]


def query_rows(queries, place, ways, tok_rows):
    width = GROUP * HEAD_DIM
    tok = KV_HEADS * tok_rows
    dtype = queries.dtype
    if tok_rows % 16:
        queries = lax.dynamic_slice_in_dim(queries, place[0] * width, width, axis=2)
        queries = queries.astype(jnp.float32)
        column = lambda i, place: (i % 2, 0, 0)
    else:
        column = lambda i, place: (i % 2, 0, place[0])
    return pl.pallas_call(
        functools.partial(rows_kernel, ways=ways, tok_rows=tok_rows),
        out_shape=jax.ShapeDtypeStruct((2 * ways, GROUP * tok, HEAD_DIM), queries.dtype),
        grid_spec=pltpu.PrefetchScalarGridSpec(
            num_scalar_prefetch=1,
            grid=(2 * ways,),
            in_specs=[pl.BlockSpec((1, queries.shape[1], width), column)],
            out_specs=pl.BlockSpec((1, GROUP * tok, HEAD_DIM), lambda i, place: (i, 0, 0)),
        ),
        name="query_rows",
    )(place, queries).astype(dtype)


def three_parts(x):
    high = x.astype(jnp.bfloat16)
    rest = x - high.astype(jnp.float32)
    mid = rest.astype(jnp.bfloat16)
    low = (rest - mid.astype(jnp.float32)).astype(jnp.bfloat16)
    return high, mid, low


def attend_kernel(
    place, x_ref, q_ref, *refs, first_slot, first, last, rows, tok, ways, tok_rows, block
):
    n_in = 0 if first else 2
    carried = refs[:n_in]
    outs = refs[n_in : n_in + (ways if last else 2)]
    k_s, v_s, acc_s, m_s, ids_s, order, pages, ids, counts, sem = refs[n_in + len(outs) :]
    step = pl.program_id(0)
    sources = x_ref.shape[0]
    src_slots = x_ref.shape[1] // (2 * PAGE_TOK)
    n_slots = sources * src_slots
    head, way = place[0], place[1]

    @pl.when(step == 0)
    def _():
        end = src_slots * 2 * PAGE_TOK
        extra = x_ref.shape[1] - end
        row = lax.broadcasted_iota(jnp.int32, (extra, HEAD_DIM), 0)
        col = lax.broadcasted_iota(jnp.int32, (extra, HEAD_DIM), 1)
        for src in range(sources):
            tail = x_ref[src, end : end + extra, :].astype(jnp.float32)
            line = jnp.sum(jnp.where(row == 2 * col, tail, 0.0), axis=0, keepdims=True)
            ids_s[src : src + 1, :] = line.astype(jnp.int32)
        copy = pltpu.make_async_copy(ids_s, ids, sem)
        copy.start()
        copy.wait()
        lowest = jnp.minimum(place[2], place[3])

        def fully(page):
            return (page >= 0) & (page * PAGE_TOK + (PAGE_TOK - 1) <= lowest)

        def put_full(i, count):
            page = ids[i // src_slots, first_slot + i % src_slots]
            pages[i] = page
            yes = fully(page)

            @pl.when(yes)
            def _():
                order[count] = i

            return count + yes.astype(jnp.int32)

        def put_rest(i, count):
            yes = (pages[i] >= 0) & jnp.logical_not(fully(pages[i]))

            @pl.when(yes)
            def _():
                order[count] = i

            return count + yes.astype(jnp.int32)

        n_full = lax.fori_loop(0, n_slots, put_full, 0)
        n_live = lax.fori_loop(0, n_slots, put_rest, n_full)
        counts[0] = n_full
        counts[1] = n_live

        row = lax.broadcasted_iota(jnp.int32, (2 * PAGE_TOK, 2 * PAGE_TOK), 0)
        col = lax.broadcasted_iota(jnp.int32, (2 * PAGE_TOK, 2 * PAGE_TOK), 1)
        want = jnp.where(row < PAGE_TOK, 2 * row, 2 * (row - PAGE_TOK) + 1)
        pick = jnp.where(col == want, 1.0, 0.0).astype(jnp.bfloat16)
        ones = jnp.ones((PAGE_TOK, HEAD_DIM), jnp.bfloat16)

        def split_step(i, carry):
            for s in range(NARROW):
                at = i * NARROW + s
                slot = order[jnp.minimum(at, n_live - 1)]
                both = jnp.dot(
                    pick,
                    x_ref[
                        slot // src_slots,
                        pl.ds(
                            pl.multiple_of(slot % src_slots * 2 * PAGE_TOK, 2 * PAGE_TOK),
                            2 * PAGE_TOK,
                        ),
                        :,
                    ],
                    preferred_element_type=jnp.float32,
                ).astype(jnp.bfloat16)
                to = pl.ds(pl.multiple_of(at * PAGE_TOK, PAGE_TOK), PAGE_TOK)
                k_s[to, :] = both[:PAGE_TOK]
                v_s[to, :HEAD_DIM] = both[PAGE_TOK:]
                v_s[to, HEAD_DIM:] = ones
            return carry

        lax.fori_loop(0, (n_live + NARROW - 1) // NARROW, split_step, 0)

    n_full, n_live = counts[0], counts[1]
    total = GROUP * tok
    if first:
        m_s[...] = jnp.full(m_s.shape, FLOOR, jnp.float32)
        acc_s[...] = jnp.zeros(acc_s.shape, jnp.float32)
    else:
        acc_s[...] = carried[0][0]
        m_s[...] = carried[1][0]

    if block is None:
        t_rel, b = step // 2, step % 2
    else:
        t_rel, b = step, block
    line = lax.broadcasted_iota(jnp.int32, (tok, PAGE_TOK), 0)
    p = line // tok_rows
    kx = place_of(p)
    token = ((kx ^ head) * ways + (t_rel ^ way)) * tok_rows + line % tok_rows
    q_at = token + jnp.where(b == 0, place[2], place[3])

    def tile_step(at, size, masked):
        span_k = pl.ds(pl.multiple_of(at * PAGE_TOK, PAGE_TOK), size * PAGE_TOK)
        keys = k_s[span_k, :]
        values = v_s[span_k, :]
        if masked:
            lane = lax.broadcasted_iota(jnp.int32, (tok, PAGE_TOK), 1)
            visible = []
            for s in range(size):
                slot = order[jnp.minimum(at + s, n_live - 1)]
                start = jnp.where(at + s < n_live, pages[slot] * PAGE_TOK, FAR)
                seen = lane + start <= q_at
                visible.append(jnp.concatenate([seen] * (rows // tok), axis=0))

        def score(part):
            return lax.dot_general(
                q_ref[0, part * rows : (part + 1) * rows, :],
                keys,
                (((1,), (1,)), ((), ())),
                preferred_element_type=jnp.float32,
            )

        def soften(part, scores):
            span = slice(part * rows, (part + 1) * rows)
            pieces = [scores[:, s * PAGE_TOK : (s + 1) * PAGE_TOK] for s in range(size)]
            if masked:
                pieces = [jnp.where(v, x, FLOOR) for v, x in zip(visible, pieces)]
            peak = functools.reduce(jnp.maximum, pieces)
            m_old = m_s[span, :]
            m_new = jnp.maximum(m_old, jnp.max(peak, axis=1, keepdims=True) * SCALE)
            shift = jnp.maximum(m_new, 0.5 * FLOOR * SCALE) if masked else m_new
            weights = jnp.concatenate(
                [jnp.exp2(x * SCALE - shift).astype(jnp.bfloat16) for x in pieces], axis=1
            )
            m_s[span, :] = m_new
            return weights, jnp.exp2(m_old - m_new)

        def gather(part, weights, alpha):
            span = slice(part * rows, (part + 1) * rows)
            mixed = jnp.dot(weights, values, preferred_element_type=jnp.float32)
            acc_s[span, :HEAD_DIM] = acc_s[span, :HEAD_DIM] * alpha + mixed[:, :HEAD_DIM]
            acc_s[span, HEAD_DIM:] = acc_s[span, HEAD_DIM:] * alpha + mixed[:, HEAD_DIM:]

        parts = total // rows
        scores = score(0)
        waiting = None
        for part in range(parts):
            following = score(part + 1) if part + 1 < parts else None
            weights, alpha = soften(part, scores)
            if waiting is not None:
                gather(*waiting)
            waiting = (part, weights, alpha)
            scores = following
        gather(*waiting)

    n_wide = n_full // WIDE
    n_open = (n_full - n_wide * WIDE) // NARROW
    base = n_wide * WIDE
    done = base + n_open * NARROW
    n_masked = (n_live - done + NARROW - 1) // NARROW

    def wide(i, carry):
        tile_step(i * WIDE, WIDE, False)
        return carry

    def narrow(i, carry):
        tile_step(base + i * NARROW, NARROW, False)
        return carry

    def masked(i, carry):
        tile_step(done + i * NARROW, NARROW, True)
        return carry

    lax.fori_loop(0, n_wide, wide, 0)
    lax.fori_loop(0, n_open, narrow, 0)
    lax.fori_loop(0, n_masked, masked, 0)

    if not last:
        outs[0][0] = acc_s[...]
        outs[1][0] = m_s[...]
    else:
        row = lax.broadcasted_iota(jnp.int32, (tok, HEAD_DIM), 0)
        col = lax.broadcasted_iota(jnp.int32, (tok, HEAD_DIM), 1)
        eye = row == col
        lines = []
        for ref, lanes in ((m_s, slice(0, HEAD_DIM)), (acc_s, slice(HEAD_DIM, 2 * HEAD_DIM))):
            for g in range(GROUP):
                span = slice(g * tok, (g + 1) * tok)
                lines.append(
                    jnp.sum(jnp.where(eye, ref[span, lanes], 0.0), axis=0, keepdims=True)
                )
        stats = jnp.concatenate(lines, axis=0)
        for w in range(ways):

            @pl.when(step == w)
            def _():
                outs[w][:total, :] = acc_s[:, :HEAD_DIM].astype(jnp.bfloat16)
                for i, piece in enumerate(three_parts(stats)):
                    at = total + i * 2 * GROUP
                    outs[w][at : at + 2 * GROUP, :] = piece


def attend(place, x, first_slot, q, carried, block, tok_rows, rows):
    sources = x.shape[0]
    src_slots = x.shape[1] // (2 * PAGE_TOK)
    steps, total, _ = q.shape
    tok = total // GROUP
    first = carried is None
    last = block is not None
    ways = steps // 2
    n_slots = -(-sources * src_slots // WIDE) * WIDE
    if last:
        grid = ways
        at = lambda i, *_: (2 * i + block, 0, 0)
    else:
        grid = steps
        at = lambda i, *_: (i, 0, 0)
    in_specs = [
        pl.BlockSpec(x.shape, lambda i, *_: (0, 0, 0)),
        pl.BlockSpec((1, total, HEAD_DIM), at),
    ]
    sent = total + 3 * 2 * GROUP
    if last:
        out_shape = (jax.ShapeDtypeStruct((sent, HEAD_DIM), jnp.bfloat16),) * ways
        out_specs = (pl.BlockSpec((sent, HEAD_DIM), lambda i, *_: (0, 0)),) * ways
    else:
        out_shape = (
            jax.ShapeDtypeStruct((steps, total, 2 * HEAD_DIM), jnp.float32),
            jax.ShapeDtypeStruct((steps, total, HEAD_DIM), jnp.float32),
        )
        out_specs = (
            pl.BlockSpec((1, total, 2 * HEAD_DIM), at),
            pl.BlockSpec((1, total, HEAD_DIM), at),
        )
    extra = ()
    if not first:
        extra = tuple(carried)
        in_specs += [
            pl.BlockSpec((1, total, 2 * HEAD_DIM), at),
            pl.BlockSpec((1, total, HEAD_DIM), at),
        ]
    flops = 8 * grid * total * sources * src_slots * PAGE_TOK * HEAD_DIM
    return pl.pallas_call(
        functools.partial(
            attend_kernel,
            first_slot=first_slot,
            first=first,
            last=last,
            rows=rows,
            tok=tok,
            ways=ways,
            tok_rows=tok_rows,
            block=block,
        ),
        out_shape=out_shape,
        grid_spec=pltpu.PrefetchScalarGridSpec(
            num_scalar_prefetch=1,
            grid=(grid,),
            in_specs=in_specs,
            out_specs=out_specs,
            scratch_shapes=[
                pltpu.VMEM((n_slots * PAGE_TOK, HEAD_DIM), jnp.bfloat16),
                pltpu.VMEM((n_slots * PAGE_TOK, 2 * HEAD_DIM), jnp.bfloat16),
                pltpu.VMEM((total, 2 * HEAD_DIM), jnp.float32),
                pltpu.VMEM((total, HEAD_DIM), jnp.float32),
                pltpu.VMEM((sources, HEAD_DIM), jnp.int32),
                pltpu.SMEM((n_slots,), jnp.int32),
                pltpu.SMEM((n_slots,), jnp.int32),
                pltpu.SMEM((sources, HEAD_DIM), jnp.int32),
                pltpu.SMEM((2,), jnp.int32),
                pltpu.SemaphoreType.DMA(()),
            ],
        ),
        cost_estimate=pl.CostEstimate(
            flops=flops, transcendentals=flops // (8 * HEAD_DIM), bytes_accessed=x.size * 2
        ),
        name="attend_last" if last else "attend_first",
    )(place, x, q, *extra)


def merge(parts, a_ref, tok):
    total = GROUP * tok
    row = lax.broadcasted_iota(jnp.int32, (tok, HEAD_DIM), 0)
    col = lax.broadcasted_iota(jnp.int32, (tok, HEAD_DIM), 1)
    eye = row == col
    stats = []
    for part in parts:
        pieces = [
            part[total + i * 2 * GROUP : total + (i + 1) * 2 * GROUP, :].astype(jnp.float32)
            for i in range(3)
        ]
        stats.append((pieces[0] + pieces[1]) + pieces[2])
    tops = functools.reduce(jnp.maximum, [s[:GROUP] for s in stats])
    factors = [jnp.exp2(s[:GROUP] - tops) for s in stats]
    totals = sum(f * s[GROUP:] for f, s in zip(factors, stats))
    for g in range(GROUP):
        span = slice(g * tok, (g + 1) * tok)
        mixed = 0.0
        for f, part in zip(factors, parts):
            ratio = jnp.where(eye, f[g : g + 1] / totals[g : g + 1], 0.0)
            mixed += jnp.sum(ratio, axis=1, keepdims=True) * part[span, :].astype(jnp.float32)
        a_ref[:, g * HEAD_DIM : (g + 1) * HEAD_DIM] = mixed.astype(jnp.bfloat16)


def project_kernel(*refs, n_parts, n_ws, tok, y_first):
    parts = refs[:n_parts]
    ws = refs[n_parts : n_parts + n_ws]
    outs = refs[n_parts + n_ws :]
    keep_ref, send_ref = outs[:2]
    if n_parts == n_ws:
        a_ref = outs[2]

        @pl.when(pl.program_id(0) == 0)
        def _():
            merge(parts, a_ref, tok)

    else:
        a_ref = parts[0]
    depth = a_ref.shape[1] // n_ws
    total = 0.0
    for s in range(n_ws):
        total += jnp.dot(
            a_ref[:, s * depth : (s + 1) * depth], ws[s][...], preferred_element_type=jnp.float32
        )
    if y_first:
        keep, send = total[: tok // 2], total[tok // 2 :]
    else:
        quarters = [total[i * tok // 4 : (i + 1) * tok // 4] for i in range(4)]
        keep = jnp.concatenate(quarters[0::2], axis=0)
        send = jnp.concatenate(quarters[1::2], axis=0)
    keep_ref[...] = keep
    send_ref[...] = send.astype(jnp.bfloat16)


def project(parts, ws, tok, column_part, y_first, width=1024):
    columns = ws[0].shape[1] // COLUMN_PARTS
    steps = columns // width
    fixed = lambda i: (0, 0)
    half = tok // 2
    depth = sum(w.shape[0] for w in ws)
    merging = len(parts) == len(ws)
    out_shape = [
        jax.ShapeDtypeStruct((half, columns), jnp.float32),
        jax.ShapeDtypeStruct((half, columns), jnp.bfloat16),
    ]
    out_specs = [
        pl.BlockSpec((half, width), lambda i: (0, i)),
        pl.BlockSpec((half, width), lambda i: (0, i)),
    ]
    if merging:
        out_shape.append(jax.ShapeDtypeStruct((tok, depth), jnp.bfloat16))
        out_specs.append(pl.BlockSpec((tok, depth), fixed))
    return pl.pallas_call(
        functools.partial(
            project_kernel, n_parts=len(parts), n_ws=len(ws), tok=tok, y_first=y_first
        ),
        out_shape=out_shape,
        grid=(steps,),
        in_specs=[pl.BlockSpec(o.shape, fixed) for o in parts]
        + [
            pl.BlockSpec((w.shape[0], width), lambda i: (0, column_part * steps + i)) for w in ws
        ],
        out_specs=out_specs,
        cost_estimate=pl.CostEstimate(
            flops=2 * tok * depth * columns, transcendentals=0, bytes_accessed=2 * depth * columns
        ),
        name="project",
    )(*parts, *ws)


def local(
    queries, kv_cache, w_out, slot_page_before, slot_page_after, move_out, move_in, positions
):
    n = lax.axis_size("pages")
    slots = kv_cache.shape[0]
    ways = n // KV_HEADS
    tok_rows = BLOCK // n
    tok = BLOCK // ways
    me = lax.axis_index("pages")
    way = me // KV_HEADS
    head = head_of(me % KV_HEADS)
    groups = [[a * KV_HEADS + b for b in range(KV_HEADS)] for a in range(ways)]

    def exchange(x):
        return lax.all_to_all(x, "pages", 0, 0, axis_index_groups=groups, tiled=True)

    ids = jnp.broadcast_to(slot_page_before[:, None, None], (slots, 2, HEAD_DIM))
    ids = ids.astype(kv_cache.dtype)
    cuts = [(0, FIRST_SLOTS), (FIRST_SLOTS, slots - FIRST_SLOTS)]
    arrived = []
    for at, count in cuts:
        piece = split_heads(kv_cache, ids, at, count)
        got = exchange(piece)
        arrived.append(got.reshape(KV_HEADS, -1, HEAD_DIM))
    place = jnp.stack([head, way, positions[0, 0], positions[1, 0]]).astype(jnp.int32)
    q = query_rows(queries, place, ways, tok_rows)

    leaving = outgoing_pages(kv_cache, move_out[0])
    landed = []
    for o in range(1, MOVE_WIN + 1):
        landed.append(permute_to(leaving[o - 1], n, lambda i: (i + o) % n))

    ws = [w_out]
    for s in range(1, ways):
        ws.append(permute_to(w_out, n, lambda i: i ^ s))

    rows = 2 * tok
    carried = attend(place, arrived[0], 0, q, None, None, tok_rows, rows)

    def merger(i, s):
        return head_of(i % KV_HEADS) * ways + ((i // KV_HEADS) ^ s)

    partial = []
    for b in range(2):
        out = attend(place, arrived[1], FIRST_SLOTS, q, carried, b, tok_rows, rows)
        parts = []
        for s in range(ways):
            parts.append(permute_to(out[s], n, lambda i: merger(i, s)))
        partial.append(parts)

    sums = []
    for b in range(2):
        merged = partial[b]
        for c in range(COLUMN_PARTS):
            y_first = (b, c) != (0, 1)
            keep, send, *a = project(merged, ws, tok, c, y_first)
            if a:
                merged = a
            turns = (1, 2, 4) if y_first else (2, 1, 4)
            got = permute_to(send, n, lambda i: i ^ (turns[0] * ways))
            sums.append((keep, got, turns))
    cache_after = arrange_pages(kv_cache, landed, slot_page_after, move_in[0], send)

    results = []
    for keep, got, turns in sums:
        for turn in turns[1:]:
            total = keep + got.astype(jnp.float32)
            half = total.shape[0] // 2
            keep = total[:half]
            got = permute_to(
                total[half:].astype(jnp.bfloat16), n, lambda i: i ^ (turn * ways)
            )
        results.append((keep + got.astype(jnp.float32)).astype(jnp.bfloat16))
    out = jnp.stack(
        [
            jnp.concatenate(results[b * COLUMN_PARTS : (b + 1) * COLUMN_PARTS], axis=1)
            for b in range(2)
        ]
    )
    return (out, cache_after)


def solution(mesh):
    in_specs = (
        P(None, "groups", None),
        P(("groups", "pages"), None, None, None),
        P("pages", None),
        P(("groups", "pages")),
        P(("groups", "pages")),
        P(("groups", "pages"), None),
        P(("groups", "pages"), None),
        P(None, "groups"),
    )
    out_specs = (P(None, ("groups", "pages"), None), P(("groups", "pages"), None, None, None))
    return jax.shard_map(local, mesh=mesh, in_specs=in_specs, out_specs=out_specs, check_vma=False)
```

```python
import functools

import jax
import jax.numpy as jnp
from jax import lax
from jax.experimental import pallas as pl
from jax.experimental.pallas import tpu as pltpu
from jax.sharding import PartitionSpec as P

HEADS = 64
KV_HEADS = 8
HEAD_DIM = 128
PAGE_TOK = 128
BLOCK = 256
MOVE_WIN = 4
GROUP = HEADS // KV_HEADS

FLOOR = -1e30
FAR = 1 << 30
SCALE = HEAD_DIM**-0.5 * 1.4426950408889634

WIDE = 16
NARROW = 8
FIRST_SLOTS = 3
COLUMN_PARTS = 2

ANY = pl.BlockSpec(memory_space=pl.ANY)


def permute_to(x, n, target):
    return lax.ppermute(x, "pages", [(i, target(i)) for i in range(n)])


def head_of(j):
    half = KV_HEADS // 2
    return (j % 2) * half + j // 2


def place_of(p):
    return (p % 2) * 4 + (p // 2 % 2) * 2 + p // 4


def split_heads_kernel(kv_ref, ids_ref, out_ref, buf, in_sems, out_sems, *, first, count):
    extra = ids_ref.shape[0]
    loads = []
    for d in range(KV_HEADS):
        lanes = pl.ds(head_of(d) * HEAD_DIM, HEAD_DIM)
        row = [
            pltpu.make_async_copy(
                kv_ref.at[first + i, :, :, lanes],
                buf.at[d, pl.ds(i * PAGE_TOK, PAGE_TOK)],
                in_sems.at[d, i],
            )
            for i in range(count)
        ]
        row.append(
            pltpu.make_async_copy(
                ids_ref, buf.at[d, pl.ds(count * PAGE_TOK, extra)], in_sems.at[d, count]
            )
        )
        loads.append(row)
    stores = [
        pltpu.make_async_copy(buf.at[d], out_ref.at[d], out_sems.at[d])
        for d in range(KV_HEADS)
    ]
    for row in loads:
        for load in row:
            load.start()
    for row, store in zip(loads, stores):
        for load in row:
            load.wait()
        store.start()
    for store in stores:
        store.wait()


def split_heads(kv_cache, ids, first, count):
    shape = (KV_HEADS, count * PAGE_TOK + ids.shape[0], 2, HEAD_DIM)
    return pl.pallas_call(
        functools.partial(split_heads_kernel, first=first, count=count),
        out_shape=jax.ShapeDtypeStruct(shape, kv_cache.dtype),
        in_specs=[ANY, ANY],
        out_specs=ANY,
        scratch_shapes=[
            pltpu.VMEM(shape, kv_cache.dtype),
            pltpu.SemaphoreType.DMA((KV_HEADS, count + 1)),
            pltpu.SemaphoreType.DMA((KV_HEADS,)),
        ],
        name="split_heads",
    )(kv_cache, ids)


def outgoing_kernel(move_out, kv_ref, *refs):
    outs = refs[:MOVE_WIN]
    buf, in_sems, out_sems = refs[MOVE_WIN:]
    loads = [
        pltpu.make_async_copy(
            kv_ref.at[jnp.maximum(move_out[o], 0)], buf.at[o], in_sems.at[o]
        )
        for o in range(MOVE_WIN)
    ]
    stores = [
        pltpu.make_async_copy(buf.at[o], outs[o], out_sems.at[o]) for o in range(MOVE_WIN)
    ]
    for load in loads:
        load.start()
    for load, store in zip(loads, stores):
        load.wait()
        store.start()
    for store in stores:
        store.wait()


def outgoing_pages(kv_cache, move_out):
    page = jax.ShapeDtypeStruct(kv_cache.shape[1:], kv_cache.dtype)
    return pl.pallas_call(
        outgoing_kernel,
        out_shape=(page,) * MOVE_WIN,
        grid_spec=pltpu.PrefetchScalarGridSpec(
            num_scalar_prefetch=1,
            grid=(),
            in_specs=[ANY],
            out_specs=(ANY,) * MOVE_WIN,
            scratch_shapes=[
                pltpu.VMEM((MOVE_WIN,) + kv_cache.shape[1:], kv_cache.dtype),
                pltpu.SemaphoreType.DMA((MOVE_WIN,)),
                pltpu.SemaphoreType.DMA((MOVE_WIN,)),
            ],
        ),
        name="outgoing_pages",
    )(move_out, kv_cache)


def arrange_kernel(page_after, move_in, kv_ref, *refs):
    arrived = refs[:MOVE_WIN]
    _, out_ref, buf, zero_ref, in_sems, out_sems = refs[MOVE_WIN:]
    slots = out_ref.shape[0]
    filled = []
    for s in range(slots):
        taken = jnp.zeros((), jnp.bool_)
        for o in reversed(range(MOVE_WIN)):
            lands = move_in[o] == s

            @pl.when(lands & jnp.logical_not(taken))
            def _():
                pltpu.make_async_copy(arrived[o], buf.at[s], in_sems.at[s]).start()

            taken = taken | lands
        kept = page_after[s] >= 0

        @pl.when(kept & jnp.logical_not(taken))
        def _():
            pltpu.make_async_copy(kv_ref.at[s], buf.at[s], in_sems.at[s]).start()

        filled.append(kept | taken)
    zero_ref[...] = jnp.zeros(zero_ref.shape, zero_ref.dtype)
    for s in range(slots):

        @pl.when(filled[s])
        def _():
            pltpu.make_async_copy(kv_ref.at[s], buf.at[s], in_sems.at[s]).wait()
            pltpu.make_async_copy(buf.at[s], out_ref.at[s], out_sems.at[s]).start()

        @pl.when(jnp.logical_not(filled[s]))
        def _():
            pltpu.make_async_copy(zero_ref, out_ref.at[s], out_sems.at[s]).start()

    for s in range(slots):
        pltpu.make_async_copy(zero_ref, out_ref.at[s], out_sems.at[s]).wait()


def arrange_pages(kv_cache, arrived, page_after, move_in, after):
    slots = kv_cache.shape[0]
    return pl.pallas_call(
        arrange_kernel,
        out_shape=jax.ShapeDtypeStruct(kv_cache.shape, kv_cache.dtype),
        grid_spec=pltpu.PrefetchScalarGridSpec(
            num_scalar_prefetch=2,
            grid=(),
            in_specs=[ANY] * (2 + MOVE_WIN),
            out_specs=ANY,
            scratch_shapes=[
                pltpu.VMEM(kv_cache.shape, kv_cache.dtype),
                pltpu.VMEM(kv_cache.shape[1:], kv_cache.dtype),
                pltpu.SemaphoreType.DMA((slots,)),
                pltpu.SemaphoreType.DMA((slots,)),
            ],
        ),
        name="arrange_pages",
    )(page_after, move_in, kv_cache, *arrived, after)


def rows_kernel(place, q_ref, out_ref, *, ways, tok_rows):
    tok = out_ref.shape[1] // GROUP
    gp = GROUP // ways
    head = place[0]
    t_rel = pl.program_id(0) // 2
    t = place[1] ^ t_rel
    for p in range(KV_HEADS):
        kx = place_of(p)
        at = pl.multiple_of(((kx ^ head) * ways + t) * tok_rows, tok_rows)
        for gx in range(GROUP):
            g = ((gx // gp) ^ t) * gp + gx % gp
            lanes = pl.ds(pl.multiple_of(g * HEAD_DIM, HEAD_DIM), HEAD_DIM)
            to = gx * tok + p * tok_rows
            out_ref[0, to : to + tok_rows, :] = q_ref[0, pl.ds(at, tok_rows), lanes]


def query_rows(queries, place, ways, tok_rows):
    width = GROUP * HEAD_DIM
    tok = KV_HEADS * tok_rows
    dtype = queries.dtype
    if tok_rows % 16:
        queries = lax.dynamic_slice_in_dim(queries, place[0] * width, width, axis=2)
        queries = queries.astype(jnp.float32)
        column = lambda i, place: (i % 2, 0, 0)
    else:
        column = lambda i, place: (i % 2, 0, place[0])
    return pl.pallas_call(
        functools.partial(rows_kernel, ways=ways, tok_rows=tok_rows),
        out_shape=jax.ShapeDtypeStruct((2 * ways, GROUP * tok, HEAD_DIM), queries.dtype),
        grid_spec=pltpu.PrefetchScalarGridSpec(
            num_scalar_prefetch=1,
            grid=(2 * ways,),
            in_specs=[pl.BlockSpec((1, queries.shape[1], width), column)],
            out_specs=pl.BlockSpec((1, GROUP * tok, HEAD_DIM), lambda i, place: (i, 0, 0)),
        ),
        name="query_rows",
    )(place, queries).astype(dtype)


def three_parts(x):
    high = x.astype(jnp.bfloat16)
    rest = x - high.astype(jnp.float32)
    mid = rest.astype(jnp.bfloat16)
    low = (rest - mid.astype(jnp.float32)).astype(jnp.bfloat16)
    return high, mid, low


def attend_kernel(
    place, x_ref, q_ref, *refs, first_slot, first, last, rows, tok, ways, tok_rows, block
):
    n_in = 0 if first else 2
    carried = refs[:n_in]
    outs = refs[n_in : n_in + (ways if last else 2)]
    k_s, v_s, *sums, ids_s, order, rest, pages, ids, counts, sem = refs[n_in + len(outs) :]
    if last:
        acc_s, m_s = sums
    else:
        acc_s, m_s = outs[0].at[0], outs[1].at[0]
    step = pl.program_id(0)
    sources = x_ref.shape[0]
    src_slots = x_ref.shape[1] // (2 * PAGE_TOK)
    n_slots = sources * src_slots
    head, way = place[0], place[1]

    @pl.when(step == 0)
    def _():
        end = src_slots * 2 * PAGE_TOK
        extra = x_ref.shape[1] - end
        row = lax.broadcasted_iota(jnp.int32, (extra, HEAD_DIM), 0)
        col = lax.broadcasted_iota(jnp.int32, (extra, HEAD_DIM), 1)
        for src in range(sources):
            tail = x_ref[src, end : end + extra, :].astype(jnp.float32)
            line = jnp.sum(jnp.where(row == 2 * col, tail, 0.0), axis=0, keepdims=True)
            ids_s[src : src + 1, :] = line.astype(jnp.int32)
        copy = pltpu.make_async_copy(ids_s, ids, sem)
        copy.start()
        copy.wait()
        lowest = jnp.minimum(place[2], place[3])

        def fully(page):
            return (page >= 0) & (page * PAGE_TOK + (PAGE_TOK - 1) <= lowest)

        n_full = jnp.int32(0)
        n_rest = jnp.int32(0)
        for i in range(n_slots):
            page = ids[i // src_slots, first_slot + i % src_slots]
            pages[i] = page
            yes = fully(page)
            order[n_full] = i
            rest[n_rest] = i
            n_full += yes.astype(jnp.int32)
            n_rest += ((page >= 0) & jnp.logical_not(yes)).astype(jnp.int32)

        def append(i, carry):
            order[n_full + i] = rest[i]
            return carry

        lax.fori_loop(0, n_rest, append, 0)
        n_live = n_full + n_rest
        counts[0] = n_full
        counts[1] = n_live

        row = lax.broadcasted_iota(jnp.int32, (2 * PAGE_TOK, 2 * PAGE_TOK), 0)
        col = lax.broadcasted_iota(jnp.int32, (2 * PAGE_TOK, 2 * PAGE_TOK), 1)
        want = jnp.where(row < PAGE_TOK, 2 * row, 2 * (row - PAGE_TOK) + 1)
        pick = jnp.where(col == want, 1.0, 0.0).astype(jnp.bfloat16)
        ones = jnp.ones((PAGE_TOK, HEAD_DIM), jnp.bfloat16)

        def split_step(i, carry):
            for s in range(NARROW):
                at = i * NARROW + s
                slot = order[jnp.minimum(at, n_live - 1)]
                both = jnp.dot(
                    pick,
                    x_ref[
                        slot // src_slots,
                        pl.ds(
                            pl.multiple_of(slot % src_slots * 2 * PAGE_TOK, 2 * PAGE_TOK),
                            2 * PAGE_TOK,
                        ),
                        :,
                    ],
                    preferred_element_type=jnp.float32,
                ).astype(jnp.bfloat16)
                to = pl.ds(pl.multiple_of(at * PAGE_TOK, PAGE_TOK), PAGE_TOK)
                k_s[to, :] = both[:PAGE_TOK]
                v_s[to, :HEAD_DIM] = both[PAGE_TOK:]
                v_s[to, HEAD_DIM:] = ones
            return carry

        lax.fori_loop(0, (n_live + NARROW - 1) // NARROW, split_step, 0)

    n_full, n_live = counts[0], counts[1]
    total = GROUP * tok
    if first:
        m_s[...] = jnp.full(m_s.shape, FLOOR, jnp.float32)
        acc_s[...] = jnp.zeros(acc_s.shape, jnp.float32)
    else:
        acc_s[...] = carried[0][0]
        m_s[...] = carried[1][0]

    if block is None:
        t_rel, b = step // 2, step % 2
    else:
        t_rel, b = step, block
    line = lax.broadcasted_iota(jnp.int32, (tok, PAGE_TOK), 0)
    p = line // tok_rows
    kx = place_of(p)
    token = ((kx ^ head) * ways + (t_rel ^ way)) * tok_rows + line % tok_rows
    q_at = token + jnp.where(b == 0, place[2], place[3])

    def tile_step(at, size, masked):
        span_k = pl.ds(pl.multiple_of(at * PAGE_TOK, PAGE_TOK), size * PAGE_TOK)
        keys = k_s[span_k, :]
        values = v_s[span_k, :]
        if masked:
            lane = lax.broadcasted_iota(jnp.int32, (tok, PAGE_TOK), 1)
            visible = []
            for s in range(size):
                slot = order[jnp.minimum(at + s, n_live - 1)]
                start = jnp.where(at + s < n_live, pages[slot] * PAGE_TOK, FAR)
                seen = lane + start <= q_at
                visible.append(jnp.concatenate([seen] * (rows // tok), axis=0))

        def score(part):
            return lax.dot_general(
                q_ref[0, part * rows : (part + 1) * rows, :],
                keys,
                (((1,), (1,)), ((), ())),
                preferred_element_type=jnp.float32,
            )

        def soften(part, scores):
            span = slice(part * rows, (part + 1) * rows)
            pieces = [scores[:, s * PAGE_TOK : (s + 1) * PAGE_TOK] for s in range(size)]
            if masked:
                pieces = [jnp.where(v, x, FLOOR) for v, x in zip(visible, pieces)]
            peak = functools.reduce(jnp.maximum, pieces)
            m_old = m_s[span, :]
            m_new = jnp.maximum(m_old, jnp.max(peak, axis=1, keepdims=True) * SCALE)
            shift = jnp.maximum(m_new, 0.5 * FLOOR * SCALE) if masked else m_new
            weights = jnp.concatenate(
                [jnp.exp2(x * SCALE - shift).astype(jnp.bfloat16) for x in pieces], axis=1
            )
            m_s[span, :] = m_new
            return weights, jnp.exp2(m_old - m_new)

        def gather(part, weights, alpha):
            span = slice(part * rows, (part + 1) * rows)
            mixed = jnp.dot(weights, values, preferred_element_type=jnp.float32)
            acc_s[span, :HEAD_DIM] = acc_s[span, :HEAD_DIM] * alpha + mixed[:, :HEAD_DIM]
            acc_s[span, HEAD_DIM:] = acc_s[span, HEAD_DIM:] * alpha + mixed[:, HEAD_DIM:]

        parts = total // rows
        scores = score(0)
        waiting = None
        for part in range(parts):
            following = score(part + 1) if part + 1 < parts else None
            weights, alpha = soften(part, scores)
            if waiting is not None:
                gather(*waiting)
            waiting = (part, weights, alpha)
            scores = following
        gather(*waiting)

    n_wide = n_full // WIDE
    n_open = (n_full - n_wide * WIDE) // NARROW
    base = n_wide * WIDE
    done = base + n_open * NARROW
    n_masked = (n_live - done + NARROW - 1) // NARROW

    def wide(i, carry):
        tile_step(i * WIDE, WIDE, False)
        return carry

    def narrow(i, carry):
        tile_step(base + i * NARROW, NARROW, False)
        return carry

    def masked(i, carry):
        tile_step(done + i * NARROW, NARROW, True)
        return carry

    lax.fori_loop(0, n_wide, wide, 0)
    lax.fori_loop(0, n_open, narrow, 0)
    lax.fori_loop(0, n_masked, masked, 0)

    if last:
        row = lax.broadcasted_iota(jnp.int32, (tok, HEAD_DIM), 0)
        col = lax.broadcasted_iota(jnp.int32, (tok, HEAD_DIM), 1)
        eye = row == col
        lines = []
        for ref, lanes in ((m_s, slice(0, HEAD_DIM)), (acc_s, slice(HEAD_DIM, 2 * HEAD_DIM))):
            for g in range(GROUP):
                span = slice(g * tok, (g + 1) * tok)
                lines.append(
                    jnp.sum(jnp.where(eye, ref[span, lanes], 0.0), axis=0, keepdims=True)
                )
        stats = jnp.concatenate(lines, axis=0)
        for w in range(ways):

            @pl.when(step == w)
            def _():
                outs[w][:total, :] = acc_s[:, :HEAD_DIM].astype(jnp.bfloat16)
                for i, piece in enumerate(three_parts(stats)):
                    at = total + i * 2 * GROUP
                    outs[w][at : at + 2 * GROUP, :] = piece


def attend(place, x, first_slot, q, carried, block, tok_rows, rows):
    sources = x.shape[0]
    src_slots = x.shape[1] // (2 * PAGE_TOK)
    steps, total, _ = q.shape
    tok = total // GROUP
    first = carried is None
    last = block is not None
    ways = steps // 2
    n_slots = -(-sources * src_slots // WIDE) * WIDE
    if last:
        grid = ways
        at = lambda i, *_: (2 * i + block, 0, 0)
    else:
        grid = steps
        at = lambda i, *_: (i, 0, 0)
    in_specs = [
        pl.BlockSpec(x.shape, lambda i, *_: (0, 0, 0)),
        pl.BlockSpec((1, total, HEAD_DIM), at),
    ]
    sent = total + 3 * 2 * GROUP
    if last:
        out_shape = (jax.ShapeDtypeStruct((sent, HEAD_DIM), jnp.bfloat16),) * ways
        out_specs = (pl.BlockSpec((sent, HEAD_DIM), lambda i, *_: (0, 0)),) * ways
    else:
        out_shape = (
            jax.ShapeDtypeStruct((steps, total, 2 * HEAD_DIM), jnp.float32),
            jax.ShapeDtypeStruct((steps, total, HEAD_DIM), jnp.float32),
        )
        out_specs = (
            pl.BlockSpec((1, total, 2 * HEAD_DIM), at),
            pl.BlockSpec((1, total, HEAD_DIM), at),
        )
    extra = ()
    sums = ()
    if last:
        sums = (
            pltpu.VMEM((total, 2 * HEAD_DIM), jnp.float32),
            pltpu.VMEM((total, HEAD_DIM), jnp.float32),
        )
    if not first:
        extra = tuple(carried)
        in_specs += [
            pl.BlockSpec((1, total, 2 * HEAD_DIM), at),
            pl.BlockSpec((1, total, HEAD_DIM), at),
        ]
    flops = 8 * grid * total * sources * src_slots * PAGE_TOK * HEAD_DIM
    return pl.pallas_call(
        functools.partial(
            attend_kernel,
            first_slot=first_slot,
            first=first,
            last=last,
            rows=rows,
            tok=tok,
            ways=ways,
            tok_rows=tok_rows,
            block=block,
        ),
        out_shape=out_shape,
        grid_spec=pltpu.PrefetchScalarGridSpec(
            num_scalar_prefetch=1,
            grid=(grid,),
            in_specs=in_specs,
            out_specs=out_specs,
            scratch_shapes=[
                pltpu.VMEM((n_slots * PAGE_TOK, HEAD_DIM), jnp.bfloat16),
                pltpu.VMEM((n_slots * PAGE_TOK, 2 * HEAD_DIM), jnp.bfloat16),
                *sums,
                pltpu.VMEM((sources, HEAD_DIM), jnp.int32),
                pltpu.SMEM((n_slots + 1,), jnp.int32),
                pltpu.SMEM((n_slots + 1,), jnp.int32),
                pltpu.SMEM((n_slots,), jnp.int32),
                pltpu.SMEM((sources, HEAD_DIM), jnp.int32),
                pltpu.SMEM((2,), jnp.int32),
                pltpu.SemaphoreType.DMA(()),
            ],
        ),
        cost_estimate=pl.CostEstimate(
            flops=flops, transcendentals=flops // (8 * HEAD_DIM), bytes_accessed=x.size * 2
        ),
        name="attend_last" if last else "attend_first",
    )(place, x, q, *extra)


def merge(parts, a_ref, tok):
    total = GROUP * tok
    row = lax.broadcasted_iota(jnp.int32, (tok, HEAD_DIM), 0)
    col = lax.broadcasted_iota(jnp.int32, (tok, HEAD_DIM), 1)
    eye = row == col
    stats = []
    for part in parts:
        pieces = [
            part[total + i * 2 * GROUP : total + (i + 1) * 2 * GROUP, :].astype(jnp.float32)
            for i in range(3)
        ]
        stats.append((pieces[0] + pieces[1]) + pieces[2])
    tops = functools.reduce(jnp.maximum, [s[:GROUP] for s in stats])
    factors = [jnp.exp2(s[:GROUP] - tops) for s in stats]
    totals = sum(f * s[GROUP:] for f, s in zip(factors, stats))
    for g in range(GROUP):
        span = slice(g * tok, (g + 1) * tok)
        mixed = 0.0
        for f, part in zip(factors, parts):
            ratio = jnp.where(eye, f[g : g + 1] / totals[g : g + 1], 0.0)
            mixed += jnp.sum(ratio, axis=1, keepdims=True) * part[span, :].astype(jnp.float32)
        a_ref[:, g * HEAD_DIM : (g + 1) * HEAD_DIM] = mixed.astype(jnp.bfloat16)


def project_kernel(*refs, n_parts, n_ws, tok, y_first):
    parts = refs[:n_parts]
    ws = refs[n_parts : n_parts + n_ws]
    outs = refs[n_parts + n_ws :]
    keep_ref, send_ref = outs[:2]
    if n_parts == n_ws:
        a_ref = outs[2]

        @pl.when(pl.program_id(0) == 0)
        def _():
            merge(parts, a_ref, tok)

    else:
        a_ref = parts[0]
    depth = a_ref.shape[1] // n_ws
    total = 0.0
    for s in range(n_ws):
        total += jnp.dot(
            a_ref[:, s * depth : (s + 1) * depth], ws[s][...], preferred_element_type=jnp.float32
        )
    if y_first:
        keep, send = total[: tok // 2], total[tok // 2 :]
    else:
        quarters = [total[i * tok // 4 : (i + 1) * tok // 4] for i in range(4)]
        keep = jnp.concatenate(quarters[0::2], axis=0)
        send = jnp.concatenate(quarters[1::2], axis=0)
    keep_ref[...] = keep
    send_ref[...] = send.astype(jnp.bfloat16)


def project(parts, ws, tok, column_part, y_first, width=1024):
    columns = ws[0].shape[1] // COLUMN_PARTS
    steps = columns // width
    fixed = lambda i: (0, 0)
    half = tok // 2
    depth = sum(w.shape[0] for w in ws)
    merging = len(parts) == len(ws)
    out_shape = [
        jax.ShapeDtypeStruct((half, columns), jnp.float32),
        jax.ShapeDtypeStruct((half, columns), jnp.bfloat16),
    ]
    out_specs = [
        pl.BlockSpec((half, width), lambda i: (0, i)),
        pl.BlockSpec((half, width), lambda i: (0, i)),
    ]
    if merging:
        out_shape.append(jax.ShapeDtypeStruct((tok, depth), jnp.bfloat16))
        out_specs.append(pl.BlockSpec((tok, depth), fixed))
    return pl.pallas_call(
        functools.partial(
            project_kernel, n_parts=len(parts), n_ws=len(ws), tok=tok, y_first=y_first
        ),
        out_shape=out_shape,
        grid=(steps,),
        in_specs=[pl.BlockSpec(o.shape, fixed) for o in parts]
        + [
            pl.BlockSpec((w.shape[0], width), lambda i: (0, column_part * steps + i)) for w in ws
        ],
        out_specs=out_specs,
        cost_estimate=pl.CostEstimate(
            flops=2 * tok * depth * columns, transcendentals=0, bytes_accessed=2 * depth * columns
        ),
        name="project",
    )(*parts, *ws)


def local(
    queries, kv_cache, w_out, slot_page_before, slot_page_after, move_out, move_in, positions
):
    n = lax.axis_size("pages")
    slots = kv_cache.shape[0]
    ways = n // KV_HEADS
    tok_rows = BLOCK // n
    tok = BLOCK // ways
    me = lax.axis_index("pages")
    way = me // KV_HEADS
    head = head_of(me % KV_HEADS)
    groups = [[a * KV_HEADS + b for b in range(KV_HEADS)] for a in range(ways)]

    def exchange(x):
        return lax.all_to_all(x, "pages", 0, 0, axis_index_groups=groups, tiled=True)

    ids = jnp.broadcast_to(slot_page_before[:, None, None], (slots, 2, HEAD_DIM))
    ids = ids.astype(kv_cache.dtype)
    cuts = [(0, FIRST_SLOTS), (FIRST_SLOTS, slots - FIRST_SLOTS)]
    arrived = []
    for at, count in cuts:
        piece = split_heads(kv_cache, ids, at, count)
        got = exchange(piece)
        arrived.append(got.reshape(KV_HEADS, -1, HEAD_DIM))
    place = jnp.stack([head, way, positions[0, 0], positions[1, 0]]).astype(jnp.int32)
    q = query_rows(queries, place, ways, tok_rows)

    leaving = outgoing_pages(kv_cache, move_out[0])
    landed = []
    for o in range(1, MOVE_WIN + 1):
        landed.append(permute_to(leaving[o - 1], n, lambda i: (i + o) % n))

    ws = [w_out]
    for s in range(1, ways):
        ws.append(permute_to(w_out, n, lambda i: i ^ s))

    rows = 2 * tok
    carried = attend(place, arrived[0], 0, q, None, None, tok_rows, rows)

    def merger(i, s):
        return head_of(i % KV_HEADS) * ways + ((i // KV_HEADS) ^ s)

    partial = []
    for b in range(2):
        out = attend(place, arrived[1], FIRST_SLOTS, q, carried, b, tok_rows, rows)
        parts = []
        for s in range(ways):
            parts.append(permute_to(out[s], n, lambda i: merger(i, s)))
        partial.append(parts)

    sums = []
    for b in range(2):
        merged = partial[b]
        for c in range(COLUMN_PARTS):
            y_first = (b, c) != (1, 1)
            keep, send, *a = project(merged, ws, tok, c, y_first)
            if a:
                merged = a
            turns = (1, 2, 4) if y_first else (2, 1, 4)
            got = permute_to(send, n, lambda i: i ^ (turns[0] * ways))
            sums.append((keep, got, turns))
    cache_after = arrange_pages(kv_cache, landed, slot_page_after, move_in[0], send)

    results = []
    for keep, got, turns in sums:
        for turn in turns[1:]:
            total = keep + got.astype(jnp.float32)
            half = total.shape[0] // 2
            keep = total[:half]
            got = permute_to(
                total[half:].astype(jnp.bfloat16), n, lambda i: i ^ (turn * ways)
            )
        results.append((keep + got.astype(jnp.float32)).astype(jnp.bfloat16))
    out = jnp.stack(
        [
            jnp.concatenate(results[b * COLUMN_PARTS : (b + 1) * COLUMN_PARTS], axis=1)
            for b in range(2)
        ]
    )
    return (out, cache_after)


def solution(mesh):
    in_specs = (
        P(None, "groups", None),
        P(("groups", "pages"), None, None, None),
        P("pages", None),
        P(("groups", "pages")),
        P(("groups", "pages")),
        P(("groups", "pages"), None),
        P(("groups", "pages"), None),
        P(None, "groups"),
    )
    out_specs = (P(None, ("groups", "pages"), None), P(("groups", "pages"), None, None, None))
    return jax.shard_map(local, mesh=mesh, in_specs=in_specs, out_specs=out_specs, check_vma=False)
```

```python
import functools

import jax
import jax.numpy as jnp
from jax import lax
from jax.experimental import pallas as pl
from jax.experimental.pallas import tpu as pltpu
from jax.sharding import PartitionSpec as P

HEADS = 64
KV_HEADS = 8
HEAD_DIM = 128
PAGE_TOK = 128
BLOCK = 256
MOVE_WIN = 4
GROUP = HEADS // KV_HEADS

FLOOR = -1e30
FAR = 1 << 30
SCALE = HEAD_DIM**-0.5 * 1.4426950408889634

WIDE = 16
NARROW = 8
FIRST_SLOTS = 5
COLUMN_PARTS = 2

ANY = pl.BlockSpec(memory_space=pl.ANY)


def permute_to(x, n, target):
    return lax.ppermute(x, "pages", [(i, target(i)) for i in range(n)])


def head_of(j):
    half = KV_HEADS // 2
    return (j % 2) * half + j // 2


def place_of(p):
    return (p % 2) * 4 + (p // 2 % 2) * 2 + p // 4


def split_heads_kernel(kv_ref, ids_ref, out_ref, buf, in_sems, out_sems, *, first, count):
    extra = ids_ref.shape[0]
    loads = []
    for d in range(KV_HEADS):
        lanes = pl.ds(head_of(d) * HEAD_DIM, HEAD_DIM)
        row = [
            pltpu.make_async_copy(
                kv_ref.at[first + i, :, :, lanes],
                buf.at[d, pl.ds(i * PAGE_TOK, PAGE_TOK)],
                in_sems.at[d, i],
            )
            for i in range(count)
        ]
        row.append(
            pltpu.make_async_copy(
                ids_ref, buf.at[d, pl.ds(count * PAGE_TOK, extra)], in_sems.at[d, count]
            )
        )
        loads.append(row)
    stores = [
        pltpu.make_async_copy(buf.at[d], out_ref.at[d], out_sems.at[d])
        for d in range(KV_HEADS)
    ]
    for row in loads:
        for load in row:
            load.start()
    for row, store in zip(loads, stores):
        for load in row:
            load.wait()
        store.start()
    for store in stores:
        store.wait()


def split_heads(kv_cache, ids, first, count):
    shape = (KV_HEADS, count * PAGE_TOK + ids.shape[0], 2, HEAD_DIM)
    return pl.pallas_call(
        functools.partial(split_heads_kernel, first=first, count=count),
        out_shape=jax.ShapeDtypeStruct(shape, kv_cache.dtype),
        in_specs=[ANY, ANY],
        out_specs=ANY,
        scratch_shapes=[
            pltpu.VMEM(shape, kv_cache.dtype),
            pltpu.SemaphoreType.DMA((KV_HEADS, count + 1)),
            pltpu.SemaphoreType.DMA((KV_HEADS,)),
        ],
        name="split_heads",
    )(kv_cache, ids)


def outgoing_kernel(move_out, kv_ref, *refs):
    outs = refs[:MOVE_WIN]
    buf, in_sems, out_sems = refs[MOVE_WIN:]
    loads = [
        pltpu.make_async_copy(
            kv_ref.at[jnp.maximum(move_out[o], 0)], buf.at[o], in_sems.at[o]
        )
        for o in range(MOVE_WIN)
    ]
    stores = [
        pltpu.make_async_copy(buf.at[o], outs[o], out_sems.at[o]) for o in range(MOVE_WIN)
    ]
    for load in loads:
        load.start()
    for load, store in zip(loads, stores):
        load.wait()
        store.start()
    for store in stores:
        store.wait()


def outgoing_pages(kv_cache, move_out):
    page = jax.ShapeDtypeStruct(kv_cache.shape[1:], kv_cache.dtype)
    return pl.pallas_call(
        outgoing_kernel,
        out_shape=(page,) * MOVE_WIN,
        grid_spec=pltpu.PrefetchScalarGridSpec(
            num_scalar_prefetch=1,
            grid=(),
            in_specs=[ANY],
            out_specs=(ANY,) * MOVE_WIN,
            scratch_shapes=[
                pltpu.VMEM((MOVE_WIN,) + kv_cache.shape[1:], kv_cache.dtype),
                pltpu.SemaphoreType.DMA((MOVE_WIN,)),
                pltpu.SemaphoreType.DMA((MOVE_WIN,)),
            ],
        ),
        name="outgoing_pages",
    )(move_out, kv_cache)


def arrange_kernel(page_after, move_in, kv_ref, *refs):
    arrived = refs[:MOVE_WIN]
    _, out_ref, buf, zero_ref, in_sems, out_sems = refs[MOVE_WIN:]
    slots = out_ref.shape[0]
    filled = []
    for s in range(slots):
        taken = jnp.zeros((), jnp.bool_)
        for o in reversed(range(MOVE_WIN)):
            lands = move_in[o] == s

            @pl.when(lands & jnp.logical_not(taken))
            def _():
                pltpu.make_async_copy(arrived[o], buf.at[s], in_sems.at[s]).start()

            taken = taken | lands
        kept = page_after[s] >= 0

        @pl.when(kept & jnp.logical_not(taken))
        def _():
            pltpu.make_async_copy(kv_ref.at[s], buf.at[s], in_sems.at[s]).start()

        filled.append(kept | taken)
    zero_ref[...] = jnp.zeros(zero_ref.shape, zero_ref.dtype)
    for s in range(slots):

        @pl.when(filled[s])
        def _():
            pltpu.make_async_copy(kv_ref.at[s], buf.at[s], in_sems.at[s]).wait()
            pltpu.make_async_copy(buf.at[s], out_ref.at[s], out_sems.at[s]).start()

        @pl.when(jnp.logical_not(filled[s]))
        def _():
            pltpu.make_async_copy(zero_ref, out_ref.at[s], out_sems.at[s]).start()

    for s in range(slots):
        pltpu.make_async_copy(zero_ref, out_ref.at[s], out_sems.at[s]).wait()


def arrange_pages(kv_cache, arrived, page_after, move_in, after):
    slots = kv_cache.shape[0]
    return pl.pallas_call(
        arrange_kernel,
        out_shape=jax.ShapeDtypeStruct(kv_cache.shape, kv_cache.dtype),
        grid_spec=pltpu.PrefetchScalarGridSpec(
            num_scalar_prefetch=2,
            grid=(),
            in_specs=[ANY] * (2 + MOVE_WIN),
            out_specs=ANY,
            scratch_shapes=[
                pltpu.VMEM(kv_cache.shape, kv_cache.dtype),
                pltpu.VMEM(kv_cache.shape[1:], kv_cache.dtype),
                pltpu.SemaphoreType.DMA((slots,)),
                pltpu.SemaphoreType.DMA((slots,)),
            ],
        ),
        name="arrange_pages",
    )(page_after, move_in, kv_cache, *arrived, after)


def rows_kernel(place, q_ref, out_ref, *, ways, tok_rows):
    tok = out_ref.shape[1] // GROUP
    gp = GROUP // ways
    head = place[0]
    t_rel = pl.program_id(0) // 2
    t = place[1] ^ t_rel
    for p in range(KV_HEADS):
        kx = place_of(p)
        at = pl.multiple_of(((kx ^ head) * ways + t) * tok_rows, tok_rows)
        for gx in range(GROUP):
            g = ((gx // gp) ^ t) * gp + gx % gp
            lanes = pl.ds(pl.multiple_of(g * HEAD_DIM, HEAD_DIM), HEAD_DIM)
            to = gx * tok + p * tok_rows
            out_ref[0, to : to + tok_rows, :] = q_ref[0, pl.ds(at, tok_rows), lanes]


def query_rows(queries, place, ways, tok_rows):
    width = GROUP * HEAD_DIM
    tok = KV_HEADS * tok_rows
    dtype = queries.dtype
    if tok_rows % 16:
        queries = lax.dynamic_slice_in_dim(queries, place[0] * width, width, axis=2)
        queries = queries.astype(jnp.float32)
        column = lambda i, place: (i % 2, 0, 0)
    else:
        column = lambda i, place: (i % 2, 0, place[0])
    return pl.pallas_call(
        functools.partial(rows_kernel, ways=ways, tok_rows=tok_rows),
        out_shape=jax.ShapeDtypeStruct((2 * ways, GROUP * tok, HEAD_DIM), queries.dtype),
        grid_spec=pltpu.PrefetchScalarGridSpec(
            num_scalar_prefetch=1,
            grid=(2 * ways,),
            in_specs=[pl.BlockSpec((1, queries.shape[1], width), column)],
            out_specs=pl.BlockSpec((1, GROUP * tok, HEAD_DIM), lambda i, place: (i, 0, 0)),
        ),
        name="query_rows",
    )(place, queries).astype(dtype)


def three_parts(x):
    high = x.astype(jnp.bfloat16)
    rest = x - high.astype(jnp.float32)
    mid = rest.astype(jnp.bfloat16)
    low = (rest - mid.astype(jnp.float32)).astype(jnp.bfloat16)
    return high, mid, low


def attend_kernel(
    place, x_ref, q_ref, after_ref, *refs, first_slot, first, last, rows, tok, ways, tok_rows, block
):
    n_in = 0 if first else 2
    carried = refs[:n_in]
    outs = refs[n_in : n_in + (ways if last else 2)]
    k_s, v_s, *sums, ids_s, order, rest, pages, ids, counts, sem = refs[n_in + len(outs) :]
    if last:
        acc_s, m_s = sums
    else:
        acc_s, m_s = outs[0].at[0], outs[1].at[0]
    step = pl.program_id(0)
    sources = x_ref.shape[0]
    src_slots = x_ref.shape[1] // (2 * PAGE_TOK)
    n_slots = sources * src_slots
    head, way = place[0], place[1]

    @pl.when(step == 0)
    def _():
        end = src_slots * 2 * PAGE_TOK
        extra = x_ref.shape[1] - end
        row = lax.broadcasted_iota(jnp.int32, (extra, HEAD_DIM), 0)
        col = lax.broadcasted_iota(jnp.int32, (extra, HEAD_DIM), 1)
        for src in range(sources):
            tail = x_ref[src, end : end + extra, :].astype(jnp.float32)
            line = jnp.sum(jnp.where(row == 2 * col, tail, 0.0), axis=0, keepdims=True)
            ids_s[src : src + 1, :] = line.astype(jnp.int32)
        copy = pltpu.make_async_copy(ids_s, ids, sem)
        copy.start()
        copy.wait()
        lowest = jnp.minimum(place[2], place[3])

        def fully(page):
            return (page >= 0) & (page * PAGE_TOK + (PAGE_TOK - 1) <= lowest)

        n_full = jnp.int32(0)
        n_rest = jnp.int32(0)
        for i in range(n_slots):
            page = ids[i // src_slots, first_slot + i % src_slots]
            pages[i] = page
            yes = fully(page)
            order[n_full] = i
            rest[n_rest] = i
            n_full += yes.astype(jnp.int32)
            n_rest += ((page >= 0) & jnp.logical_not(yes)).astype(jnp.int32)

        def append(i, carry):
            order[n_full + i] = rest[i]
            return carry

        lax.fori_loop(0, n_rest, append, 0)
        n_live = n_full + n_rest
        counts[0] = n_full
        counts[1] = n_live

        row = lax.broadcasted_iota(jnp.int32, (2 * PAGE_TOK, 2 * PAGE_TOK), 0)
        col = lax.broadcasted_iota(jnp.int32, (2 * PAGE_TOK, 2 * PAGE_TOK), 1)
        want = jnp.where(row < PAGE_TOK, 2 * row, 2 * (row - PAGE_TOK) + 1)
        pick = jnp.where(col == want, 1.0, 0.0).astype(jnp.bfloat16)
        ones = jnp.ones((PAGE_TOK, HEAD_DIM), jnp.bfloat16)

        def split_step(i, carry):
            for s in range(NARROW):
                at = i * NARROW + s
                slot = order[jnp.minimum(at, n_live - 1)]
                both = jnp.dot(
                    pick,
                    x_ref[
                        slot // src_slots,
                        pl.ds(
                            pl.multiple_of(slot % src_slots * 2 * PAGE_TOK, 2 * PAGE_TOK),
                            2 * PAGE_TOK,
                        ),
                        :,
                    ],
                    preferred_element_type=jnp.float32,
                ).astype(jnp.bfloat16)
                to = pl.ds(pl.multiple_of(at * PAGE_TOK, PAGE_TOK), PAGE_TOK)
                k_s[to, :] = both[:PAGE_TOK]
                v_s[to, :HEAD_DIM] = both[PAGE_TOK:]
                v_s[to, HEAD_DIM:] = ones
            return carry

        lax.fori_loop(0, (n_live + NARROW - 1) // NARROW, split_step, 0)

    n_full, n_live = counts[0], counts[1]
    total = GROUP * tok
    if first:
        m_s[...] = jnp.full(m_s.shape, FLOOR, jnp.float32)
        acc_s[...] = jnp.zeros(acc_s.shape, jnp.float32)
    else:
        acc_s[...] = carried[0][0]
        m_s[...] = carried[1][0]

    line = lax.broadcasted_iota(jnp.int32, (tok, PAGE_TOK), 0)
    p = line // tok_rows
    kx = place_of(p)
    token = ((kx ^ head) * ways + (step ^ way)) * tok_rows + line % tok_rows
    q_at = token + place[2 + block]

    def tile_step(at, size, masked):
        span_k = pl.ds(pl.multiple_of(at * PAGE_TOK, PAGE_TOK), size * PAGE_TOK)
        keys = k_s[span_k, :]
        values = v_s[span_k, :]
        if masked:
            lane = lax.broadcasted_iota(jnp.int32, (tok, PAGE_TOK), 1)
            visible = []
            for s in range(size):
                slot = order[jnp.minimum(at + s, n_live - 1)]
                start = jnp.where(at + s < n_live, pages[slot] * PAGE_TOK, FAR)
                seen = lane + start <= q_at
                visible.append(jnp.concatenate([seen] * (rows // tok), axis=0))

        def score(part):
            return lax.dot_general(
                q_ref[0, part * rows : (part + 1) * rows, :],
                keys,
                (((1,), (1,)), ((), ())),
                preferred_element_type=jnp.float32,
            )

        def soften(part, scores):
            span = slice(part * rows, (part + 1) * rows)
            pieces = [scores[:, s * PAGE_TOK : (s + 1) * PAGE_TOK] for s in range(size)]
            if masked:
                pieces = [jnp.where(v, x, FLOOR) for v, x in zip(visible, pieces)]
            peak = functools.reduce(jnp.maximum, pieces)
            m_old = m_s[span, :]
            m_new = jnp.maximum(m_old, jnp.max(peak, axis=1, keepdims=True) * SCALE)
            shift = jnp.maximum(m_new, 0.5 * FLOOR * SCALE) if masked else m_new
            weights = jnp.concatenate(
                [jnp.exp2(x * SCALE - shift).astype(jnp.bfloat16) for x in pieces], axis=1
            )
            m_s[span, :] = m_new
            return weights, jnp.exp2(m_old - m_new)

        def gather(part, weights, alpha):
            span = slice(part * rows, (part + 1) * rows)
            mixed = jnp.dot(weights, values, preferred_element_type=jnp.float32)
            acc_s[span, :HEAD_DIM] = acc_s[span, :HEAD_DIM] * alpha + mixed[:, :HEAD_DIM]
            acc_s[span, HEAD_DIM:] = acc_s[span, HEAD_DIM:] * alpha + mixed[:, HEAD_DIM:]

        parts = total // rows
        scores = score(0)
        waiting = None
        for part in range(parts):
            following = score(part + 1) if part + 1 < parts else None
            weights, alpha = soften(part, scores)
            if waiting is not None:
                gather(*waiting)
            waiting = (part, weights, alpha)
            scores = following
        gather(*waiting)

    n_wide = n_full // WIDE
    n_open = (n_full - n_wide * WIDE) // NARROW
    base = n_wide * WIDE
    done = base + n_open * NARROW
    n_masked = (n_live - done + NARROW - 1) // NARROW

    def wide(i, carry):
        tile_step(i * WIDE, WIDE, False)
        return carry

    def narrow(i, carry):
        tile_step(base + i * NARROW, NARROW, False)
        return carry

    def masked(i, carry):
        tile_step(done + i * NARROW, NARROW, True)
        return carry

    lax.fori_loop(0, n_wide, wide, 0)
    lax.fori_loop(0, n_open, narrow, 0)
    lax.fori_loop(0, n_masked, masked, 0)

    if last:
        row = lax.broadcasted_iota(jnp.int32, (tok, HEAD_DIM), 0)
        col = lax.broadcasted_iota(jnp.int32, (tok, HEAD_DIM), 1)
        eye = row == col
        lines = []
        for ref, lanes in ((m_s, slice(0, HEAD_DIM)), (acc_s, slice(HEAD_DIM, 2 * HEAD_DIM))):
            for g in range(GROUP):
                span = slice(g * tok, (g + 1) * tok)
                lines.append(
                    jnp.sum(jnp.where(eye, ref[span, lanes], 0.0), axis=0, keepdims=True)
                )
        stats = jnp.concatenate(lines, axis=0)
        for w in range(ways):

            @pl.when(step == w)
            def _():
                outs[w][:total, :] = acc_s[:, :HEAD_DIM].astype(jnp.bfloat16)
                for i, piece in enumerate(three_parts(stats)):
                    at = total + i * 2 * GROUP
                    outs[w][at : at + 2 * GROUP, :] = piece


def attend(place, x, first_slot, q, after, carried, block, last, tok_rows, rows):
    sources = x.shape[0]
    src_slots = x.shape[1] // (2 * PAGE_TOK)
    steps, total, _ = q.shape
    tok = total // GROUP
    first = carried is None
    ways = steps // 2
    n_slots = -(-sources * src_slots // WIDE) * WIDE
    straight = lambda i, *_: (i, 0, 0)
    in_specs = [
        pl.BlockSpec(x.shape, lambda i, *_: (0, 0, 0)),
        pl.BlockSpec((1, total, HEAD_DIM), lambda i, *_: (2 * i + block, 0, 0)),
        ANY,
    ]
    sent = total + 3 * 2 * GROUP
    if last:
        out_shape = (jax.ShapeDtypeStruct((sent, HEAD_DIM), jnp.bfloat16),) * ways
        out_specs = (pl.BlockSpec((sent, HEAD_DIM), lambda i, *_: (0, 0)),) * ways
    else:
        out_shape = (
            jax.ShapeDtypeStruct((ways, total, 2 * HEAD_DIM), jnp.float32),
            jax.ShapeDtypeStruct((ways, total, HEAD_DIM), jnp.float32),
        )
        out_specs = (
            pl.BlockSpec((1, total, 2 * HEAD_DIM), straight),
            pl.BlockSpec((1, total, HEAD_DIM), straight),
        )
    extra = ()
    sums = ()
    if last:
        sums = (
            pltpu.VMEM((total, 2 * HEAD_DIM), jnp.float32),
            pltpu.VMEM((total, HEAD_DIM), jnp.float32),
        )
    if not first:
        extra = tuple(carried)
        in_specs += [
            pl.BlockSpec((1, total, 2 * HEAD_DIM), straight),
            pl.BlockSpec((1, total, HEAD_DIM), straight),
        ]
    flops = 8 * ways * total * sources * src_slots * PAGE_TOK * HEAD_DIM
    return pl.pallas_call(
        functools.partial(
            attend_kernel,
            first_slot=first_slot,
            first=first,
            last=last,
            rows=rows,
            tok=tok,
            ways=ways,
            tok_rows=tok_rows,
            block=block,
        ),
        out_shape=out_shape,
        grid_spec=pltpu.PrefetchScalarGridSpec(
            num_scalar_prefetch=1,
            grid=(ways,),
            in_specs=in_specs,
            out_specs=out_specs,
            scratch_shapes=[
                pltpu.VMEM((n_slots * PAGE_TOK, HEAD_DIM), jnp.bfloat16),
                pltpu.VMEM((n_slots * PAGE_TOK, 2 * HEAD_DIM), jnp.bfloat16),
                *sums,
                pltpu.VMEM((sources, HEAD_DIM), jnp.int32),
                pltpu.SMEM((n_slots + 1,), jnp.int32),
                pltpu.SMEM((n_slots + 1,), jnp.int32),
                pltpu.SMEM((n_slots,), jnp.int32),
                pltpu.SMEM((sources, HEAD_DIM), jnp.int32),
                pltpu.SMEM((2,), jnp.int32),
                pltpu.SemaphoreType.DMA(()),
            ],
        ),
        cost_estimate=pl.CostEstimate(
            flops=flops, transcendentals=flops // (8 * HEAD_DIM), bytes_accessed=x.size * 2
        ),
        name="attend_last" if last else "attend_first",
    )(place, x, q, after, *extra)


def merge(parts, a_ref, tok):
    total = GROUP * tok
    row = lax.broadcasted_iota(jnp.int32, (tok, HEAD_DIM), 0)
    col = lax.broadcasted_iota(jnp.int32, (tok, HEAD_DIM), 1)
    eye = row == col
    stats = []
    for part in parts:
        pieces = [
            part[total + i * 2 * GROUP : total + (i + 1) * 2 * GROUP, :].astype(jnp.float32)
            for i in range(3)
        ]
        stats.append((pieces[0] + pieces[1]) + pieces[2])
    tops = functools.reduce(jnp.maximum, [s[:GROUP] for s in stats])
    factors = [jnp.exp2(s[:GROUP] - tops) for s in stats]
    totals = sum(f * s[GROUP:] for f, s in zip(factors, stats))
    for g in range(GROUP):
        span = slice(g * tok, (g + 1) * tok)
        mixed = 0.0
        for f, part in zip(factors, parts):
            ratio = jnp.where(eye, f[g : g + 1] / totals[g : g + 1], 0.0)
            mixed += jnp.sum(ratio, axis=1, keepdims=True) * part[span, :].astype(jnp.float32)
        a_ref[:, g * HEAD_DIM : (g + 1) * HEAD_DIM] = mixed.astype(jnp.bfloat16)


def project_kernel(*refs, n_parts, n_ws, tok, y_first):
    parts = refs[:n_parts]
    ws = refs[n_parts : n_parts + n_ws]
    outs = refs[n_parts + n_ws :]
    keep_ref, send_ref = outs[:2]
    if n_parts == n_ws:
        a_ref = outs[2]

        @pl.when(pl.program_id(0) == 0)
        def _():
            merge(parts, a_ref, tok)

    else:
        a_ref = parts[0]
    depth = a_ref.shape[1] // n_ws
    total = 0.0
    for s in range(n_ws):
        total += jnp.dot(
            a_ref[:, s * depth : (s + 1) * depth], ws[s][...], preferred_element_type=jnp.float32
        )
    if y_first:
        keep, send = total[: tok // 2], total[tok // 2 :]
    else:
        quarters = [total[i * tok // 4 : (i + 1) * tok // 4] for i in range(4)]
        keep = jnp.concatenate(quarters[0::2], axis=0)
        send = jnp.concatenate(quarters[1::2], axis=0)
    keep_ref[...] = keep
    send_ref[...] = send.astype(jnp.bfloat16)


def project(parts, ws, tok, column_part, y_first, width=1024):
    columns = ws[0].shape[1] // COLUMN_PARTS
    steps = columns // width
    fixed = lambda i: (0, 0)
    half = tok // 2
    depth = sum(w.shape[0] for w in ws)
    merging = len(parts) == len(ws)
    out_shape = [
        jax.ShapeDtypeStruct((half, columns), jnp.float32),
        jax.ShapeDtypeStruct((half, columns), jnp.bfloat16),
    ]
    out_specs = [
        pl.BlockSpec((half, width), lambda i: (0, i)),
        pl.BlockSpec((half, width), lambda i: (0, i)),
    ]
    if merging:
        out_shape.append(jax.ShapeDtypeStruct((tok, depth), jnp.bfloat16))
        out_specs.append(pl.BlockSpec((tok, depth), fixed))
    return pl.pallas_call(
        functools.partial(
            project_kernel, n_parts=len(parts), n_ws=len(ws), tok=tok, y_first=y_first
        ),
        out_shape=out_shape,
        grid=(steps,),
        in_specs=[pl.BlockSpec(o.shape, fixed) for o in parts]
        + [
            pl.BlockSpec((w.shape[0], width), lambda i: (0, column_part * steps + i)) for w in ws
        ],
        out_specs=out_specs,
        cost_estimate=pl.CostEstimate(
            flops=2 * tok * depth * columns, transcendentals=0, bytes_accessed=2 * depth * columns
        ),
        name="project",
    )(*parts, *ws)


def local(
    queries, kv_cache, w_out, slot_page_before, slot_page_after, move_out, move_in, positions
):
    n = lax.axis_size("pages")
    slots = kv_cache.shape[0]
    ways = n // KV_HEADS
    tok_rows = BLOCK // n
    tok = BLOCK // ways
    me = lax.axis_index("pages")
    way = me // KV_HEADS
    head = head_of(me % KV_HEADS)
    groups = [[a * KV_HEADS + b for b in range(KV_HEADS)] for a in range(ways)]

    def exchange(x):
        return lax.all_to_all(x, "pages", 0, 0, axis_index_groups=groups, tiled=True)

    ids = jnp.broadcast_to(slot_page_before[:, None, None], (slots, 2, HEAD_DIM))
    ids = ids.astype(kv_cache.dtype)
    cuts = [(0, FIRST_SLOTS), (FIRST_SLOTS, slots - FIRST_SLOTS)]
    arrived = []
    for at, count in cuts:
        piece = split_heads(kv_cache, ids, at, count)
        got = exchange(piece)
        arrived.append(got.reshape(KV_HEADS, -1, HEAD_DIM))
    place = jnp.stack([head, way, positions[0, 0], positions[1, 0]]).astype(jnp.int32)
    q = query_rows(queries, place, ways, tok_rows)

    leaving = outgoing_pages(kv_cache, move_out[0])
    landed = []
    for o in range(1, MOVE_WIN + 1):
        landed.append(permute_to(leaving[o - 1], n, lambda i: (i + o) % n))

    ws = [w_out]
    for s in range(1, ways):
        ws.append(permute_to(w_out, n, lambda i: i ^ s))

    rows = 2 * tok

    def merger(i, s):
        return head_of(i % KV_HEADS) * ways + ((i // KV_HEADS) ^ s)

    partial = []
    after = leaving[0]
    for b in range(2):
        carried = attend(place, arrived[0], 0, q, after, None, b, False, tok_rows, rows)
        out = attend(
            place, arrived[1], FIRST_SLOTS, q, after, carried, b, True, tok_rows, rows
        )
        after = out[0]
        parts = []
        for s in range(ways):
            parts.append(permute_to(out[s], n, lambda i: merger(i, s)))
        partial.append(parts)

    sums = []
    for b in range(2):
        merged = partial[b]
        for c in range(COLUMN_PARTS):
            y_first = (b, c) != (0, 1)
            keep, send, *a = project(merged, ws, tok, c, y_first)
            if a:
                merged = a
            turns = (1, 2, 4) if y_first else (2, 1, 4)
            got = permute_to(send, n, lambda i: i ^ (turns[0] * ways))
            sums.append((keep, got, turns))
    cache_after = arrange_pages(kv_cache, landed, slot_page_after, move_in[0], send)

    results = []
    for keep, got, turns in sums:
        for turn in turns[1:]:
            total = keep + got.astype(jnp.float32)
            half = total.shape[0] // 2
            keep = total[:half]
            got = permute_to(
                total[half:].astype(jnp.bfloat16), n, lambda i: i ^ (turn * ways)
            )
        results.append((keep + got.astype(jnp.float32)).astype(jnp.bfloat16))
    out = jnp.stack(
        [
            jnp.concatenate(results[b * COLUMN_PARTS : (b + 1) * COLUMN_PARTS], axis=1)
            for b in range(2)
        ]
    )
    return (out, cache_after)


def solution(mesh):
    in_specs = (
        P(None, "groups", None),
        P(("groups", "pages"), None, None, None),
        P("pages", None),
        P(("groups", "pages")),
        P(("groups", "pages")),
        P(("groups", "pages"), None),
        P(("groups", "pages"), None),
        P(None, "groups"),
    )
    out_specs = (P(None, ("groups", "pages"), None), P(("groups", "pages"), None, None, None))
    return jax.shard_map(local, mesh=mesh, in_specs=in_specs, out_specs=out_specs, check_vma=False)
```

```python
import functools

import jax
import jax.numpy as jnp
from jax import lax
from jax.experimental import pallas as pl
from jax.experimental.pallas import tpu as pltpu
from jax.sharding import PartitionSpec as P

HEADS = 64
KV_HEADS = 8
HEAD_DIM = 128
PAGE_TOK = 128
BLOCK = 256
MOVE_WIN = 4
GROUP = HEADS // KV_HEADS

FLOOR = -1e30
FAR = 1 << 30
SCALE = HEAD_DIM**-0.5 * 1.4426950408889634

WIDE = 16
NARROW = 8
FIRST_SLOTS = 4
COLUMN_PARTS = 2

ANY = pl.BlockSpec(memory_space=pl.ANY)


def permute_to(x, n, target):
    return lax.ppermute(x, "pages", [(i, target(i)) for i in range(n)])


def head_of(j):
    half = KV_HEADS // 2
    return (j % 2) * half + j // 2


def place_of(p):
    return (p % 2) * 4 + (p // 2 % 2) * 2 + p // 4


def split_heads_kernel(place, kv_ref, ids_ref, *refs, first, count, apart):
    outs = refs[: KV_HEADS if apart else 1]
    buf, in_sems, out_sems = refs[len(outs) :]
    extra = ids_ref.shape[0]
    loads = []
    stores = []
    for d in range(KV_HEADS):
        head = head_of(place[4] ^ d) if apart else head_of(d)
        lanes = pl.ds(pl.multiple_of(head * HEAD_DIM, HEAD_DIM), HEAD_DIM)
        row = [
            pltpu.make_async_copy(
                kv_ref.at[first + i, :, :, lanes],
                buf.at[d, pl.ds(i * PAGE_TOK, PAGE_TOK)],
                in_sems.at[d, i],
            )
            for i in range(count)
        ]
        row.append(
            pltpu.make_async_copy(
                ids_ref, buf.at[d, pl.ds(count * PAGE_TOK, extra)], in_sems.at[d, count]
            )
        )
        loads.append(row)
        to = outs[d] if apart else outs[0].at[d]
        stores.append(pltpu.make_async_copy(buf.at[d], to, out_sems.at[d]))
    for row in loads:
        for load in row:
            load.start()
    for row, store in zip(loads, stores):
        for load in row:
            load.wait()
        store.start()
    for store in stores:
        store.wait()


def split_heads(place, kv_cache, ids, first, count, apart):
    piece = (count * PAGE_TOK + ids.shape[0], 2, HEAD_DIM)
    shape = (KV_HEADS,) + piece
    if apart:
        out_shape = (jax.ShapeDtypeStruct(piece, kv_cache.dtype),) * KV_HEADS
    else:
        out_shape = (jax.ShapeDtypeStruct(shape, kv_cache.dtype),)
    return pl.pallas_call(
        functools.partial(split_heads_kernel, first=first, count=count, apart=apart),
        out_shape=out_shape,
        grid_spec=pltpu.PrefetchScalarGridSpec(
            num_scalar_prefetch=1,
            grid=(),
            in_specs=[ANY, ANY],
            out_specs=(ANY,) * len(out_shape),
            scratch_shapes=[
                pltpu.VMEM(shape, kv_cache.dtype),
                pltpu.SemaphoreType.DMA((KV_HEADS, count + 1)),
                pltpu.SemaphoreType.DMA((KV_HEADS,)),
            ],
        ),
        name="split_heads",
    )(place, kv_cache, ids)


def outgoing_kernel(move_out, kv_ref, *refs):
    outs = refs[:MOVE_WIN]
    buf, in_sems, out_sems = refs[MOVE_WIN:]
    loads = [
        pltpu.make_async_copy(
            kv_ref.at[jnp.maximum(move_out[o], 0)], buf.at[o], in_sems.at[o]
        )
        for o in range(MOVE_WIN)
    ]
    stores = [
        pltpu.make_async_copy(buf.at[o], outs[o], out_sems.at[o]) for o in range(MOVE_WIN)
    ]
    for load in loads:
        load.start()
    for load, store in zip(loads, stores):
        load.wait()
        store.start()
    for store in stores:
        store.wait()


def outgoing_pages(kv_cache, move_out):
    page = jax.ShapeDtypeStruct(kv_cache.shape[1:], kv_cache.dtype)
    return pl.pallas_call(
        outgoing_kernel,
        out_shape=(page,) * MOVE_WIN,
        grid_spec=pltpu.PrefetchScalarGridSpec(
            num_scalar_prefetch=1,
            grid=(),
            in_specs=[ANY],
            out_specs=(ANY,) * MOVE_WIN,
            scratch_shapes=[
                pltpu.VMEM((MOVE_WIN,) + kv_cache.shape[1:], kv_cache.dtype),
                pltpu.SemaphoreType.DMA((MOVE_WIN,)),
                pltpu.SemaphoreType.DMA((MOVE_WIN,)),
            ],
        ),
        name="outgoing_pages",
    )(move_out, kv_cache)


def arrange_kernel(page_after, move_in, kv_ref, *refs):
    arrived = refs[:MOVE_WIN]
    _, out_ref, buf, zero_ref, in_sems, out_sems = refs[MOVE_WIN:]
    slots = out_ref.shape[0]
    filled = []
    for s in range(slots):
        taken = jnp.zeros((), jnp.bool_)
        for o in reversed(range(MOVE_WIN)):
            lands = move_in[o] == s

            @pl.when(lands & jnp.logical_not(taken))
            def _():
                pltpu.make_async_copy(arrived[o], buf.at[s], in_sems.at[s]).start()

            taken = taken | lands
        kept = page_after[s] >= 0

        @pl.when(kept & jnp.logical_not(taken))
        def _():
            pltpu.make_async_copy(kv_ref.at[s], buf.at[s], in_sems.at[s]).start()

        filled.append(kept | taken)
    zero_ref[...] = jnp.zeros(zero_ref.shape, zero_ref.dtype)
    for s in range(slots):

        @pl.when(filled[s])
        def _():
            pltpu.make_async_copy(kv_ref.at[s], buf.at[s], in_sems.at[s]).wait()
            pltpu.make_async_copy(buf.at[s], out_ref.at[s], out_sems.at[s]).start()

        @pl.when(jnp.logical_not(filled[s]))
        def _():
            pltpu.make_async_copy(zero_ref, out_ref.at[s], out_sems.at[s]).start()

    for s in range(slots):
        pltpu.make_async_copy(zero_ref, out_ref.at[s], out_sems.at[s]).wait()


def arrange_pages(kv_cache, arrived, page_after, move_in, after):
    slots = kv_cache.shape[0]
    return pl.pallas_call(
        arrange_kernel,
        out_shape=jax.ShapeDtypeStruct(kv_cache.shape, kv_cache.dtype),
        grid_spec=pltpu.PrefetchScalarGridSpec(
            num_scalar_prefetch=2,
            grid=(),
            in_specs=[ANY] * (2 + MOVE_WIN),
            out_specs=ANY,
            scratch_shapes=[
                pltpu.VMEM(kv_cache.shape, kv_cache.dtype),
                pltpu.VMEM(kv_cache.shape[1:], kv_cache.dtype),
                pltpu.SemaphoreType.DMA((slots,)),
                pltpu.SemaphoreType.DMA((slots,)),
            ],
        ),
        name="arrange_pages",
    )(page_after, move_in, kv_cache, *arrived, after)


def rows_kernel(place, q_ref, out_ref, *, ways, tok_rows):
    tok = out_ref.shape[1] // GROUP
    gp = GROUP // ways
    head = place[0]
    t_rel = pl.program_id(0) // 2
    t = place[1] ^ t_rel
    for p in range(KV_HEADS):
        kx = place_of(p)
        at = pl.multiple_of(((kx ^ head) * ways + t) * tok_rows, tok_rows)
        for gx in range(GROUP):
            g = ((gx // gp) ^ t) * gp + gx % gp
            lanes = pl.ds(pl.multiple_of(g * HEAD_DIM, HEAD_DIM), HEAD_DIM)
            to = gx * tok + p * tok_rows
            out_ref[0, to : to + tok_rows, :] = q_ref[0, pl.ds(at, tok_rows), lanes]


def query_rows(queries, place, ways, tok_rows):
    width = GROUP * HEAD_DIM
    tok = KV_HEADS * tok_rows
    dtype = queries.dtype
    if tok_rows % 16:
        queries = lax.dynamic_slice_in_dim(queries, place[0] * width, width, axis=2)
        queries = queries.astype(jnp.float32)
        column = lambda i, place: (i % 2, 0, 0)
    else:
        column = lambda i, place: (i % 2, 0, place[0])
    return pl.pallas_call(
        functools.partial(rows_kernel, ways=ways, tok_rows=tok_rows),
        out_shape=jax.ShapeDtypeStruct((2 * ways, GROUP * tok, HEAD_DIM), queries.dtype),
        grid_spec=pltpu.PrefetchScalarGridSpec(
            num_scalar_prefetch=1,
            grid=(2 * ways,),
            in_specs=[pl.BlockSpec((1, queries.shape[1], width), column)],
            out_specs=pl.BlockSpec((1, GROUP * tok, HEAD_DIM), lambda i, place: (i, 0, 0)),
        ),
        name="query_rows",
    )(place, queries).astype(dtype)


def three_parts(x):
    high = x.astype(jnp.bfloat16)
    rest = x - high.astype(jnp.float32)
    mid = rest.astype(jnp.bfloat16)
    low = (rest - mid.astype(jnp.float32)).astype(jnp.bfloat16)
    return high, mid, low


def attend_kernel(
    place, *refs, n_x, first_slot, first, last, rows, tok, ways, tok_rows, block
):
    xs, q_ref, refs = refs[:n_x], refs[n_x], refs[n_x + 1 :]
    if n_x == 1:
        x_ref = xs[0]
    else:
        refs, x_ref, x_sems = refs[:-2], refs[-2], refs[-1]
    n_in = 0 if first else 2
    carried = refs[:n_in]
    outs = refs[n_in : n_in + (ways if last else 2)]
    k_s, v_s, *sums, ids_s, order, rest, pages, ids, counts, sem = refs[n_in + len(outs) :]
    if last:
        acc_s, m_s = sums
    else:
        acc_s, m_s = outs[0].at[0], outs[1].at[0]
    step = pl.program_id(0)
    sources = x_ref.shape[0]
    src_slots = x_ref.shape[1] // (2 * PAGE_TOK)
    n_slots = sources * src_slots
    head, way = place[0], place[1]

    @pl.when(step == 0)
    def _():
        if n_x > 1:
            loads = [
                pltpu.make_async_copy(x, x_ref.at[i], x_sems.at[i]) for i, x in enumerate(xs)
            ]
            for load in loads:
                load.start()
            for load in loads:
                load.wait()
        end = src_slots * 2 * PAGE_TOK
        extra = x_ref.shape[1] - end
        row = lax.broadcasted_iota(jnp.int32, (extra, HEAD_DIM), 0)
        col = lax.broadcasted_iota(jnp.int32, (extra, HEAD_DIM), 1)
        for src in range(sources):
            tail = x_ref[src, end : end + extra, :].astype(jnp.float32)
            line = jnp.sum(jnp.where(row == 2 * col, tail, 0.0), axis=0, keepdims=True)
            ids_s[src : src + 1, :] = line.astype(jnp.int32)
        copy = pltpu.make_async_copy(ids_s, ids, sem)
        copy.start()
        copy.wait()
        lowest = jnp.minimum(place[2], place[3])

        def fully(page):
            return (page >= 0) & (page * PAGE_TOK + (PAGE_TOK - 1) <= lowest)

        n_full = jnp.int32(0)
        n_rest = jnp.int32(0)
        for i in range(n_slots):
            page = ids[i // src_slots, first_slot + i % src_slots]
            pages[i] = page
            yes = fully(page)
            order[n_full] = i
            rest[n_rest] = i
            n_full += yes.astype(jnp.int32)
            n_rest += ((page >= 0) & jnp.logical_not(yes)).astype(jnp.int32)

        def append(i, carry):
            order[n_full + i] = rest[i]
            return carry

        lax.fori_loop(0, n_rest, append, 0)
        n_live = n_full + n_rest
        counts[0] = n_full
        counts[1] = n_live

        row = lax.broadcasted_iota(jnp.int32, (2 * PAGE_TOK, 2 * PAGE_TOK), 0)
        col = lax.broadcasted_iota(jnp.int32, (2 * PAGE_TOK, 2 * PAGE_TOK), 1)
        want = jnp.where(row < PAGE_TOK, 2 * row, 2 * (row - PAGE_TOK) + 1)
        pick = jnp.where(col == want, 1.0, 0.0).astype(jnp.bfloat16)
        ones = jnp.ones((PAGE_TOK, HEAD_DIM), jnp.bfloat16)

        def split_step(i, carry):
            for s in range(NARROW):
                at = i * NARROW + s
                slot = order[jnp.minimum(at, n_live - 1)]
                both = jnp.dot(
                    pick,
                    x_ref[
                        slot // src_slots,
                        pl.ds(
                            pl.multiple_of(slot % src_slots * 2 * PAGE_TOK, 2 * PAGE_TOK),
                            2 * PAGE_TOK,
                        ),
                        :,
                    ],
                    preferred_element_type=jnp.float32,
                ).astype(jnp.bfloat16)
                to = pl.ds(pl.multiple_of(at * PAGE_TOK, PAGE_TOK), PAGE_TOK)
                k_s[to, :] = both[:PAGE_TOK]
                v_s[to, :HEAD_DIM] = both[PAGE_TOK:]
                v_s[to, HEAD_DIM:] = ones
            return carry

        lax.fori_loop(0, (n_live + NARROW - 1) // NARROW, split_step, 0)

    n_full, n_live = counts[0], counts[1]
    total = GROUP * tok
    if first:
        m_s[...] = jnp.full(m_s.shape, FLOOR, jnp.float32)
        acc_s[...] = jnp.zeros(acc_s.shape, jnp.float32)
    else:
        acc_s[...] = carried[0][0]
        m_s[...] = carried[1][0]

    if block is None:
        t_rel, b = step // 2, step % 2
    else:
        t_rel, b = step, block
    line = lax.broadcasted_iota(jnp.int32, (tok, PAGE_TOK), 0)
    p = line // tok_rows
    kx = place_of(p)
    token = ((kx ^ head) * ways + (t_rel ^ way)) * tok_rows + line % tok_rows
    q_at = token + jnp.where(b == 0, place[2], place[3])

    def tile_step(at, size, masked):
        span_k = pl.ds(pl.multiple_of(at * PAGE_TOK, PAGE_TOK), size * PAGE_TOK)
        keys = k_s[span_k, :]
        values = v_s[span_k, :]
        if masked:
            lane = lax.broadcasted_iota(jnp.int32, (tok, PAGE_TOK), 1)
            visible = []
            for s in range(size):
                slot = order[jnp.minimum(at + s, n_live - 1)]
                start = jnp.where(at + s < n_live, pages[slot] * PAGE_TOK, FAR)
                seen = lane + start <= q_at
                visible.append(jnp.concatenate([seen] * (rows // tok), axis=0))

        def score(part):
            return lax.dot_general(
                q_ref[0, part * rows : (part + 1) * rows, :],
                keys,
                (((1,), (1,)), ((), ())),
                preferred_element_type=jnp.float32,
            )

        def soften(part, scores):
            span = slice(part * rows, (part + 1) * rows)
            pieces = [scores[:, s * PAGE_TOK : (s + 1) * PAGE_TOK] for s in range(size)]
            if masked:
                pieces = [jnp.where(v, x, FLOOR) for v, x in zip(visible, pieces)]
            peak = functools.reduce(jnp.maximum, pieces)
            m_old = m_s[span, :]
            m_new = jnp.maximum(m_old, jnp.max(peak, axis=1, keepdims=True) * SCALE)
            shift = jnp.maximum(m_new, 0.5 * FLOOR * SCALE) if masked else m_new
            weights = jnp.concatenate(
                [jnp.exp2(x * SCALE - shift).astype(jnp.bfloat16) for x in pieces], axis=1
            )
            m_s[span, :] = m_new
            return weights, jnp.exp2(m_old - m_new)

        def gather(part, weights, alpha):
            span = slice(part * rows, (part + 1) * rows)
            mixed = jnp.dot(weights, values, preferred_element_type=jnp.float32)
            acc_s[span, :HEAD_DIM] = acc_s[span, :HEAD_DIM] * alpha + mixed[:, :HEAD_DIM]
            acc_s[span, HEAD_DIM:] = acc_s[span, HEAD_DIM:] * alpha + mixed[:, HEAD_DIM:]

        parts = total // rows
        scores = score(0)
        waiting = None
        for part in range(parts):
            following = score(part + 1) if part + 1 < parts else None
            weights, alpha = soften(part, scores)
            if waiting is not None:
                gather(*waiting)
            waiting = (part, weights, alpha)
            scores = following
        gather(*waiting)

    n_wide = n_full // WIDE
    n_open = (n_full - n_wide * WIDE) // NARROW
    base = n_wide * WIDE
    done = base + n_open * NARROW
    n_masked = (n_live - done + NARROW - 1) // NARROW

    def wide(i, carry):
        tile_step(i * WIDE, WIDE, False)
        return carry

    def narrow(i, carry):
        tile_step(base + i * NARROW, NARROW, False)
        return carry

    def masked(i, carry):
        tile_step(done + i * NARROW, NARROW, True)
        return carry

    lax.fori_loop(0, n_wide, wide, 0)
    lax.fori_loop(0, n_open, narrow, 0)
    lax.fori_loop(0, n_masked, masked, 0)

    if last:
        row = lax.broadcasted_iota(jnp.int32, (tok, HEAD_DIM), 0)
        col = lax.broadcasted_iota(jnp.int32, (tok, HEAD_DIM), 1)
        eye = row == col
        lines = []
        for ref, lanes in ((m_s, slice(0, HEAD_DIM)), (acc_s, slice(HEAD_DIM, 2 * HEAD_DIM))):
            for g in range(GROUP):
                span = slice(g * tok, (g + 1) * tok)
                lines.append(
                    jnp.sum(jnp.where(eye, ref[span, lanes], 0.0), axis=0, keepdims=True)
                )
        stats = jnp.concatenate(lines, axis=0)
        for w in range(ways):

            @pl.when(step == w)
            def _():
                outs[w][:total, :] = acc_s[:, :HEAD_DIM].astype(jnp.bfloat16)
                for i, piece in enumerate(three_parts(stats)):
                    at = total + i * 2 * GROUP
                    outs[w][at : at + 2 * GROUP, :] = piece


def attend(place, xs, first_slot, q, carried, block, tok_rows, rows):
    sources = KV_HEADS
    depth = xs[0].shape[-2]
    src_slots = depth // (2 * PAGE_TOK)
    steps, total, _ = q.shape
    tok = total // GROUP
    first = carried is None
    last = block is not None
    ways = steps // 2
    n_slots = -(-sources * src_slots // WIDE) * WIDE
    if last:
        grid = ways
        at = lambda i, *_: (2 * i + block, 0, 0)
    else:
        grid = steps
        at = lambda i, *_: (i, 0, 0)
    if len(xs) == 1:
        in_specs = [pl.BlockSpec(xs[0].shape, lambda i, *_: (0, 0, 0))]
        landing = []
    else:
        in_specs = [ANY] * len(xs)
        landing = [
            pltpu.VMEM((sources, depth, HEAD_DIM), xs[0].dtype),
            pltpu.SemaphoreType.DMA((sources,)),
        ]
    in_specs.append(pl.BlockSpec((1, total, HEAD_DIM), at))
    sent = total + 3 * 2 * GROUP
    if last:
        out_shape = (jax.ShapeDtypeStruct((sent, HEAD_DIM), jnp.bfloat16),) * ways
        out_specs = (pl.BlockSpec((sent, HEAD_DIM), lambda i, *_: (0, 0)),) * ways
    else:
        out_shape = (
            jax.ShapeDtypeStruct((steps, total, 2 * HEAD_DIM), jnp.float32),
            jax.ShapeDtypeStruct((steps, total, HEAD_DIM), jnp.float32),
        )
        out_specs = (
            pl.BlockSpec((1, total, 2 * HEAD_DIM), at),
            pl.BlockSpec((1, total, HEAD_DIM), at),
        )
    extra = ()
    sums = ()
    if last:
        sums = (
            pltpu.VMEM((total, 2 * HEAD_DIM), jnp.float32),
            pltpu.VMEM((total, HEAD_DIM), jnp.float32),
        )
    if not first:
        extra = tuple(carried)
        in_specs += [
            pl.BlockSpec((1, total, 2 * HEAD_DIM), at),
            pl.BlockSpec((1, total, HEAD_DIM), at),
        ]
    flops = 8 * grid * total * sources * src_slots * PAGE_TOK * HEAD_DIM
    return pl.pallas_call(
        functools.partial(
            attend_kernel,
            n_x=len(xs),
            first_slot=first_slot,
            first=first,
            last=last,
            rows=rows,
            tok=tok,
            ways=ways,
            tok_rows=tok_rows,
            block=block,
        ),
        out_shape=out_shape,
        grid_spec=pltpu.PrefetchScalarGridSpec(
            num_scalar_prefetch=1,
            grid=(grid,),
            in_specs=in_specs,
            out_specs=out_specs,
            scratch_shapes=[
                pltpu.VMEM((n_slots * PAGE_TOK, HEAD_DIM), jnp.bfloat16),
                pltpu.VMEM((n_slots * PAGE_TOK, 2 * HEAD_DIM), jnp.bfloat16),
                *sums,
                pltpu.VMEM((sources, HEAD_DIM), jnp.int32),
                pltpu.SMEM((n_slots + 1,), jnp.int32),
                pltpu.SMEM((n_slots + 1,), jnp.int32),
                pltpu.SMEM((n_slots,), jnp.int32),
                pltpu.SMEM((sources, HEAD_DIM), jnp.int32),
                pltpu.SMEM((2,), jnp.int32),
                pltpu.SemaphoreType.DMA(()),
                *landing,
            ],
        ),
        cost_estimate=pl.CostEstimate(
            flops=flops,
            transcendentals=flops // (8 * HEAD_DIM),
            bytes_accessed=4 * sources * depth * HEAD_DIM,
        ),
        name="attend_last" if last else "attend_first",
    )(place, *xs, q, *extra)


def merge(parts, a_ref, tok):
    total = GROUP * tok
    row = lax.broadcasted_iota(jnp.int32, (tok, HEAD_DIM), 0)
    col = lax.broadcasted_iota(jnp.int32, (tok, HEAD_DIM), 1)
    eye = row == col
    stats = []
    for part in parts:
        pieces = [
            part[total + i * 2 * GROUP : total + (i + 1) * 2 * GROUP, :].astype(jnp.float32)
            for i in range(3)
        ]
        stats.append((pieces[0] + pieces[1]) + pieces[2])
    tops = functools.reduce(jnp.maximum, [s[:GROUP] for s in stats])
    factors = [jnp.exp2(s[:GROUP] - tops) for s in stats]
    totals = sum(f * s[GROUP:] for f, s in zip(factors, stats))
    for g in range(GROUP):
        span = slice(g * tok, (g + 1) * tok)
        mixed = 0.0
        for f, part in zip(factors, parts):
            ratio = jnp.where(eye, f[g : g + 1] / totals[g : g + 1], 0.0)
            mixed += jnp.sum(ratio, axis=1, keepdims=True) * part[span, :].astype(jnp.float32)
        a_ref[:, g * HEAD_DIM : (g + 1) * HEAD_DIM] = mixed.astype(jnp.bfloat16)


def project_kernel(*refs, n_parts, n_ws, tok, y_first):
    parts = refs[:n_parts]
    ws = refs[n_parts : n_parts + n_ws]
    outs = refs[n_parts + n_ws :]
    keep_ref, send_ref = outs[:2]
    if n_parts == n_ws:
        a_ref = outs[2]

        @pl.when(pl.program_id(0) == 0)
        def _():
            merge(parts, a_ref, tok)

    else:
        a_ref = parts[0]
    depth = a_ref.shape[1] // n_ws
    total = 0.0
    for s in range(n_ws):
        total += jnp.dot(
            a_ref[:, s * depth : (s + 1) * depth], ws[s][...], preferred_element_type=jnp.float32
        )
    if y_first:
        keep, send = total[: tok // 2], total[tok // 2 :]
    else:
        quarters = [total[i * tok // 4 : (i + 1) * tok // 4] for i in range(4)]
        keep = jnp.concatenate(quarters[0::2], axis=0)
        send = jnp.concatenate(quarters[1::2], axis=0)
    keep_ref[...] = keep
    send_ref[...] = send.astype(jnp.bfloat16)


def project(parts, ws, tok, column_part, y_first, width=1024):
    columns = ws[0].shape[1] // COLUMN_PARTS
    steps = columns // width
    fixed = lambda i: (0, 0)
    half = tok // 2
    depth = sum(w.shape[0] for w in ws)
    merging = len(parts) == len(ws)
    out_shape = [
        jax.ShapeDtypeStruct((half, columns), jnp.float32),
        jax.ShapeDtypeStruct((half, columns), jnp.bfloat16),
    ]
    out_specs = [
        pl.BlockSpec((half, width), lambda i: (0, i)),
        pl.BlockSpec((half, width), lambda i: (0, i)),
    ]
    if merging:
        out_shape.append(jax.ShapeDtypeStruct((tok, depth), jnp.bfloat16))
        out_specs.append(pl.BlockSpec((tok, depth), fixed))
    return pl.pallas_call(
        functools.partial(
            project_kernel, n_parts=len(parts), n_ws=len(ws), tok=tok, y_first=y_first
        ),
        out_shape=out_shape,
        grid=(steps,),
        in_specs=[pl.BlockSpec(o.shape, fixed) for o in parts]
        + [
            pl.BlockSpec((w.shape[0], width), lambda i: (0, column_part * steps + i)) for w in ws
        ],
        out_specs=out_specs,
        cost_estimate=pl.CostEstimate(
            flops=2 * tok * depth * columns, transcendentals=0, bytes_accessed=2 * depth * columns
        ),
        name="project",
    )(*parts, *ws)


def local(
    queries, kv_cache, w_out, slot_page_before, slot_page_after, move_out, move_in, positions
):
    n = lax.axis_size("pages")
    slots = kv_cache.shape[0]
    ways = n // KV_HEADS
    tok_rows = BLOCK // n
    tok = BLOCK // ways
    me = lax.axis_index("pages")
    way = me // KV_HEADS
    head = head_of(me % KV_HEADS)
    groups = [[a * KV_HEADS + b for b in range(KV_HEADS)] for a in range(ways)]

    def exchange(x):
        return lax.all_to_all(x, "pages", 0, 0, axis_index_groups=groups, tiled=True)

    ids = jnp.broadcast_to(slot_page_before[:, None, None], (slots, 2, HEAD_DIM))
    ids = ids.astype(kv_cache.dtype)
    spots = [head, way, positions[0, 0], positions[1, 0], me % KV_HEADS]
    place = jnp.stack(spots).astype(jnp.int32)
    (piece,) = split_heads(slot_page_before, kv_cache, ids, 0, FIRST_SLOTS, False)
    early = [exchange(piece).reshape(KV_HEADS, -1, HEAD_DIM)]
    pieces = split_heads(place, kv_cache, ids, FIRST_SLOTS, slots - FIRST_SLOTS, True)
    late = [pieces[0]]
    for d in range(1, KV_HEADS):
        late.append(permute_to(pieces[d], n, lambda i: i ^ d))
    late = [x.reshape(-1, HEAD_DIM) for x in late]
    q = query_rows(queries, place, ways, tok_rows)

    leaving = outgoing_pages(kv_cache, move_out[0])
    landed = []
    for o in range(1, MOVE_WIN + 1):
        landed.append(permute_to(leaving[o - 1], n, lambda i: (i + o) % n))

    ws = [w_out]
    for s in range(1, ways):
        ws.append(permute_to(w_out, n, lambda i: i ^ s))

    rows = 2 * tok
    carried = attend(place, early, 0, q, None, None, tok_rows, rows)

    def merger(i, s):
        return head_of(i % KV_HEADS) * ways + ((i // KV_HEADS) ^ s)

    partial = []
    for b in range(2):
        out = attend(place, late, FIRST_SLOTS, q, carried, b, tok_rows, rows)
        parts = []
        for s in range(ways):
            parts.append(permute_to(out[s], n, lambda i: merger(i, s)))
        partial.append(parts)

    sums = []
    for b in range(2):
        merged = partial[b]
        for c in range(COLUMN_PARTS):
            y_first = (b, c) != (0, 1)
            keep, send, *a = project(merged, ws, tok, c, y_first)
            if a:
                merged = a
            turns = (1, 2, 4) if y_first else (2, 1, 4)
            got = permute_to(send, n, lambda i: i ^ (turns[0] * ways))
            sums.append((keep, got, turns))
    cache_after = arrange_pages(kv_cache, landed, slot_page_after, move_in[0], send)

    results = []
    for keep, got, turns in sums:
        for turn in turns[1:]:
            total = keep + got.astype(jnp.float32)
            half = total.shape[0] // 2
            keep = total[:half]
            got = permute_to(
                total[half:].astype(jnp.bfloat16), n, lambda i: i ^ (turn * ways)
            )
        results.append((keep + got.astype(jnp.float32)).astype(jnp.bfloat16))
    out = jnp.stack(
        [
            jnp.concatenate(results[b * COLUMN_PARTS : (b + 1) * COLUMN_PARTS], axis=1)
            for b in range(2)
        ]
    )
    return (out, cache_after)


def solution(mesh):
    in_specs = (
        P(None, "groups", None),
        P(("groups", "pages"), None, None, None),
        P("pages", None),
        P(("groups", "pages")),
        P(("groups", "pages")),
        P(("groups", "pages"), None),
        P(("groups", "pages"), None),
        P(None, "groups"),
    )
    out_specs = (P(None, ("groups", "pages"), None), P(("groups", "pages"), None, None, None))
    return jax.shard_map(local, mesh=mesh, in_specs=in_specs, out_specs=out_specs, check_vma=False)
```

```python
import functools

import jax
import jax.numpy as jnp
from jax import lax
from jax.experimental import pallas as pl
from jax.experimental.pallas import tpu as pltpu
from jax.sharding import PartitionSpec as P

HEADS = 64
KV_HEADS = 8
HEAD_DIM = 128
PAGE_TOK = 128
BLOCK = 256
MOVE_WIN = 4
GROUP = HEADS // KV_HEADS

FLOOR = -1e30
FAR = 1 << 30
SCALE = HEAD_DIM**-0.5 * 1.4426950408889634

WIDE = 16
NARROW = 8
FIRST_SLOTS = 5
COLUMN_PARTS = 2

ANY = pl.BlockSpec(memory_space=pl.ANY)


def permute_to(x, n, target):
    return lax.ppermute(x, "pages", [(i, target(i)) for i in range(n)])


def head_of(j):
    half = KV_HEADS // 2
    return (j % 2) * half + j // 2


def place_of(p):
    return (p % 2) * 4 + (p // 2 % 2) * 2 + p // 4


def split_heads_kernel(kv_ref, ids_ref, out_ref, buf, in_sems, out_sems, *, first, count):
    extra = ids_ref.shape[0]
    loads = []
    for d in range(KV_HEADS):
        lanes = pl.ds(head_of(d) * HEAD_DIM, HEAD_DIM)
        row = [
            pltpu.make_async_copy(
                kv_ref.at[first + i, :, :, lanes],
                buf.at[d, pl.ds(i * PAGE_TOK, PAGE_TOK)],
                in_sems.at[d, i],
            )
            for i in range(count)
        ]
        row.append(
            pltpu.make_async_copy(
                ids_ref, buf.at[d, pl.ds(count * PAGE_TOK, extra)], in_sems.at[d, count]
            )
        )
        loads.append(row)
    stores = [
        pltpu.make_async_copy(buf.at[d], out_ref.at[d], out_sems.at[d])
        for d in range(KV_HEADS)
    ]
    for row in loads:
        for load in row:
            load.start()
    for row, store in zip(loads, stores):
        for load in row:
            load.wait()
        store.start()
    for store in stores:
        store.wait()


def split_heads(kv_cache, ids, first, count):
    shape = (KV_HEADS, count * PAGE_TOK + ids.shape[0], 2, HEAD_DIM)
    return pl.pallas_call(
        functools.partial(split_heads_kernel, first=first, count=count),
        out_shape=jax.ShapeDtypeStruct(shape, kv_cache.dtype),
        in_specs=[ANY, ANY],
        out_specs=ANY,
        scratch_shapes=[
            pltpu.VMEM(shape, kv_cache.dtype),
            pltpu.SemaphoreType.DMA((KV_HEADS, count + 1)),
            pltpu.SemaphoreType.DMA((KV_HEADS,)),
        ],
        name="split_heads",
    )(kv_cache, ids)


def outgoing_kernel(move_out, kv_ref, *refs):
    outs = refs[:MOVE_WIN]
    buf, in_sems, out_sems = refs[MOVE_WIN:]
    loads = [
        pltpu.make_async_copy(
            kv_ref.at[jnp.maximum(move_out[o], 0)], buf.at[o], in_sems.at[o]
        )
        for o in range(MOVE_WIN)
    ]
    stores = [
        pltpu.make_async_copy(buf.at[o], outs[o], out_sems.at[o]) for o in range(MOVE_WIN)
    ]
    for load in loads:
        load.start()
    for load, store in zip(loads, stores):
        load.wait()
        store.start()
    for store in stores:
        store.wait()


def outgoing_pages(kv_cache, move_out):
    page = jax.ShapeDtypeStruct(kv_cache.shape[1:], kv_cache.dtype)
    return pl.pallas_call(
        outgoing_kernel,
        out_shape=(page,) * MOVE_WIN,
        grid_spec=pltpu.PrefetchScalarGridSpec(
            num_scalar_prefetch=1,
            grid=(),
            in_specs=[ANY],
            out_specs=(ANY,) * MOVE_WIN,
            scratch_shapes=[
                pltpu.VMEM((MOVE_WIN,) + kv_cache.shape[1:], kv_cache.dtype),
                pltpu.SemaphoreType.DMA((MOVE_WIN,)),
                pltpu.SemaphoreType.DMA((MOVE_WIN,)),
            ],
        ),
        name="outgoing_pages",
    )(move_out, kv_cache)


def arrange_kernel(page_after, move_in, kv_ref, *refs):
    arrived = refs[:MOVE_WIN]
    _, out_ref, buf, zero_ref, in_sems, out_sems = refs[MOVE_WIN:]
    slots = out_ref.shape[0]
    filled = []
    for s in range(slots):
        taken = jnp.zeros((), jnp.bool_)
        for o in reversed(range(MOVE_WIN)):
            lands = move_in[o] == s

            @pl.when(lands & jnp.logical_not(taken))
            def _():
                pltpu.make_async_copy(arrived[o], buf.at[s], in_sems.at[s]).start()

            taken = taken | lands
        kept = page_after[s] >= 0

        @pl.when(kept & jnp.logical_not(taken))
        def _():
            pltpu.make_async_copy(kv_ref.at[s], buf.at[s], in_sems.at[s]).start()

        filled.append(kept | taken)
    zero_ref[...] = jnp.zeros(zero_ref.shape, zero_ref.dtype)
    for s in range(slots):

        @pl.when(filled[s])
        def _():
            pltpu.make_async_copy(kv_ref.at[s], buf.at[s], in_sems.at[s]).wait()
            pltpu.make_async_copy(buf.at[s], out_ref.at[s], out_sems.at[s]).start()

        @pl.when(jnp.logical_not(filled[s]))
        def _():
            pltpu.make_async_copy(zero_ref, out_ref.at[s], out_sems.at[s]).start()

    for s in range(slots):
        pltpu.make_async_copy(zero_ref, out_ref.at[s], out_sems.at[s]).wait()


def arrange_pages(kv_cache, arrived, page_after, move_in, after):
    slots = kv_cache.shape[0]
    return pl.pallas_call(
        arrange_kernel,
        out_shape=jax.ShapeDtypeStruct(kv_cache.shape, kv_cache.dtype),
        grid_spec=pltpu.PrefetchScalarGridSpec(
            num_scalar_prefetch=2,
            grid=(),
            in_specs=[ANY] * (2 + MOVE_WIN),
            out_specs=ANY,
            scratch_shapes=[
                pltpu.VMEM(kv_cache.shape, kv_cache.dtype),
                pltpu.VMEM(kv_cache.shape[1:], kv_cache.dtype),
                pltpu.SemaphoreType.DMA((slots,)),
                pltpu.SemaphoreType.DMA((slots,)),
            ],
        ),
        name="arrange_pages",
    )(page_after, move_in, kv_cache, *arrived, after)


def rows_kernel(place, q_ref, out_ref, *, ways, tok_rows):
    tok = out_ref.shape[1] // GROUP
    gp = GROUP // ways
    head = place[0]
    t_rel = pl.program_id(0) // 2
    t = place[1] ^ t_rel
    for p in range(KV_HEADS):
        kx = place_of(p)
        at = pl.multiple_of(((kx ^ head) * ways + t) * tok_rows, tok_rows)
        for gx in range(GROUP):
            g = ((gx // gp) ^ t) * gp + gx % gp
            lanes = pl.ds(pl.multiple_of(g * HEAD_DIM, HEAD_DIM), HEAD_DIM)
            to = gx * tok + p * tok_rows
            out_ref[0, to : to + tok_rows, :] = q_ref[0, pl.ds(at, tok_rows), lanes]


def query_rows(queries, place, ways, tok_rows):
    width = GROUP * HEAD_DIM
    tok = KV_HEADS * tok_rows
    dtype = queries.dtype
    if tok_rows % 16:
        queries = lax.dynamic_slice_in_dim(queries, place[0] * width, width, axis=2)
        queries = queries.astype(jnp.float32)
        column = lambda i, place: (i % 2, 0, 0)
    else:
        column = lambda i, place: (i % 2, 0, place[0])
    return pl.pallas_call(
        functools.partial(rows_kernel, ways=ways, tok_rows=tok_rows),
        out_shape=jax.ShapeDtypeStruct((2 * ways, GROUP * tok, HEAD_DIM), queries.dtype),
        grid_spec=pltpu.PrefetchScalarGridSpec(
            num_scalar_prefetch=1,
            grid=(2 * ways,),
            in_specs=[pl.BlockSpec((1, queries.shape[1], width), column)],
            out_specs=pl.BlockSpec((1, GROUP * tok, HEAD_DIM), lambda i, place: (i, 0, 0)),
        ),
        name="query_rows",
    )(place, queries).astype(dtype)


def three_parts(x):
    high = x.astype(jnp.bfloat16)
    rest = x - high.astype(jnp.float32)
    mid = rest.astype(jnp.bfloat16)
    low = (rest - mid.astype(jnp.float32)).astype(jnp.bfloat16)
    return high, mid, low


def attend_kernel(
    place, x_ref, q_ref, *refs, first_slot, first, last, rows, tok, ways, tok_rows, block
):
    n_in = 0 if first else 2
    carried = refs[:n_in]
    outs = refs[n_in : n_in + (ways if last else 2)]
    k_s, v_s, *sums, ids_s, order, rest, pages, ids, counts, sem = refs[n_in + len(outs) :]
    if last:
        acc_s, m_s = sums
    else:
        acc_s, m_s = outs[0].at[0], outs[1].at[0]
    step = pl.program_id(0)
    sources = x_ref.shape[0]
    src_slots = x_ref.shape[1] // (2 * PAGE_TOK)
    n_slots = sources * src_slots
    head, way = place[0], place[1]

    @pl.when(step == 0)
    def _():
        end = src_slots * 2 * PAGE_TOK
        extra = x_ref.shape[1] - end
        row = lax.broadcasted_iota(jnp.int32, (extra, HEAD_DIM), 0)
        col = lax.broadcasted_iota(jnp.int32, (extra, HEAD_DIM), 1)
        for src in range(sources):
            tail = x_ref[src, end : end + extra, :].astype(jnp.float32)
            line = jnp.sum(jnp.where(row == 2 * col, tail, 0.0), axis=0, keepdims=True)
            ids_s[src : src + 1, :] = line.astype(jnp.int32)
        copy = pltpu.make_async_copy(ids_s, ids, sem)
        copy.start()
        copy.wait()
        lowest = jnp.minimum(place[2], place[3])

        def fully(page):
            return (page >= 0) & (page * PAGE_TOK + (PAGE_TOK - 1) <= lowest)

        n_full = jnp.int32(0)
        n_rest = jnp.int32(0)
        for i in range(n_slots):
            page = ids[i // src_slots, first_slot + i % src_slots]
            pages[i] = page
            yes = fully(page)
            order[n_full] = i
            rest[n_rest] = i
            n_full += yes.astype(jnp.int32)
            n_rest += ((page >= 0) & jnp.logical_not(yes)).astype(jnp.int32)

        def append(i, carry):
            order[n_full + i] = rest[i]
            return carry

        lax.fori_loop(0, n_rest, append, 0)
        n_live = n_full + n_rest
        counts[0] = n_full
        counts[1] = n_live

        row = lax.broadcasted_iota(jnp.int32, (2 * PAGE_TOK, 2 * PAGE_TOK), 0)
        col = lax.broadcasted_iota(jnp.int32, (2 * PAGE_TOK, 2 * PAGE_TOK), 1)
        want = jnp.where(row < PAGE_TOK, 2 * row, 2 * (row - PAGE_TOK) + 1)
        pick = jnp.where(col == want, 1.0, 0.0).astype(jnp.bfloat16)
        ones = jnp.ones((PAGE_TOK, HEAD_DIM), jnp.bfloat16)

        def split_step(i, carry):
            for s in range(NARROW):
                at = i * NARROW + s
                slot = order[jnp.minimum(at, n_live - 1)]
                both = jnp.dot(
                    pick,
                    x_ref[
                        slot // src_slots,
                        pl.ds(
                            pl.multiple_of(slot % src_slots * 2 * PAGE_TOK, 2 * PAGE_TOK),
                            2 * PAGE_TOK,
                        ),
                        :,
                    ],
                    preferred_element_type=jnp.float32,
                ).astype(jnp.bfloat16)
                to = pl.ds(pl.multiple_of(at * PAGE_TOK, PAGE_TOK), PAGE_TOK)
                k_s[to, :] = both[:PAGE_TOK]
                v_s[to, :HEAD_DIM] = both[PAGE_TOK:]
                v_s[to, HEAD_DIM:] = ones
            return carry

        lax.fori_loop(0, (n_live + NARROW - 1) // NARROW, split_step, 0)

    n_full, n_live = counts[0], counts[1]
    total = GROUP * tok
    if first:
        m_s[...] = jnp.full(m_s.shape, FLOOR, jnp.float32)
        acc_s[...] = jnp.zeros(acc_s.shape, jnp.float32)
    else:
        acc_s[...] = carried[0][0]
        m_s[...] = carried[1][0]

    if block is None:
        t_rel, b = step // 2, step % 2
    else:
        t_rel, b = step, block
    line = lax.broadcasted_iota(jnp.int32, (tok, PAGE_TOK), 0)
    p = line // tok_rows
    kx = place_of(p)
    token = ((kx ^ head) * ways + (t_rel ^ way)) * tok_rows + line % tok_rows
    q_at = token + jnp.where(b == 0, place[2], place[3])

    def tile_step(at, size, masked):
        span_k = pl.ds(pl.multiple_of(at * PAGE_TOK, PAGE_TOK), size * PAGE_TOK)
        keys = k_s[span_k, :]
        values = v_s[span_k, :]
        if masked:
            lane = lax.broadcasted_iota(jnp.int32, (tok, PAGE_TOK), 1)
            visible = []
            for s in range(size):
                slot = order[jnp.minimum(at + s, n_live - 1)]
                start = jnp.where(at + s < n_live, pages[slot] * PAGE_TOK, FAR)
                seen = lane + start <= q_at
                visible.append(jnp.concatenate([seen] * (rows // tok), axis=0))

        def score(part):
            return lax.dot_general(
                q_ref[0, part * rows : (part + 1) * rows, :],
                keys,
                (((1,), (1,)), ((), ())),
                preferred_element_type=jnp.float32,
            )

        def soften(part, scores):
            span = slice(part * rows, (part + 1) * rows)
            pieces = [scores[:, s * PAGE_TOK : (s + 1) * PAGE_TOK] for s in range(size)]
            if masked:
                pieces = [jnp.where(v, x, FLOOR) for v, x in zip(visible, pieces)]
            peak = functools.reduce(jnp.maximum, pieces)
            m_old = m_s[span, :]
            m_new = jnp.maximum(m_old, jnp.max(peak, axis=1, keepdims=True) * SCALE)
            shift = jnp.maximum(m_new, 0.5 * FLOOR * SCALE) if masked else m_new
            weights = jnp.concatenate(
                [jnp.exp2(x * SCALE - shift).astype(jnp.bfloat16) for x in pieces], axis=1
            )
            m_s[span, :] = m_new
            return weights, jnp.exp2(m_old - m_new)

        def gather(part, weights, alpha):
            span = slice(part * rows, (part + 1) * rows)
            mixed = jnp.dot(weights, values, preferred_element_type=jnp.float32)
            acc_s[span, :HEAD_DIM] = acc_s[span, :HEAD_DIM] * alpha + mixed[:, :HEAD_DIM]
            acc_s[span, HEAD_DIM:] = acc_s[span, HEAD_DIM:] * alpha + mixed[:, HEAD_DIM:]

        parts = total // rows
        scores = score(0)
        waiting = None
        for part in range(parts):
            following = score(part + 1) if part + 1 < parts else None
            weights, alpha = soften(part, scores)
            if waiting is not None:
                gather(*waiting)
            waiting = (part, weights, alpha)
            scores = following
        gather(*waiting)

    n_wide = n_full // WIDE
    n_open = (n_full - n_wide * WIDE) // NARROW
    base = n_wide * WIDE
    done = base + n_open * NARROW
    n_masked = (n_live - done + NARROW - 1) // NARROW

    def wide(i, carry):
        tile_step(i * WIDE, WIDE, False)
        return carry

    def narrow(i, carry):
        tile_step(base + i * NARROW, NARROW, False)
        return carry

    def masked(i, carry):
        tile_step(done + i * NARROW, NARROW, True)
        return carry

    lax.fori_loop(0, n_wide, wide, 0)
    lax.fori_loop(0, n_open, narrow, 0)
    lax.fori_loop(0, n_masked, masked, 0)

    if last:
        row = lax.broadcasted_iota(jnp.int32, (tok, HEAD_DIM), 0)
        col = lax.broadcasted_iota(jnp.int32, (tok, HEAD_DIM), 1)
        eye = row == col
        lines = []
        for ref, lanes in ((m_s, slice(0, HEAD_DIM)), (acc_s, slice(HEAD_DIM, 2 * HEAD_DIM))):
            for g in range(GROUP):
                span = slice(g * tok, (g + 1) * tok)
                lines.append(
                    jnp.sum(jnp.where(eye, ref[span, lanes], 0.0), axis=0, keepdims=True)
                )
        stats = jnp.concatenate(lines, axis=0)
        for w in range(ways):

            @pl.when(step == w)
            def _():
                outs[w][:total, :] = acc_s[:, :HEAD_DIM].astype(jnp.bfloat16)
                for i, piece in enumerate(three_parts(stats)):
                    at = total + i * 2 * GROUP
                    outs[w][at : at + 2 * GROUP, :] = piece


def attend(place, x, first_slot, q, carried, block, tok_rows, rows):
    sources = x.shape[0]
    src_slots = x.shape[1] // (2 * PAGE_TOK)
    steps, total, _ = q.shape
    tok = total // GROUP
    first = carried is None
    last = block is not None
    ways = steps // 2
    n_slots = -(-sources * src_slots // WIDE) * WIDE
    if last:
        grid = ways
        at = lambda i, *_: (2 * i + block, 0, 0)
    else:
        grid = steps
        at = lambda i, *_: (i, 0, 0)
    in_specs = [
        pl.BlockSpec(x.shape, lambda i, *_: (0, 0, 0)),
        pl.BlockSpec((1, total, HEAD_DIM), at),
    ]
    sent = total + 3 * 2 * GROUP
    if last:
        out_shape = (jax.ShapeDtypeStruct((sent, HEAD_DIM), jnp.bfloat16),) * ways
        out_specs = (pl.BlockSpec((sent, HEAD_DIM), lambda i, *_: (0, 0)),) * ways
    else:
        out_shape = (
            jax.ShapeDtypeStruct((steps, total, 2 * HEAD_DIM), jnp.float32),
            jax.ShapeDtypeStruct((steps, total, HEAD_DIM), jnp.float32),
        )
        out_specs = (
            pl.BlockSpec((1, total, 2 * HEAD_DIM), at),
            pl.BlockSpec((1, total, HEAD_DIM), at),
        )
    extra = ()
    sums = ()
    if last:
        sums = (
            pltpu.VMEM((total, 2 * HEAD_DIM), jnp.float32),
            pltpu.VMEM((total, HEAD_DIM), jnp.float32),
        )
    if not first:
        extra = tuple(carried)
        in_specs += [
            pl.BlockSpec((1, total, 2 * HEAD_DIM), at),
            pl.BlockSpec((1, total, HEAD_DIM), at),
        ]
    flops = 8 * grid * total * sources * src_slots * PAGE_TOK * HEAD_DIM
    return pl.pallas_call(
        functools.partial(
            attend_kernel,
            first_slot=first_slot,
            first=first,
            last=last,
            rows=rows,
            tok=tok,
            ways=ways,
            tok_rows=tok_rows,
            block=block,
        ),
        out_shape=out_shape,
        grid_spec=pltpu.PrefetchScalarGridSpec(
            num_scalar_prefetch=1,
            grid=(grid,),
            in_specs=in_specs,
            out_specs=out_specs,
            scratch_shapes=[
                pltpu.VMEM((n_slots * PAGE_TOK, HEAD_DIM), jnp.bfloat16),
                pltpu.VMEM((n_slots * PAGE_TOK, 2 * HEAD_DIM), jnp.bfloat16),
                *sums,
                pltpu.VMEM((sources, HEAD_DIM), jnp.int32),
                pltpu.SMEM((n_slots + 1,), jnp.int32),
                pltpu.SMEM((n_slots + 1,), jnp.int32),
                pltpu.SMEM((n_slots,), jnp.int32),
                pltpu.SMEM((sources, HEAD_DIM), jnp.int32),
                pltpu.SMEM((2,), jnp.int32),
                pltpu.SemaphoreType.DMA(()),
            ],
        ),
        cost_estimate=pl.CostEstimate(
            flops=flops, transcendentals=flops // (8 * HEAD_DIM), bytes_accessed=x.size * 2
        ),
        name="attend_last" if last else "attend_first",
    )(place, x, q, *extra)


def merge(parts, a_ref, tok):
    total = GROUP * tok
    row = lax.broadcasted_iota(jnp.int32, (tok, HEAD_DIM), 0)
    col = lax.broadcasted_iota(jnp.int32, (tok, HEAD_DIM), 1)
    eye = row == col
    stats = []
    for part in parts:
        pieces = [
            part[total + i * 2 * GROUP : total + (i + 1) * 2 * GROUP, :].astype(jnp.float32)
            for i in range(3)
        ]
        stats.append((pieces[0] + pieces[1]) + pieces[2])
    tops = functools.reduce(jnp.maximum, [s[:GROUP] for s in stats])
    factors = [jnp.exp2(s[:GROUP] - tops) for s in stats]
    totals = sum(f * s[GROUP:] for f, s in zip(factors, stats))
    for g in range(GROUP):
        span = slice(g * tok, (g + 1) * tok)
        mixed = 0.0
        for f, part in zip(factors, parts):
            ratio = jnp.where(eye, f[g : g + 1] / totals[g : g + 1], 0.0)
            mixed += jnp.sum(ratio, axis=1, keepdims=True) * part[span, :].astype(jnp.float32)
        a_ref[:, g * HEAD_DIM : (g + 1) * HEAD_DIM] = mixed.astype(jnp.bfloat16)


def project_kernel(*refs, n_parts, n_ws, tok, y_first):
    parts = refs[:n_parts]
    ws = refs[n_parts : n_parts + n_ws]
    outs = refs[n_parts + n_ws :]
    keep_ref, send_ref = outs[:2]
    if n_parts == n_ws:
        a_ref = outs[2]

        @pl.when(pl.program_id(0) == 0)
        def _():
            merge(parts, a_ref, tok)

    else:
        a_ref = parts[0]
    depth = a_ref.shape[1] // n_ws
    total = 0.0
    for s in range(n_ws):
        total += jnp.dot(
            a_ref[:, s * depth : (s + 1) * depth], ws[s][...], preferred_element_type=jnp.float32
        )
    if y_first:
        keep, send = total[: tok // 2], total[tok // 2 :]
    else:
        quarters = [total[i * tok // 4 : (i + 1) * tok // 4] for i in range(4)]
        keep = jnp.concatenate(quarters[0::2], axis=0)
        send = jnp.concatenate(quarters[1::2], axis=0)
    keep_ref[...] = keep
    send_ref[...] = send.astype(jnp.bfloat16)


def project(parts, ws, tok, column_part, y_first, width=2048):
    columns = ws[0].shape[1] // COLUMN_PARTS
    steps = columns // width
    fixed = lambda i: (0, 0)
    half = tok // 2
    depth = sum(w.shape[0] for w in ws)
    merging = len(parts) == len(ws)
    out_shape = [
        jax.ShapeDtypeStruct((half, columns), jnp.float32),
        jax.ShapeDtypeStruct((half, columns), jnp.bfloat16),
    ]
    out_specs = [
        pl.BlockSpec((half, width), lambda i: (0, i)),
        pl.BlockSpec((half, width), lambda i: (0, i)),
    ]
    if merging:
        out_shape.append(jax.ShapeDtypeStruct((tok, depth), jnp.bfloat16))
        out_specs.append(pl.BlockSpec((tok, depth), fixed))
    return pl.pallas_call(
        functools.partial(
            project_kernel, n_parts=len(parts), n_ws=len(ws), tok=tok, y_first=y_first
        ),
        out_shape=out_shape,
        grid=(steps,),
        in_specs=[pl.BlockSpec(o.shape, fixed) for o in parts]
        + [
            pl.BlockSpec((w.shape[0], width), lambda i: (0, column_part * steps + i)) for w in ws
        ],
        out_specs=out_specs,
        cost_estimate=pl.CostEstimate(
            flops=2 * tok * depth * columns, transcendentals=0, bytes_accessed=2 * depth * columns
        ),
        name="project",
    )(*parts, *ws)


def local(
    queries, kv_cache, w_out, slot_page_before, slot_page_after, move_out, move_in, positions
):
    n = lax.axis_size("pages")
    slots = kv_cache.shape[0]
    ways = n // KV_HEADS
    tok_rows = BLOCK // n
    tok = BLOCK // ways
    me = lax.axis_index("pages")
    way = me // KV_HEADS
    head = head_of(me % KV_HEADS)
    groups = [[a * KV_HEADS + b for b in range(KV_HEADS)] for a in range(ways)]

    def exchange(x):
        return lax.all_to_all(x, "pages", 0, 0, axis_index_groups=groups, tiled=True)

    ids = jnp.broadcast_to(slot_page_before[:, None, None], (slots, 2, HEAD_DIM))
    ids = ids.astype(kv_cache.dtype)
    cuts = [(0, FIRST_SLOTS), (FIRST_SLOTS, slots - FIRST_SLOTS)]
    arrived = []
    for at, count in cuts:
        piece = split_heads(kv_cache, ids, at, count)
        got = exchange(piece)
        arrived.append(got.reshape(KV_HEADS, -1, HEAD_DIM))
    place = jnp.stack([head, way, positions[0, 0], positions[1, 0]]).astype(jnp.int32)
    q = query_rows(queries, place, ways, tok_rows)

    leaving = outgoing_pages(kv_cache, move_out[0])
    landed = []
    for o in range(1, MOVE_WIN + 1):
        landed.append(permute_to(leaving[o - 1], n, lambda i: (i + o) % n))

    ws = [w_out]
    for s in range(1, ways):
        ws.append(permute_to(w_out, n, lambda i: i ^ s))

    rows = 2 * tok
    carried = attend(place, arrived[0], 0, q, None, None, tok_rows, rows)

    def merger(i, s):
        return head_of(i % KV_HEADS) * ways + ((i // KV_HEADS) ^ s)

    partial = []
    for b in range(2):
        out = attend(place, arrived[1], FIRST_SLOTS, q, carried, b, tok_rows, rows)
        parts = []
        for s in range(ways):
            parts.append(permute_to(out[s], n, lambda i: merger(i, s)))
        partial.append(parts)

    sums = []
    for b in range(2):
        merged = partial[b]
        for c in range(COLUMN_PARTS):
            y_first = (b, c) != (0, 1)
            keep, send, *a = project(merged, ws, tok, c, y_first)
            if a:
                merged = a
            turns = (1, 2, 4) if y_first else (2, 1, 4)
            got = permute_to(send, n, lambda i: i ^ (turns[0] * ways))
            sums.append((keep, got, turns))
    cache_after = arrange_pages(kv_cache, landed, slot_page_after, move_in[0], send)

    results = []
    for keep, got, turns in sums:
        for turn in turns[1:]:
            total = keep + got.astype(jnp.float32)
            half = total.shape[0] // 2
            keep = total[:half]
            got = permute_to(
                total[half:].astype(jnp.bfloat16), n, lambda i: i ^ (turn * ways)
            )
        results.append((keep + got.astype(jnp.float32)).astype(jnp.bfloat16))
    out = jnp.stack(
        [
            jnp.concatenate(results[b * COLUMN_PARTS : (b + 1) * COLUMN_PARTS], axis=1)
            for b in range(2)
        ]
    )
    return (out, cache_after)


def solution(mesh):
    in_specs = (
        P(None, "groups", None),
        P(("groups", "pages"), None, None, None),
        P("pages", None),
        P(("groups", "pages")),
        P(("groups", "pages")),
        P(("groups", "pages"), None),
        P(("groups", "pages"), None),
        P(None, "groups"),
    )
    out_specs = (P(None, ("groups", "pages"), None), P(("groups", "pages"), None, None, None))
    return jax.shard_map(local, mesh=mesh, in_specs=in_specs, out_specs=out_specs, check_vma=False)
```

```python
import functools

import jax
import jax.numpy as jnp
from jax import lax
from jax.experimental import pallas as pl
from jax.experimental.pallas import tpu as pltpu
from jax.sharding import PartitionSpec as P

HEADS = 64
KV_HEADS = 8
HEAD_DIM = 128
PAGE_TOK = 128
BLOCK = 256
MOVE_WIN = 4
GROUP = HEADS // KV_HEADS

FLOOR = -1e30
FAR = 1 << 30
SCALE = HEAD_DIM**-0.5 * 1.4426950408889634

WIDE = 16
NARROW = 8
FIRST_SLOTS = 5
COLUMN_PARTS = 2

ANY = pl.BlockSpec(memory_space=pl.ANY)


def permute_to(x, n, target):
    return lax.ppermute(x, "pages", [(i, target(i)) for i in range(n)])


def head_of(j):
    half = KV_HEADS // 2
    return (j % 2) * half + j // 2


def place_of(p):
    return (p % 2) * 4 + (p // 2 % 2) * 2 + p // 4


def split_heads_kernel(kv_ref, ids_ref, out_ref, buf, in_sems, out_sems, *, first, count):
    extra = ids_ref.shape[0]
    loads = []
    for d in range(KV_HEADS):
        lanes = pl.ds(head_of(d) * HEAD_DIM, HEAD_DIM)
        row = [
            pltpu.make_async_copy(
                kv_ref.at[first + i, :, :, lanes],
                buf.at[d, pl.ds(i * PAGE_TOK, PAGE_TOK)],
                in_sems.at[d, i],
            )
            for i in range(count)
        ]
        row.append(
            pltpu.make_async_copy(
                ids_ref, buf.at[d, pl.ds(count * PAGE_TOK, extra)], in_sems.at[d, count]
            )
        )
        loads.append(row)
    stores = [
        pltpu.make_async_copy(buf.at[d], out_ref.at[d], out_sems.at[d])
        for d in range(KV_HEADS)
    ]
    for row in loads:
        for load in row:
            load.start()
    for row, store in zip(loads, stores):
        for load in row:
            load.wait()
        store.start()
    for store in stores:
        store.wait()


def split_heads(kv_cache, ids, first, count):
    shape = (KV_HEADS, count * PAGE_TOK + ids.shape[0], 2, HEAD_DIM)
    return pl.pallas_call(
        functools.partial(split_heads_kernel, first=first, count=count),
        out_shape=jax.ShapeDtypeStruct(shape, kv_cache.dtype),
        in_specs=[ANY, ANY],
        out_specs=ANY,
        scratch_shapes=[
            pltpu.VMEM(shape, kv_cache.dtype),
            pltpu.SemaphoreType.DMA((KV_HEADS, count + 1)),
            pltpu.SemaphoreType.DMA((KV_HEADS,)),
        ],
        name="split_heads",
    )(kv_cache, ids)


def outgoing_kernel(move_out, kv_ref, *refs):
    outs = refs[:MOVE_WIN]
    buf, in_sems, out_sems = refs[MOVE_WIN:]
    loads = [
        pltpu.make_async_copy(
            kv_ref.at[jnp.maximum(move_out[o], 0)], buf.at[o], in_sems.at[o]
        )
        for o in range(MOVE_WIN)
    ]
    stores = [
        pltpu.make_async_copy(buf.at[o], outs[o], out_sems.at[o]) for o in range(MOVE_WIN)
    ]
    for load in loads:
        load.start()
    for load, store in zip(loads, stores):
        load.wait()
        store.start()
    for store in stores:
        store.wait()


def outgoing_pages(kv_cache, move_out):
    page = jax.ShapeDtypeStruct(kv_cache.shape[1:], kv_cache.dtype)
    return pl.pallas_call(
        outgoing_kernel,
        out_shape=(page,) * MOVE_WIN,
        grid_spec=pltpu.PrefetchScalarGridSpec(
            num_scalar_prefetch=1,
            grid=(),
            in_specs=[ANY],
            out_specs=(ANY,) * MOVE_WIN,
            scratch_shapes=[
                pltpu.VMEM((MOVE_WIN,) + kv_cache.shape[1:], kv_cache.dtype),
                pltpu.SemaphoreType.DMA((MOVE_WIN,)),
                pltpu.SemaphoreType.DMA((MOVE_WIN,)),
            ],
        ),
        name="outgoing_pages",
    )(move_out, kv_cache)


def arrange_kernel(page_after, move_in, kv_ref, *refs):
    arrived = refs[:MOVE_WIN]
    _, out_ref, buf, zero_ref, in_sems, out_sems = refs[MOVE_WIN:]
    slots = out_ref.shape[0]
    filled = []
    for s in range(slots):
        taken = jnp.zeros((), jnp.bool_)
        for o in reversed(range(MOVE_WIN)):
            lands = move_in[o] == s

            @pl.when(lands & jnp.logical_not(taken))
            def _():
                pltpu.make_async_copy(arrived[o], buf.at[s], in_sems.at[s]).start()

            taken = taken | lands
        kept = page_after[s] >= 0

        @pl.when(kept & jnp.logical_not(taken))
        def _():
            pltpu.make_async_copy(kv_ref.at[s], buf.at[s], in_sems.at[s]).start()

        filled.append(kept | taken)
    zero_ref[...] = jnp.zeros(zero_ref.shape, zero_ref.dtype)
    for s in range(slots):

        @pl.when(filled[s])
        def _():
            pltpu.make_async_copy(kv_ref.at[s], buf.at[s], in_sems.at[s]).wait()
            pltpu.make_async_copy(buf.at[s], out_ref.at[s], out_sems.at[s]).start()

        @pl.when(jnp.logical_not(filled[s]))
        def _():
            pltpu.make_async_copy(zero_ref, out_ref.at[s], out_sems.at[s]).start()

    for s in range(slots):
        pltpu.make_async_copy(zero_ref, out_ref.at[s], out_sems.at[s]).wait()


def arrange_pages(kv_cache, arrived, page_after, move_in, after):
    slots = kv_cache.shape[0]
    return pl.pallas_call(
        arrange_kernel,
        out_shape=jax.ShapeDtypeStruct(kv_cache.shape, kv_cache.dtype),
        grid_spec=pltpu.PrefetchScalarGridSpec(
            num_scalar_prefetch=2,
            grid=(),
            in_specs=[ANY] * (2 + MOVE_WIN),
            out_specs=ANY,
            scratch_shapes=[
                pltpu.VMEM(kv_cache.shape, kv_cache.dtype),
                pltpu.VMEM(kv_cache.shape[1:], kv_cache.dtype),
                pltpu.SemaphoreType.DMA((slots,)),
                pltpu.SemaphoreType.DMA((slots,)),
            ],
        ),
        name="arrange_pages",
    )(page_after, move_in, kv_cache, *arrived, after)


def rows_kernel(place, q_ref, out_ref, *, ways, tok_rows):
    tok = out_ref.shape[1] // GROUP
    gp = GROUP // ways
    head = place[0]
    t_rel = pl.program_id(0) // 2
    t = place[1] ^ t_rel
    for p in range(KV_HEADS):
        kx = place_of(p)
        at = pl.multiple_of(((kx ^ head) * ways + t) * tok_rows, tok_rows)
        for gx in range(GROUP):
            g = ((gx // gp) ^ t) * gp + gx % gp
            lanes = pl.ds(pl.multiple_of(g * HEAD_DIM, HEAD_DIM), HEAD_DIM)
            to = gx * tok + p * tok_rows
            out_ref[0, to : to + tok_rows, :] = q_ref[0, pl.ds(at, tok_rows), lanes]


def query_rows(queries, place, ways, tok_rows):
    width = GROUP * HEAD_DIM
    tok = KV_HEADS * tok_rows
    dtype = queries.dtype
    if tok_rows % 16:
        queries = lax.dynamic_slice_in_dim(queries, place[0] * width, width, axis=2)
        queries = queries.astype(jnp.float32)
        column = lambda i, place: (i % 2, 0, 0)
    else:
        column = lambda i, place: (i % 2, 0, place[0])
    return pl.pallas_call(
        functools.partial(rows_kernel, ways=ways, tok_rows=tok_rows),
        out_shape=jax.ShapeDtypeStruct((2 * ways, GROUP * tok, HEAD_DIM), queries.dtype),
        grid_spec=pltpu.PrefetchScalarGridSpec(
            num_scalar_prefetch=1,
            grid=(2 * ways,),
            in_specs=[pl.BlockSpec((1, queries.shape[1], width), column)],
            out_specs=pl.BlockSpec((1, GROUP * tok, HEAD_DIM), lambda i, place: (i, 0, 0)),
        ),
        name="query_rows",
    )(place, queries).astype(dtype)


def three_parts(x):
    high = x.astype(jnp.bfloat16)
    rest = x - high.astype(jnp.float32)
    mid = rest.astype(jnp.bfloat16)
    low = (rest - mid.astype(jnp.float32)).astype(jnp.bfloat16)
    return high, mid, low


def attend_kernel(
    place, x_ref, q_ref, *refs, first_slot, first, last, rows, tok, ways, tok_rows, block
):
    n_in = 0 if first else 2
    carried = refs[:n_in]
    outs = refs[n_in : n_in + (ways if last else 2)]
    k_s, v_s, *sums, ids_s, order, rest, pages, ids, counts, sem = refs[n_in + len(outs) :]
    if last:
        acc_s, m_s = sums
    else:
        acc_s, m_s = outs[0].at[0], outs[1].at[0]
    step = pl.program_id(0)
    sources = x_ref.shape[0]
    src_slots = x_ref.shape[1] // (2 * PAGE_TOK)
    n_slots = sources * src_slots
    head, way = place[0], place[1]

    @pl.when(step == 0)
    def _():
        end = src_slots * 2 * PAGE_TOK
        extra = x_ref.shape[1] - end
        row = lax.broadcasted_iota(jnp.int32, (extra, HEAD_DIM), 0)
        col = lax.broadcasted_iota(jnp.int32, (extra, HEAD_DIM), 1)
        for src in range(sources):
            tail = x_ref[src, end : end + extra, :].astype(jnp.float32)
            line = jnp.sum(jnp.where(row == 2 * col, tail, 0.0), axis=0, keepdims=True)
            ids_s[src : src + 1, :] = line.astype(jnp.int32)
        copy = pltpu.make_async_copy(ids_s, ids, sem)
        copy.start()
        copy.wait()
        lowest = jnp.minimum(place[2], place[3])

        def fully(page):
            return (page >= 0) & (page * PAGE_TOK + (PAGE_TOK - 1) <= lowest)

        n_full = jnp.int32(0)
        n_rest = jnp.int32(0)
        for i in range(n_slots):
            page = ids[i // src_slots, first_slot + i % src_slots]
            pages[i] = page
            yes = fully(page)
            order[n_full] = i
            rest[n_rest] = i
            n_full += yes.astype(jnp.int32)
            n_rest += ((page >= 0) & jnp.logical_not(yes)).astype(jnp.int32)

        def append(i, carry):
            order[n_full + i] = rest[i]
            return carry

        lax.fori_loop(0, n_rest, append, 0)
        n_live = n_full + n_rest
        counts[0] = n_full
        counts[1] = n_live

        row = lax.broadcasted_iota(jnp.int32, (2 * PAGE_TOK, 2 * PAGE_TOK), 0)
        col = lax.broadcasted_iota(jnp.int32, (2 * PAGE_TOK, 2 * PAGE_TOK), 1)
        want = jnp.where(row < PAGE_TOK, 2 * row, 2 * (row - PAGE_TOK) + 1)
        pick = jnp.where(col == want, 1.0, 0.0).astype(jnp.bfloat16)
        ones = jnp.ones((PAGE_TOK, HEAD_DIM), jnp.bfloat16)

        def split_step(i, carry):
            for s in range(NARROW):
                at = i * NARROW + s
                slot = order[jnp.minimum(at, n_live - 1)]
                both = jnp.dot(
                    pick,
                    x_ref[
                        slot // src_slots,
                        pl.ds(
                            pl.multiple_of(slot % src_slots * 2 * PAGE_TOK, 2 * PAGE_TOK),
                            2 * PAGE_TOK,
                        ),
                        :,
                    ],
                    preferred_element_type=jnp.float32,
                ).astype(jnp.bfloat16)
                to = pl.ds(pl.multiple_of(at * PAGE_TOK, PAGE_TOK), PAGE_TOK)
                k_s[to, :] = both[:PAGE_TOK]
                v_s[to, :HEAD_DIM] = both[PAGE_TOK:]
                v_s[to, HEAD_DIM:] = ones
            return carry

        lax.fori_loop(0, (n_live + NARROW - 1) // NARROW, split_step, 0)

    n_full, n_live = counts[0], counts[1]
    total = GROUP * tok
    if first:
        m_s[...] = jnp.full(m_s.shape, FLOOR, jnp.float32)
        acc_s[...] = jnp.zeros(acc_s.shape, jnp.float32)
    else:
        acc_s[...] = carried[0][0]
        m_s[...] = carried[1][0]

    if block is None:
        t_rel, b = step // 2, step % 2
    else:
        t_rel, b = step, block
    line = lax.broadcasted_iota(jnp.int32, (tok, PAGE_TOK), 0)
    p = line // tok_rows
    kx = place_of(p)
    token = ((kx ^ head) * ways + (t_rel ^ way)) * tok_rows + line % tok_rows
    q_at = token + jnp.where(b == 0, place[2], place[3])

    def tile_step(at, size, masked):
        span_k = pl.ds(pl.multiple_of(at * PAGE_TOK, PAGE_TOK), size * PAGE_TOK)
        keys = k_s[span_k, :]
        values = v_s[span_k, :]
        if masked:
            lane = lax.broadcasted_iota(jnp.int32, (tok, PAGE_TOK), 1)
            visible = []
            for s in range(size):
                slot = order[jnp.minimum(at + s, n_live - 1)]
                start = jnp.where(at + s < n_live, pages[slot] * PAGE_TOK, FAR)
                seen = lane + start <= q_at
                visible.append(jnp.concatenate([seen] * (rows // tok), axis=0))

        def score(part):
            return lax.dot_general(
                q_ref[0, part * rows : (part + 1) * rows, :],
                keys,
                (((1,), (1,)), ((), ())),
                preferred_element_type=jnp.float32,
            )

        def soften(part, scores):
            span = slice(part * rows, (part + 1) * rows)
            pieces = [scores[:, s * PAGE_TOK : (s + 1) * PAGE_TOK] for s in range(size)]
            if masked:
                pieces = [jnp.where(v, x, FLOOR) for v, x in zip(visible, pieces)]
            peak = functools.reduce(jnp.maximum, pieces)
            m_old = m_s[span, :]
            m_new = jnp.maximum(m_old, jnp.max(peak, axis=1, keepdims=True) * SCALE)
            shift = jnp.maximum(m_new, 0.5 * FLOOR * SCALE) if masked else m_new
            weights = jnp.concatenate(
                [jnp.exp2(x * SCALE - shift).astype(jnp.bfloat16) for x in pieces], axis=1
            )
            m_s[span, :] = m_new
            return weights, jnp.exp2(m_old - m_new)

        def gather(part, weights, alpha):
            span = slice(part * rows, (part + 1) * rows)
            mixed = jnp.dot(weights, values, preferred_element_type=jnp.float32)
            acc_s[span, :HEAD_DIM] = acc_s[span, :HEAD_DIM] * alpha + mixed[:, :HEAD_DIM]
            acc_s[span, HEAD_DIM:] = acc_s[span, HEAD_DIM:] * alpha + mixed[:, HEAD_DIM:]

        parts = total // rows
        scores = score(0)
        waiting = None
        for part in range(parts):
            following = score(part + 1) if part + 1 < parts else None
            weights, alpha = soften(part, scores)
            if waiting is not None:
                gather(*waiting)
            waiting = (part, weights, alpha)
            scores = following
        gather(*waiting)

    n_wide = n_full // WIDE
    n_open = (n_full - n_wide * WIDE) // NARROW
    base = n_wide * WIDE
    done = base + n_open * NARROW
    n_masked = (n_live - done + NARROW - 1) // NARROW

    def wide(i, carry):
        tile_step(i * WIDE, WIDE, False)
        return carry

    def narrow(i, carry):
        tile_step(base + i * NARROW, NARROW, False)
        return carry

    def masked(i, carry):
        tile_step(done + i * NARROW, NARROW, True)
        return carry

    lax.fori_loop(0, n_wide, wide, 0)
    lax.fori_loop(0, n_open, narrow, 0)
    lax.fori_loop(0, n_masked, masked, 0)

    if last:
        row = lax.broadcasted_iota(jnp.int32, (tok, HEAD_DIM), 0)
        col = lax.broadcasted_iota(jnp.int32, (tok, HEAD_DIM), 1)
        eye = row == col
        lines = []
        for ref, lanes in ((m_s, slice(0, HEAD_DIM)), (acc_s, slice(HEAD_DIM, 2 * HEAD_DIM))):
            for g in range(GROUP):
                span = slice(g * tok, (g + 1) * tok)
                lines.append(
                    jnp.sum(jnp.where(eye, ref[span, lanes], 0.0), axis=0, keepdims=True)
                )
        stats = jnp.concatenate(lines, axis=0)
        for w in range(ways):

            @pl.when(step == w)
            def _():
                outs[w][:total, :] = acc_s[:, :HEAD_DIM].astype(jnp.bfloat16)
                for i, piece in enumerate(three_parts(stats)):
                    at = total + i * 2 * GROUP
                    outs[w][at : at + 2 * GROUP, :] = piece


def attend(place, x, first_slot, q, carried, block, tok_rows, rows):
    sources = x.shape[0]
    src_slots = x.shape[1] // (2 * PAGE_TOK)
    steps, total, _ = q.shape
    tok = total // GROUP
    first = carried is None
    last = block is not None
    ways = steps // 2
    n_slots = -(-sources * src_slots // WIDE) * WIDE
    if last:
        grid = ways
        at = lambda i, *_: (2 * i + block, 0, 0)
    else:
        grid = steps
        at = lambda i, *_: (i, 0, 0)
    in_specs = [
        pl.BlockSpec(x.shape, lambda i, *_: (0, 0, 0)),
        pl.BlockSpec((1, total, HEAD_DIM), at),
    ]
    sent = total + 3 * 2 * GROUP
    if last:
        out_shape = (jax.ShapeDtypeStruct((sent, HEAD_DIM), jnp.bfloat16),) * ways
        out_specs = (pl.BlockSpec((sent, HEAD_DIM), lambda i, *_: (0, 0)),) * ways
    else:
        out_shape = (
            jax.ShapeDtypeStruct((steps, total, 2 * HEAD_DIM), jnp.float32),
            jax.ShapeDtypeStruct((steps, total, HEAD_DIM), jnp.float32),
        )
        out_specs = (
            pl.BlockSpec((1, total, 2 * HEAD_DIM), at),
            pl.BlockSpec((1, total, HEAD_DIM), at),
        )
    extra = ()
    sums = ()
    if last:
        sums = (
            pltpu.VMEM((total, 2 * HEAD_DIM), jnp.float32),
            pltpu.VMEM((total, HEAD_DIM), jnp.float32),
        )
    if not first:
        extra = tuple(carried)
        in_specs += [
            pl.BlockSpec((1, total, 2 * HEAD_DIM), at),
            pl.BlockSpec((1, total, HEAD_DIM), at),
        ]
    flops = 8 * grid * total * sources * src_slots * PAGE_TOK * HEAD_DIM
    return pl.pallas_call(
        functools.partial(
            attend_kernel,
            first_slot=first_slot,
            first=first,
            last=last,
            rows=rows,
            tok=tok,
            ways=ways,
            tok_rows=tok_rows,
            block=block,
        ),
        out_shape=out_shape,
        grid_spec=pltpu.PrefetchScalarGridSpec(
            num_scalar_prefetch=1,
            grid=(grid,),
            in_specs=in_specs,
            out_specs=out_specs,
            scratch_shapes=[
                pltpu.VMEM((n_slots * PAGE_TOK, HEAD_DIM), jnp.bfloat16),
                pltpu.VMEM((n_slots * PAGE_TOK, 2 * HEAD_DIM), jnp.bfloat16),
                *sums,
                pltpu.VMEM((sources, HEAD_DIM), jnp.int32),
                pltpu.SMEM((n_slots + 1,), jnp.int32),
                pltpu.SMEM((n_slots + 1,), jnp.int32),
                pltpu.SMEM((n_slots,), jnp.int32),
                pltpu.SMEM((sources, HEAD_DIM), jnp.int32),
                pltpu.SMEM((2,), jnp.int32),
                pltpu.SemaphoreType.DMA(()),
            ],
        ),
        cost_estimate=pl.CostEstimate(
            flops=flops, transcendentals=flops // (8 * HEAD_DIM), bytes_accessed=x.size * 2
        ),
        name="attend_last" if last else "attend_first",
    )(place, x, q, *extra)


def merge(parts, a_ref, tok):
    total = GROUP * tok
    row = lax.broadcasted_iota(jnp.int32, (tok, HEAD_DIM), 0)
    col = lax.broadcasted_iota(jnp.int32, (tok, HEAD_DIM), 1)
    eye = row == col
    stats = []
    for part in parts:
        pieces = [
            part[total + i * 2 * GROUP : total + (i + 1) * 2 * GROUP, :].astype(jnp.float32)
            for i in range(3)
        ]
        stats.append((pieces[0] + pieces[1]) + pieces[2])
    tops = functools.reduce(jnp.maximum, [s[:GROUP] for s in stats])
    factors = [jnp.exp2(s[:GROUP] - tops) for s in stats]
    totals = sum(f * s[GROUP:] for f, s in zip(factors, stats))
    for g in range(GROUP):
        span = slice(g * tok, (g + 1) * tok)
        mixed = 0.0
        for f, part in zip(factors, parts):
            ratio = jnp.where(eye, f[g : g + 1] / totals[g : g + 1], 0.0)
            mixed += jnp.sum(ratio, axis=1, keepdims=True) * part[span, :].astype(jnp.float32)
        a_ref[:, g * HEAD_DIM : (g + 1) * HEAD_DIM] = mixed.astype(jnp.bfloat16)


def project_kernel(*refs, n_parts, n_ws, tok, y_first):
    parts = refs[:n_parts]
    ws = refs[n_parts : n_parts + n_ws]
    outs = refs[n_parts + n_ws :]
    keep_ref, send_ref = outs[:2]
    if n_parts == n_ws:
        a_ref = outs[2]

        @pl.when(pl.program_id(0) == 0)
        def _():
            merge(parts, a_ref, tok)

    else:
        a_ref = parts[0]
    depth = a_ref.shape[1] // n_ws
    total = 0.0
    for s in range(n_ws):
        total += jnp.dot(
            a_ref[:, s * depth : (s + 1) * depth], ws[s][...], preferred_element_type=jnp.float32
        )
    if y_first:
        keep, send = total[: tok // 2], total[tok // 2 :]
    else:
        quarters = [total[i * tok // 4 : (i + 1) * tok // 4] for i in range(4)]
        keep = jnp.concatenate(quarters[0::2], axis=0)
        send = jnp.concatenate(quarters[1::2], axis=0)
    keep_ref[...] = keep
    send_ref[...] = send.astype(jnp.bfloat16)


def project(parts, ws, tok, column_part, y_first, width=2048):
    columns = ws[0].shape[1] // COLUMN_PARTS
    steps = columns // width
    fixed = lambda i: (0, 0)
    half = tok // 2
    depth = sum(w.shape[0] for w in ws)
    merging = len(parts) == len(ws)
    out_shape = [
        jax.ShapeDtypeStruct((half, columns), jnp.float32),
        jax.ShapeDtypeStruct((half, columns), jnp.bfloat16),
    ]
    out_specs = [
        pl.BlockSpec((half, width), lambda i: (0, i)),
        pl.BlockSpec((half, width), lambda i: (0, i)),
    ]
    if merging:
        out_shape.append(jax.ShapeDtypeStruct((tok, depth), jnp.bfloat16))
        out_specs.append(pl.BlockSpec((tok, depth), fixed))
    return pl.pallas_call(
        functools.partial(
            project_kernel, n_parts=len(parts), n_ws=len(ws), tok=tok, y_first=y_first
        ),
        out_shape=out_shape,
        grid=(steps,),
        in_specs=[pl.BlockSpec(o.shape, fixed) for o in parts]
        + [
            pl.BlockSpec((w.shape[0], width), lambda i: (0, column_part * steps + i)) for w in ws
        ],
        out_specs=out_specs,
        cost_estimate=pl.CostEstimate(
            flops=2 * tok * depth * columns, transcendentals=0, bytes_accessed=2 * depth * columns
        ),
        name="project",
    )(*parts, *ws)


def local(
    queries, kv_cache, w_out, slot_page_before, slot_page_after, move_out, move_in, positions
):
    n = lax.axis_size("pages")
    slots = kv_cache.shape[0]
    ways = n // KV_HEADS
    tok_rows = BLOCK // n
    tok = BLOCK // ways
    me = lax.axis_index("pages")
    way = me // KV_HEADS
    head = head_of(me % KV_HEADS)
    groups = [[a * KV_HEADS + b for b in range(KV_HEADS)] for a in range(ways)]

    def exchange(x):
        return lax.all_to_all(x, "pages", 0, 0, axis_index_groups=groups, tiled=True)

    ids = jnp.broadcast_to(slot_page_before[:, None, None], (slots, 2, HEAD_DIM))
    ids = ids.astype(kv_cache.dtype)
    cuts = [(0, FIRST_SLOTS), (FIRST_SLOTS, slots - FIRST_SLOTS)]
    arrived = []
    for at, count in cuts:
        piece = split_heads(kv_cache, ids, at, count)
        got = exchange(piece)
        arrived.append(got.reshape(KV_HEADS, -1, HEAD_DIM))
    place = jnp.stack([head, way, positions[0, 0], positions[1, 0]]).astype(jnp.int32)
    q = query_rows(queries, place, ways, tok_rows)

    leaving = outgoing_pages(kv_cache, move_out[0])
    landed = []
    for o in range(1, MOVE_WIN + 1):
        landed.append(permute_to(leaving[o - 1], n, lambda i: (i + o) % n))

    ws = [w_out]
    for s in range(1, ways):
        ws.append(permute_to(w_out, n, lambda i: i ^ s))

    rows = 2 * tok
    carried = attend(place, arrived[0], 0, q, None, None, tok_rows, rows)

    def merger(i, s):
        return head_of(i % KV_HEADS) * ways + ((i // KV_HEADS) ^ s)

    partial = []
    for b in range(2):
        out = attend(place, arrived[1], FIRST_SLOTS, q, carried, b, tok_rows, rows)
        parts = []
        for s in range(ways):
            parts.append(permute_to(out[s], n, lambda i: merger(i, s)))
        partial.append(parts)

    sums = []
    for b in range(2):
        merged = partial[b]
        for c in range(COLUMN_PARTS):
            y_first = (b, c) != (0, 1)
            keep, send, *a = project(merged, ws, tok, c, y_first)
            if a:
                merged = a
            turns = (1, 2, 4) if y_first else (2, 1, 4)
            got = permute_to(send, n, lambda i: i ^ (turns[0] * ways))
            sums.append((keep, got, turns))
    cache_after = arrange_pages(kv_cache, landed, slot_page_after, move_in[0], send)

    results = []
    for keep, got, turns in sums:
        for turn in turns[1:]:
            total = keep + got.astype(jnp.float32)
            half = total.shape[0] // 2
            keep = total[:half]
            send = total[half:].astype(jnp.bfloat16)
            got = permute_to(send, n, lambda i: i ^ (turn * ways))
        results.append((keep + got.astype(jnp.float32)).astype(jnp.bfloat16))
    out = jnp.stack(
        [
            jnp.concatenate(results[b * COLUMN_PARTS : (b + 1) * COLUMN_PARTS], axis=1)
            for b in range(2)
        ]
    )
    return (out, cache_after)


def solution(mesh):
    in_specs = (
        P(None, "groups", None),
        P(("groups", "pages"), None, None, None),
        P("pages", None),
        P(("groups", "pages")),
        P(("groups", "pages")),
        P(("groups", "pages"), None),
        P(("groups", "pages"), None),
        P(None, "groups"),
    )
    out_specs = (P(None, ("groups", "pages"), None), P(("groups", "pages"), None, None, None))
    return jax.shard_map(local, mesh=mesh, in_specs=in_specs, out_specs=out_specs, check_vma=False)
```

```python
import functools

import jax
import jax.numpy as jnp
from jax import lax
from jax.experimental import pallas as pl
from jax.experimental.pallas import tpu as pltpu
from jax.sharding import PartitionSpec as P

HEADS = 64
KV_HEADS = 8
HEAD_DIM = 128
PAGE_TOK = 128
BLOCK = 256
MOVE_WIN = 4
GROUP = HEADS // KV_HEADS

FLOOR = -1e30
FAR = 1 << 30
SCALE = HEAD_DIM**-0.5 * 1.4426950408889634

WIDE = 16
NARROW = 8
FIRST_SLOTS = 5
COLUMN_PARTS = 2

ANY = pl.BlockSpec(memory_space=pl.ANY)


def permute_to(x, n, target):
    return lax.ppermute(x, "pages", [(i, target(i)) for i in range(n)])


def head_of(j):
    half = KV_HEADS // 2
    return (j % 2) * half + j // 2


def place_of(p):
    return (p % 2) * 4 + (p // 2 % 2) * 2 + p // 4


def split_heads_kernel(pages, kv_ref, out_ref, buf, in_sems, out_sems, *, first, count):
    loads = []
    for d in range(KV_HEADS):
        lanes = pl.ds(head_of(d) * HEAD_DIM, HEAD_DIM)
        loads.append(
            [
                pltpu.make_async_copy(
                    kv_ref.at[first + i, :, :, lanes],
                    buf.at[d, pl.ds(i * PAGE_TOK, PAGE_TOK)],
                    in_sems.at[d, i],
                )
                for i in range(count)
            ]
        )
    stores = [
        pltpu.make_async_copy(buf.at[d], out_ref.at[d], out_sems.at[d])
        for d in range(KV_HEADS)
    ]
    for row in loads:
        for load in row:
            load.start()
    for t in range(kv_ref.shape[0]):
        line = jnp.full((2, HEAD_DIM), pages[t], jnp.int32)
        line = line.astype(jnp.float32).astype(buf.dtype)
        for d in range(KV_HEADS):
            buf[d, count * PAGE_TOK + t] = line
    for row, store in zip(loads, stores):
        for load in row:
            load.wait()
        store.start()
    for store in stores:
        store.wait()


def split_heads(kv_cache, pages, first, count):
    shape = (KV_HEADS, count * PAGE_TOK + kv_cache.shape[0], 2, HEAD_DIM)
    return pl.pallas_call(
        functools.partial(split_heads_kernel, first=first, count=count),
        out_shape=jax.ShapeDtypeStruct(shape, kv_cache.dtype),
        grid_spec=pltpu.PrefetchScalarGridSpec(
            num_scalar_prefetch=1,
            grid=(),
            in_specs=[ANY],
            out_specs=ANY,
            scratch_shapes=[
                pltpu.VMEM(shape, kv_cache.dtype),
                pltpu.SemaphoreType.DMA((KV_HEADS, count)),
                pltpu.SemaphoreType.DMA((KV_HEADS,)),
            ],
        ),
        name="split_heads",
    )(pages, kv_cache)


def outgoing_kernel(move_out, kv_ref, *refs):
    outs = refs[:MOVE_WIN]
    buf, in_sems, out_sems = refs[MOVE_WIN:]
    loads = [
        pltpu.make_async_copy(
            kv_ref.at[jnp.maximum(move_out[o], 0)], buf.at[o], in_sems.at[o]
        )
        for o in range(MOVE_WIN)
    ]
    stores = [
        pltpu.make_async_copy(buf.at[o], outs[o], out_sems.at[o]) for o in range(MOVE_WIN)
    ]
    for load in loads:
        load.start()
    for load, store in zip(loads, stores):
        load.wait()
        store.start()
    for store in stores:
        store.wait()


def outgoing_pages(kv_cache, move_out):
    page = jax.ShapeDtypeStruct(kv_cache.shape[1:], kv_cache.dtype)
    return pl.pallas_call(
        outgoing_kernel,
        out_shape=(page,) * MOVE_WIN,
        grid_spec=pltpu.PrefetchScalarGridSpec(
            num_scalar_prefetch=1,
            grid=(),
            in_specs=[ANY],
            out_specs=(ANY,) * MOVE_WIN,
            scratch_shapes=[
                pltpu.VMEM((MOVE_WIN,) + kv_cache.shape[1:], kv_cache.dtype),
                pltpu.SemaphoreType.DMA((MOVE_WIN,)),
                pltpu.SemaphoreType.DMA((MOVE_WIN,)),
            ],
        ),
        name="outgoing_pages",
    )(move_out, kv_cache)


def arrange_kernel(page_after, move_in, kv_ref, *refs):
    arrived = refs[:MOVE_WIN]
    _, out_ref, buf, zero_ref, in_sems, out_sems = refs[MOVE_WIN:]
    slots = out_ref.shape[0]
    filled = []
    for s in range(slots):
        taken = jnp.zeros((), jnp.bool_)
        for o in reversed(range(MOVE_WIN)):
            lands = move_in[o] == s

            @pl.when(lands & jnp.logical_not(taken))
            def _():
                pltpu.make_async_copy(arrived[o], buf.at[s], in_sems.at[s]).start()

            taken = taken | lands
        kept = page_after[s] >= 0

        @pl.when(kept & jnp.logical_not(taken))
        def _():
            pltpu.make_async_copy(kv_ref.at[s], buf.at[s], in_sems.at[s]).start()

        filled.append(kept | taken)
    zero_ref[...] = jnp.zeros(zero_ref.shape, zero_ref.dtype)
    for s in range(slots):

        @pl.when(filled[s])
        def _():
            pltpu.make_async_copy(kv_ref.at[s], buf.at[s], in_sems.at[s]).wait()
            pltpu.make_async_copy(buf.at[s], out_ref.at[s], out_sems.at[s]).start()

        @pl.when(jnp.logical_not(filled[s]))
        def _():
            pltpu.make_async_copy(zero_ref, out_ref.at[s], out_sems.at[s]).start()

    for s in range(slots):
        pltpu.make_async_copy(zero_ref, out_ref.at[s], out_sems.at[s]).wait()


def arrange_pages(kv_cache, arrived, page_after, move_in, after):
    slots = kv_cache.shape[0]
    return pl.pallas_call(
        arrange_kernel,
        out_shape=jax.ShapeDtypeStruct(kv_cache.shape, kv_cache.dtype),
        grid_spec=pltpu.PrefetchScalarGridSpec(
            num_scalar_prefetch=2,
            grid=(),
            in_specs=[ANY] * (2 + MOVE_WIN),
            out_specs=ANY,
            scratch_shapes=[
                pltpu.VMEM(kv_cache.shape, kv_cache.dtype),
                pltpu.VMEM(kv_cache.shape[1:], kv_cache.dtype),
                pltpu.SemaphoreType.DMA((slots,)),
                pltpu.SemaphoreType.DMA((slots,)),
            ],
        ),
        name="arrange_pages",
    )(page_after, move_in, kv_cache, *arrived, after)


def rows_kernel(place, q_ref, out_ref, *, ways, tok_rows):
    tok = out_ref.shape[1] // GROUP
    gp = GROUP // ways
    head = place[0]
    t_rel = pl.program_id(0) // 2
    t = place[1] ^ t_rel
    for p in range(KV_HEADS):
        kx = place_of(p)
        at = pl.multiple_of(((kx ^ head) * ways + t) * tok_rows, tok_rows)
        for gx in range(GROUP):
            g = ((gx // gp) ^ t) * gp + gx % gp
            lanes = pl.ds(pl.multiple_of(g * HEAD_DIM, HEAD_DIM), HEAD_DIM)
            to = gx * tok + p * tok_rows
            out_ref[0, to : to + tok_rows, :] = q_ref[0, pl.ds(at, tok_rows), lanes]


def query_rows(queries, place, ways, tok_rows):
    width = GROUP * HEAD_DIM
    tok = KV_HEADS * tok_rows
    dtype = queries.dtype
    if tok_rows % 16:
        queries = lax.dynamic_slice_in_dim(queries, place[0] * width, width, axis=2)
        queries = queries.astype(jnp.float32)
        column = lambda i, place: (i % 2, 0, 0)
    else:
        column = lambda i, place: (i % 2, 0, place[0])
    return pl.pallas_call(
        functools.partial(rows_kernel, ways=ways, tok_rows=tok_rows),
        out_shape=jax.ShapeDtypeStruct((2 * ways, GROUP * tok, HEAD_DIM), queries.dtype),
        grid_spec=pltpu.PrefetchScalarGridSpec(
            num_scalar_prefetch=1,
            grid=(2 * ways,),
            in_specs=[pl.BlockSpec((1, queries.shape[1], width), column)],
            out_specs=pl.BlockSpec((1, GROUP * tok, HEAD_DIM), lambda i, place: (i, 0, 0)),
        ),
        name="query_rows",
    )(place, queries).astype(dtype)


def three_parts(x):
    high = x.astype(jnp.bfloat16)
    rest = x - high.astype(jnp.float32)
    mid = rest.astype(jnp.bfloat16)
    low = (rest - mid.astype(jnp.float32)).astype(jnp.bfloat16)
    return high, mid, low


def attend_kernel(
    place, x_ref, q_ref, *refs, first_slot, first, last, rows, tok, ways, tok_rows, block
):
    n_in = 0 if first else 2
    carried = refs[:n_in]
    outs = refs[n_in : n_in + (ways if last else 2)]
    k_s, v_s, *sums, ids_s, order, rest, pages, ids, counts, sem = refs[n_in + len(outs) :]
    if last:
        acc_s, m_s = sums
    else:
        acc_s, m_s = outs[0].at[0], outs[1].at[0]
    step = pl.program_id(0)
    sources = x_ref.shape[0]
    src_slots = x_ref.shape[1] // (2 * PAGE_TOK)
    n_slots = sources * src_slots
    head, way = place[0], place[1]

    @pl.when(step == 0)
    def _():
        end = src_slots * 2 * PAGE_TOK
        extra = x_ref.shape[1] - end
        row = lax.broadcasted_iota(jnp.int32, (extra, HEAD_DIM), 0)
        col = lax.broadcasted_iota(jnp.int32, (extra, HEAD_DIM), 1)
        for src in range(sources):
            tail = x_ref[src, end : end + extra, :].astype(jnp.float32)
            line = jnp.sum(jnp.where(row == 2 * col, tail, 0.0), axis=0, keepdims=True)
            ids_s[src : src + 1, :] = line.astype(jnp.int32)
        copy = pltpu.make_async_copy(ids_s, ids, sem)
        copy.start()
        copy.wait()
        lowest = jnp.minimum(place[2], place[3])

        def fully(page):
            return (page >= 0) & (page * PAGE_TOK + (PAGE_TOK - 1) <= lowest)

        n_full = jnp.int32(0)
        n_rest = jnp.int32(0)
        for i in range(n_slots):
            page = ids[i // src_slots, first_slot + i % src_slots]
            pages[i] = page
            yes = fully(page)
            order[n_full] = i
            rest[n_rest] = i
            n_full += yes.astype(jnp.int32)
            n_rest += ((page >= 0) & jnp.logical_not(yes)).astype(jnp.int32)

        def append(i, carry):
            order[n_full + i] = rest[i]
            return carry

        lax.fori_loop(0, n_rest, append, 0)
        n_live = n_full + n_rest
        counts[0] = n_full
        counts[1] = n_live

        row = lax.broadcasted_iota(jnp.int32, (2 * PAGE_TOK, 2 * PAGE_TOK), 0)
        col = lax.broadcasted_iota(jnp.int32, (2 * PAGE_TOK, 2 * PAGE_TOK), 1)
        want = jnp.where(row < PAGE_TOK, 2 * row, 2 * (row - PAGE_TOK) + 1)
        pick = jnp.where(col == want, 1.0, 0.0).astype(jnp.bfloat16)
        ones = jnp.ones((PAGE_TOK, HEAD_DIM), jnp.bfloat16)

        def split_step(i, carry):
            for s in range(NARROW):
                at = i * NARROW + s
                slot = order[jnp.minimum(at, n_live - 1)]
                both = jnp.dot(
                    pick,
                    x_ref[
                        slot // src_slots,
                        pl.ds(
                            pl.multiple_of(slot % src_slots * 2 * PAGE_TOK, 2 * PAGE_TOK),
                            2 * PAGE_TOK,
                        ),
                        :,
                    ],
                    preferred_element_type=jnp.float32,
                ).astype(jnp.bfloat16)
                to = pl.ds(pl.multiple_of(at * PAGE_TOK, PAGE_TOK), PAGE_TOK)
                k_s[to, :] = both[:PAGE_TOK]
                v_s[to, :HEAD_DIM] = both[PAGE_TOK:]
                v_s[to, HEAD_DIM:] = ones
            return carry

        lax.fori_loop(0, (n_live + NARROW - 1) // NARROW, split_step, 0)

    n_full, n_live = counts[0], counts[1]
    total = GROUP * tok
    if first:
        m_s[...] = jnp.full(m_s.shape, FLOOR, jnp.float32)
        acc_s[...] = jnp.zeros(acc_s.shape, jnp.float32)
    else:
        acc_s[...] = carried[0][0]
        m_s[...] = carried[1][0]

    if block is None:
        t_rel, b = step // 2, step % 2
    else:
        t_rel, b = step, block
    line = lax.broadcasted_iota(jnp.int32, (tok, PAGE_TOK), 0)
    p = line // tok_rows
    kx = place_of(p)
    token = ((kx ^ head) * ways + (t_rel ^ way)) * tok_rows + line % tok_rows
    q_at = token + jnp.where(b == 0, place[2], place[3])

    def tile_step(at, size, masked):
        span_k = pl.ds(pl.multiple_of(at * PAGE_TOK, PAGE_TOK), size * PAGE_TOK)
        keys = k_s[span_k, :]
        values = v_s[span_k, :]
        if masked:
            lane = lax.broadcasted_iota(jnp.int32, (tok, PAGE_TOK), 1)
            visible = []
            for s in range(size):
                slot = order[jnp.minimum(at + s, n_live - 1)]
                start = jnp.where(at + s < n_live, pages[slot] * PAGE_TOK, FAR)
                seen = lane + start <= q_at
                visible.append(jnp.concatenate([seen] * (rows // tok), axis=0))

        def score(part):
            return lax.dot_general(
                q_ref[0, part * rows : (part + 1) * rows, :],
                keys,
                (((1,), (1,)), ((), ())),
                preferred_element_type=jnp.float32,
            )

        def soften(part, scores):
            span = slice(part * rows, (part + 1) * rows)
            pieces = [scores[:, s * PAGE_TOK : (s + 1) * PAGE_TOK] for s in range(size)]
            if masked:
                pieces = [jnp.where(v, x, FLOOR) for v, x in zip(visible, pieces)]
            peak = functools.reduce(jnp.maximum, pieces)
            m_old = m_s[span, :]
            m_new = jnp.maximum(m_old, jnp.max(peak, axis=1, keepdims=True) * SCALE)
            shift = jnp.maximum(m_new, 0.5 * FLOOR * SCALE) if masked else m_new
            weights = jnp.concatenate(
                [jnp.exp2(x * SCALE - shift).astype(jnp.bfloat16) for x in pieces], axis=1
            )
            m_s[span, :] = m_new
            return weights, jnp.exp2(m_old - m_new)

        def gather(part, weights, alpha):
            span = slice(part * rows, (part + 1) * rows)
            mixed = jnp.dot(weights, values, preferred_element_type=jnp.float32)
            acc_s[span, :HEAD_DIM] = acc_s[span, :HEAD_DIM] * alpha + mixed[:, :HEAD_DIM]
            acc_s[span, HEAD_DIM:] = acc_s[span, HEAD_DIM:] * alpha + mixed[:, HEAD_DIM:]

        parts = total // rows
        scores = score(0)
        waiting = None
        for part in range(parts):
            following = score(part + 1) if part + 1 < parts else None
            weights, alpha = soften(part, scores)
            if waiting is not None:
                gather(*waiting)
            waiting = (part, weights, alpha)
            scores = following
        gather(*waiting)

    n_wide = n_full // WIDE
    n_open = (n_full - n_wide * WIDE) // NARROW
    base = n_wide * WIDE
    done = base + n_open * NARROW
    n_masked = (n_live - done + NARROW - 1) // NARROW

    def wide(i, carry):
        tile_step(i * WIDE, WIDE, False)
        return carry

    def narrow(i, carry):
        tile_step(base + i * NARROW, NARROW, False)
        return carry

    def masked(i, carry):
        tile_step(done + i * NARROW, NARROW, True)
        return carry

    lax.fori_loop(0, n_wide, wide, 0)
    lax.fori_loop(0, n_open, narrow, 0)
    lax.fori_loop(0, n_masked, masked, 0)

    if last:
        row = lax.broadcasted_iota(jnp.int32, (tok, HEAD_DIM), 0)
        col = lax.broadcasted_iota(jnp.int32, (tok, HEAD_DIM), 1)
        eye = row == col
        lines = []
        for ref, lanes in ((m_s, slice(0, HEAD_DIM)), (acc_s, slice(HEAD_DIM, 2 * HEAD_DIM))):
            for g in range(GROUP):
                span = slice(g * tok, (g + 1) * tok)
                lines.append(
                    jnp.sum(jnp.where(eye, ref[span, lanes], 0.0), axis=0, keepdims=True)
                )
        stats = jnp.concatenate(lines, axis=0)
        for w in range(ways):

            @pl.when(step == w)
            def _():
                outs[w][:total, :] = acc_s[:, :HEAD_DIM].astype(jnp.bfloat16)
                for i, piece in enumerate(three_parts(stats)):
                    at = total + i * 2 * GROUP
                    outs[w][at : at + 2 * GROUP, :] = piece


def attend(place, x, first_slot, q, carried, block, tok_rows, rows):
    sources = x.shape[0]
    src_slots = x.shape[1] // (2 * PAGE_TOK)
    steps, total, _ = q.shape
    tok = total // GROUP
    first = carried is None
    last = block is not None
    ways = steps // 2
    n_slots = -(-sources * src_slots // WIDE) * WIDE
    if last:
        grid = ways
        at = lambda i, *_: (2 * i + block, 0, 0)
    else:
        grid = steps
        at = lambda i, *_: (i, 0, 0)
    in_specs = [
        pl.BlockSpec(x.shape, lambda i, *_: (0, 0, 0)),
        pl.BlockSpec((1, total, HEAD_DIM), at),
    ]
    sent = total + 3 * 2 * GROUP
    if last:
        out_shape = (jax.ShapeDtypeStruct((sent, HEAD_DIM), jnp.bfloat16),) * ways
        out_specs = (pl.BlockSpec((sent, HEAD_DIM), lambda i, *_: (0, 0)),) * ways
    else:
        out_shape = (
            jax.ShapeDtypeStruct((steps, total, 2 * HEAD_DIM), jnp.float32),
            jax.ShapeDtypeStruct((steps, total, HEAD_DIM), jnp.float32),
        )
        out_specs = (
            pl.BlockSpec((1, total, 2 * HEAD_DIM), at),
            pl.BlockSpec((1, total, HEAD_DIM), at),
        )
    extra = ()
    sums = ()
    if last:
        sums = (
            pltpu.VMEM((total, 2 * HEAD_DIM), jnp.float32),
            pltpu.VMEM((total, HEAD_DIM), jnp.float32),
        )
    if not first:
        extra = tuple(carried)
        in_specs += [
            pl.BlockSpec((1, total, 2 * HEAD_DIM), at),
            pl.BlockSpec((1, total, HEAD_DIM), at),
        ]
    flops = 8 * grid * total * sources * src_slots * PAGE_TOK * HEAD_DIM
    return pl.pallas_call(
        functools.partial(
            attend_kernel,
            first_slot=first_slot,
            first=first,
            last=last,
            rows=rows,
            tok=tok,
            ways=ways,
            tok_rows=tok_rows,
            block=block,
        ),
        out_shape=out_shape,
        grid_spec=pltpu.PrefetchScalarGridSpec(
            num_scalar_prefetch=1,
            grid=(grid,),
            in_specs=in_specs,
            out_specs=out_specs,
            scratch_shapes=[
                pltpu.VMEM((n_slots * PAGE_TOK, HEAD_DIM), jnp.bfloat16),
                pltpu.VMEM((n_slots * PAGE_TOK, 2 * HEAD_DIM), jnp.bfloat16),
                *sums,
                pltpu.VMEM((sources, HEAD_DIM), jnp.int32),
                pltpu.SMEM((n_slots + 1,), jnp.int32),
                pltpu.SMEM((n_slots + 1,), jnp.int32),
                pltpu.SMEM((n_slots,), jnp.int32),
                pltpu.SMEM((sources, HEAD_DIM), jnp.int32),
                pltpu.SMEM((2,), jnp.int32),
                pltpu.SemaphoreType.DMA(()),
            ],
        ),
        cost_estimate=pl.CostEstimate(
            flops=flops, transcendentals=flops // (8 * HEAD_DIM), bytes_accessed=x.size * 2
        ),
        name="attend_last" if last else "attend_first",
    )(place, x, q, *extra)


def merge(parts, a_ref, tok):
    total = GROUP * tok
    row = lax.broadcasted_iota(jnp.int32, (tok, HEAD_DIM), 0)
    col = lax.broadcasted_iota(jnp.int32, (tok, HEAD_DIM), 1)
    eye = row == col
    stats = []
    for part in parts:
        pieces = [
            part[total + i * 2 * GROUP : total + (i + 1) * 2 * GROUP, :].astype(jnp.float32)
            for i in range(3)
        ]
        stats.append((pieces[0] + pieces[1]) + pieces[2])
    tops = functools.reduce(jnp.maximum, [s[:GROUP] for s in stats])
    factors = [jnp.exp2(s[:GROUP] - tops) for s in stats]
    totals = sum(f * s[GROUP:] for f, s in zip(factors, stats))
    for g in range(GROUP):
        span = slice(g * tok, (g + 1) * tok)
        mixed = 0.0
        for f, part in zip(factors, parts):
            ratio = jnp.where(eye, f[g : g + 1] / totals[g : g + 1], 0.0)
            mixed += jnp.sum(ratio, axis=1, keepdims=True) * part[span, :].astype(jnp.float32)
        a_ref[:, g * HEAD_DIM : (g + 1) * HEAD_DIM] = mixed.astype(jnp.bfloat16)


def project_kernel(*refs, n_parts, n_ws, tok, y_first):
    parts = refs[:n_parts]
    ws = refs[n_parts : n_parts + n_ws]
    outs = refs[n_parts + n_ws :]
    keep_ref, send_ref = outs[:2]
    if n_parts == n_ws:
        a_ref = outs[2]

        @pl.when(pl.program_id(0) == 0)
        def _():
            merge(parts, a_ref, tok)

    else:
        a_ref = parts[0]
    depth = a_ref.shape[1] // n_ws
    total = 0.0
    for s in range(n_ws):
        total += jnp.dot(
            a_ref[:, s * depth : (s + 1) * depth], ws[s][...], preferred_element_type=jnp.float32
        )
    if y_first:
        keep, send = total[: tok // 2], total[tok // 2 :]
    else:
        quarters = [total[i * tok // 4 : (i + 1) * tok // 4] for i in range(4)]
        keep = jnp.concatenate(quarters[0::2], axis=0)
        send = jnp.concatenate(quarters[1::2], axis=0)
    keep_ref[...] = keep
    send_ref[...] = send.astype(jnp.bfloat16)


def project(parts, ws, tok, column_part, y_first, width=2048):
    columns = ws[0].shape[1] // COLUMN_PARTS
    steps = columns // width
    fixed = lambda i: (0, 0)
    half = tok // 2
    depth = sum(w.shape[0] for w in ws)
    merging = len(parts) == len(ws)
    out_shape = [
        jax.ShapeDtypeStruct((half, columns), jnp.float32),
        jax.ShapeDtypeStruct((half, columns), jnp.bfloat16),
    ]
    out_specs = [
        pl.BlockSpec((half, width), lambda i: (0, i)),
        pl.BlockSpec((half, width), lambda i: (0, i)),
    ]
    if merging:
        out_shape.append(jax.ShapeDtypeStruct((tok, depth), jnp.bfloat16))
        out_specs.append(pl.BlockSpec((tok, depth), fixed))
    return pl.pallas_call(
        functools.partial(
            project_kernel, n_parts=len(parts), n_ws=len(ws), tok=tok, y_first=y_first
        ),
        out_shape=out_shape,
        grid=(steps,),
        in_specs=[pl.BlockSpec(o.shape, fixed) for o in parts]
        + [
            pl.BlockSpec((w.shape[0], width), lambda i: (0, column_part * steps + i)) for w in ws
        ],
        out_specs=out_specs,
        cost_estimate=pl.CostEstimate(
            flops=2 * tok * depth * columns, transcendentals=0, bytes_accessed=2 * depth * columns
        ),
        name="project",
    )(*parts, *ws)


def local(
    queries, kv_cache, w_out, slot_page_before, slot_page_after, move_out, move_in, positions
):
    n = lax.axis_size("pages")
    slots = kv_cache.shape[0]
    ways = n // KV_HEADS
    tok_rows = BLOCK // n
    tok = BLOCK // ways
    me = lax.axis_index("pages")
    way = me // KV_HEADS
    head = head_of(me % KV_HEADS)
    groups = [[a * KV_HEADS + b for b in range(KV_HEADS)] for a in range(ways)]

    def exchange(x):
        return lax.all_to_all(x, "pages", 0, 0, axis_index_groups=groups, tiled=True)

    cuts = [(0, FIRST_SLOTS), (FIRST_SLOTS, slots - FIRST_SLOTS)]
    arrived = []
    for at, count in cuts:
        piece = split_heads(kv_cache, slot_page_before, at, count)
        got = exchange(piece)
        arrived.append(got.reshape(KV_HEADS, -1, HEAD_DIM))
    place = jnp.stack([head, way, positions[0, 0], positions[1, 0]]).astype(jnp.int32)
    q = query_rows(queries, place, ways, tok_rows)

    leaving = outgoing_pages(kv_cache, move_out[0])
    landed = []
    for o in range(1, MOVE_WIN + 1):
        landed.append(permute_to(leaving[o - 1], n, lambda i: (i + o) % n))

    ws = [w_out]
    for s in range(1, ways):
        ws.append(permute_to(w_out, n, lambda i: i ^ s))

    rows = 2 * tok
    carried = attend(place, arrived[0], 0, q, None, None, tok_rows, rows)

    def merger(i, s):
        return head_of(i % KV_HEADS) * ways + ((i // KV_HEADS) ^ s)

    partial = []
    for b in range(2):
        out = attend(place, arrived[1], FIRST_SLOTS, q, carried, b, tok_rows, rows)
        parts = []
        for s in range(ways):
            parts.append(permute_to(out[s], n, lambda i: merger(i, s)))
        partial.append(parts)

    sums = []
    for b in range(2):
        merged = partial[b]
        for c in range(COLUMN_PARTS):
            y_first = (b, c) != (0, 1)
            keep, send, *a = project(merged, ws, tok, c, y_first)
            if a:
                merged = a
            turns = (1, 2, 4) if y_first else (2, 1, 4)
            got = permute_to(send, n, lambda i: i ^ (turns[0] * ways))
            sums.append((keep, got, turns))
    cache_after = arrange_pages(kv_cache, landed, slot_page_after, move_in[0], send)

    results = []
    for keep, got, turns in sums:
        for turn in turns[1:]:
            total = keep + got.astype(jnp.float32)
            half = total.shape[0] // 2
            keep = total[:half]
            send = total[half:].astype(jnp.bfloat16)
            got = permute_to(send, n, lambda i: i ^ (turn * ways))
        results.append((keep + got.astype(jnp.float32)).astype(jnp.bfloat16))
    out = jnp.stack(
        [
            jnp.concatenate(results[b * COLUMN_PARTS : (b + 1) * COLUMN_PARTS], axis=1)
            for b in range(2)
        ]
    )
    return (out, cache_after)


def solution(mesh):
    in_specs = (
        P(None, "groups", None),
        P(("groups", "pages"), None, None, None),
        P("pages", None),
        P(("groups", "pages")),
        P(("groups", "pages")),
        P(("groups", "pages"), None),
        P(("groups", "pages"), None),
        P(None, "groups"),
    )
    out_specs = (P(None, ("groups", "pages"), None), P(("groups", "pages"), None, None, None))
    return jax.shard_map(local, mesh=mesh, in_specs=in_specs, out_specs=out_specs, check_vma=False)
```
